32 devices in a mesh: groups: 1, expert: 8 (over z, core), dp: 4 (over y, x).
Axes of the slice: x: 2, y: 2, z: 4, core: 2. Of those that a mesh axis runs over, the one named last changes fastest.
Arguments:
- tokens: bfloat16 [128, 4096], P(('groups', 'expert', 'dp')), may hold values from -6 to 6
- expert_ids: int32 [128, 2], P(('groups', 'expert', 'dp')), may hold values from 0 to 7, as said below
- gate_weights: bfloat16 [128, 2], P(('groups', 'expert', 'dp')), may hold values from 0.099609375 to 1
- placement: int32 [2, 2], P('groups'), may hold values from 0 to 7, as said below
- w_gate: bfloat16 [8, 1536, 4096], P('expert', 'dp'), may hold values from -0.09375 to 0.09375
- w_up: bfloat16 [8, 1536, 4096], P('expert', 'dp'), may hold values from -0.09375 to 0.09375
- w_down: bfloat16 [8, 1536, 4096], P('expert', 'dp'), may hold values from -0.15625 to 0.15625
Outputs:
- mixed: bfloat16 [128, 4096], P(('groups', 'expert', 'dp'))
The draws below stay inside these ranges and needn't reach their ends.
Inputs may be any that keep to these rules, and one draw needn't show every extreme that they name: `expert_ids`: each row names 2 different experts. In each aligned block of 16 rows (the tokens of one index of expert) no expert is named by more than 6 rows, and some expert is named by exactly that many. `placement`: row 0 holds 2 different experts; row 1 holds 2 different expert indices, none of which appears in row 0.
All inputs are finite; a program needn't handle non-finite values.
Results may differ from the reference program's by a relative error of at most 0.015.
Values may be sent and summed in bfloat16 or wider, within the bound.
A program may use at most 64 MiB of HBM per device.

```python
import math
import jax
import jax.numpy as jnp
from jax import lax

D = 4096
FF = 1536
HOT = 2
EXPERTS = 8
TOPK = 2
GROUP = 16
TOKENS = 128
CAP = 4
OVF = 2
N_EXPERT = 8
N_DP = 4


def listed_pairs(key):
    others = jax.random.permutation(jax.random.fold_in(key, 11), EXPERTS - 1).astype(jnp.int32)
    picked = others[:2 * HOT]
    position = jax.random.randint(jax.random.fold_in(key, 13), (), 0, 2 * HOT).astype(jnp.int32)
    slot_iota = jnp.arange(2 * HOT, dtype=jnp.int32)
    picked = jnp.where(slot_iota == position, EXPERTS - 1, picked).astype(jnp.int32)
    return (picked[:HOT], picked[HOT:2 * HOT])


def draw_placement(key, part):
    chosen, owners = listed_pairs(key)
    return jnp.stack([chosen, owners]).astype(jnp.int32)


def route_block(key, chosen, block_index):
    slots = CAP + OVF
    total = GROUP * TOPK
    block_key = jax.random.fold_in(jax.random.fold_in(key, 23), block_index)
    shuffled = jax.random.permutation(jax.random.fold_in(block_key, 1), EXPERTS).astype(jnp.int32)
    experts_iota = jnp.arange(EXPERTS, dtype=jnp.int32)
    is_listed = jnp.any(experts_iota[:, None] == chosen[None, :], axis=1)
    score = jnp.where(is_listed, 0, 1 + shuffled).astype(jnp.int32)
    order = jnp.argsort(score, stable=True).astype(jnp.int32)
    counts = jnp.clip(total - experts_iota * slots, 0, slots).astype(jnp.int32)
    ends = jnp.cumsum(counts).astype(jnp.int32)
    pair_iota = jnp.arange(total, dtype=jnp.int32)
    which = jnp.sum((pair_iota[:, None] >= ends[None, :]).astype(jnp.int32), axis=1)
    named = order[which]
    grid = named.reshape(TOPK, GROUP).T
    row_order = jax.random.permutation(jax.random.fold_in(block_key, 2), GROUP)
    return grid[row_order].astype(jnp.int32)


def draw_expert_ids(key, part):
    chosen, owners = listed_pairs(key)
    blocks = jax.vmap(lambda index: route_block(key, chosen, index))(jnp.arange(N_EXPERT, dtype=jnp.int32))
    return blocks.reshape(TOKENS, TOPK).astype(jnp.int32)


def level_of(own_key, shape, cuts, low, high):
    gain = 1.0
    for dim, blocks in cuts:
        draws = jax.random.uniform(jax.random.fold_in(jax.random.fold_in(own_key, 6), dim), (blocks,), jnp.float32, low / len(cuts), high / len(cuts))
        gain = gain * jnp.repeat(jnp.exp(draws), shape[dim] // blocks).reshape((-1,) + (1,) * (len(shape) - 1 - dim))
    return gain


def scatter_about(key, dims, width, reach, cuts=(), kind=jnp.bfloat16):
    array = jax.random.normal(key, dims, jnp.float32) * width
    if len(cuts) > 0:
        array = level_of(key, dims, cuts, -0.22, 0.18) * array
    return jnp.clip(array, min=-reach, max=reach).astype(kind)


def setup_inputs(seed: int = 0, part: int = 0) -> dict:
    key_list = jax.random.split(jax.random.key(seed), 8)
    part_keys = jax.random.split(jax.random.fold_in(key_list[7], part), 8)
    return {
        "tokens": scatter_about(part_keys[0], (TOKENS, D), 1.0, 6.0, ((0, 32),)),
        "expert_ids": draw_expert_ids(jax.random.fold_in(jax.random.fold_in(key_list[7], part), 71), part),
        "gate_weights": jnp.clip(jnp.exp(math.log(1.0) - 2.306499 * jax.random.uniform(part_keys[2], (TOKENS, TOPK), jnp.float32) ** level_of(part_keys[2], (TOKENS, TOPK), ((0, 32),), -0.2, 0.2)), 0.099609375, 1.0).astype(jnp.bfloat16),
        "placement": draw_placement(jax.random.fold_in(jax.random.fold_in(key_list[7], part), 71), part),
        "w_gate": scatter_about(key_list[4], (EXPERTS, FF, D), D ** -0.5, 0.09375, ((0, 8), (1, 4))),
        "w_up": scatter_about(key_list[5], (EXPERTS, FF, D), D ** -0.5, 0.09375, ((0, 8), (1, 4))),
        "w_down": scatter_about(key_list[6], (EXPERTS, FF, D), FF ** -0.5, 0.15625, ((0, 8), (1, 4))),
    }


def reference(tokens, expert_ids, gate_weights, placement, w_gate, w_up, w_down):
    slots = CAP + OVF
    pairs = GROUP * TOPK
    flat_ids = expert_ids.reshape(N_EXPERT, pairs)
    onehot = (flat_ids[:, :, None] == jnp.arange(EXPERTS, dtype=jnp.int32)[None, None, :]).astype(jnp.int32)
    before = jnp.cumsum(onehot, axis=1) - onehot
    rank = jnp.sum(before * onehot, axis=2)
    listed = jnp.any(flat_ids[:, :, None] == placement[0][None, None, :], axis=2)
    keep = (rank < CAP) | (listed & (rank < slots))
    group_index = jnp.arange(N_EXPERT, dtype=jnp.int32)[:, None]
    total_rows = EXPERTS * N_EXPERT * slots
    row = flat_ids * (N_EXPERT * slots) + group_index * slots + rank
    row = jnp.where(keep, row, total_rows).astype(jnp.int32).reshape(-1)
    token_index = (group_index * GROUP + jnp.arange(pairs, dtype=jnp.int32)[None, :] // TOPK).astype(jnp.int32).reshape(-1)
    table = jnp.zeros((total_rows + 1,), jnp.int32).at[row].set(token_index)[:-1]
    weight_table = jnp.zeros((total_rows + 1,), jnp.float32).at[row].set(gate_weights.astype(jnp.float32).reshape(-1))[:-1]
    table = table.reshape(EXPERTS, N_EXPERT * slots)
    block = FF // N_DP
    contract = (((1,), (1,)), ((), ()))

    def expert(args):
        index, gate_w, up_w, down_w = args
        rows = tokens[index]
        gate = lax.dot_general(rows, gate_w, contract, preferred_element_type=jnp.float32)
        up = lax.dot_general(rows, up_w, contract, preferred_element_type=jnp.float32)
        hidden = (jax.nn.silu(gate) * up).astype(jnp.bfloat16)
        pieces = jnp.einsum("rbf,bfd->rbd", hidden.reshape(-1, N_DP, block).astype(jnp.float32),
                            down_w.reshape(N_DP, block, D).astype(jnp.float32))
        pieces = pieces.astype(jnp.bfloat16).astype(jnp.float32)
        return jnp.sum(pieces, axis=1)

    results = lax.map(expert, (table, w_gate, w_up, w_down))
    weighted = results.reshape(total_rows, D) * weight_table[:, None]
    mixed = jnp.zeros((TOKENS, D), jnp.float32).at[table.reshape(-1)].add(weighted)
    return mixed.astype(jnp.bfloat16)
```

```python
import functools

import jax
import jax.numpy as jnp
from jax import lax
from jax.experimental import pallas as pl
from jax.experimental.pallas import tpu as pltpu
from jax.sharding import PartitionSpec as P

MESH = pl.DeviceIdType.MESH
F32 = jnp.float32
BF16 = jnp.bfloat16


def each(count, step):
    if count <= 8:
        for i in range(count):
            step(i)
    else:
        def turn(i, carry):
            step(i)
            return carry

        lax.fori_loop(0, count, turn, 0)


def each_from(first, count, step):
    each(count - first, lambda i: step(i + first))


def kernel(experts, dp, topk, first, slots, padded,
           tok_hbm, ids_hbm, gates_hbm, placement_hbm, wg_hbm, wu_hbm, wd_hbm, out,
           tok, ids, gates, placement,
           wg, wu, wd, tok_s, tok_r, info_s, info_r, group_x, disp_s, rows_r, rows_f, part_f,
           part_s, part_r, back_s, back_r, wsel, mix_s,
           w_sem, s1, r1, si, ri, s2, r2, s3, r3, s4, r4, s5, r5, s6, r6):
    me_e = lax.axis_index("expert")
    me_j = lax.axis_index("dp")
    own, width = tok.shape
    block = width // dp
    group = own * dp
    pairs = group * topk
    lanes = info_s.shape[1]
    total = experts * padded

    if dp == 4:
        low, high = lax.rem(me_j, 2), me_j // 2
        across = (me_j, high * 2 + (1 - low), (1 - high) * 2 + low, (1 - high) * 2 + (1 - low))
        onward = backward = lambda s: across[s]
    else:
        onward = lambda s: lax.rem(me_j + s, dp)
        backward = lambda s: lax.rem(me_j + dp - s, dp)

    def to_dp(src, dst, send, recv, s):
        return pltpu.make_async_remote_copy(
            src_ref=src, dst_ref=dst, send_sem=send, recv_sem=recv,
            device_id={"dp": onward(s)}, device_id_type=MESH)

    def to_expert(src, dst, send, recv, shift):
        return pltpu.make_async_remote_copy(
            src_ref=src, dst_ref=dst, send_sem=send, recv_sem=recv,
            device_id={"expert": lax.rem(me_e + shift, experts)}, device_id_type=MESH)

    def cols(j):
        return pl.ds(pl.multiple_of(j * block, 128), block)

    barrier = pltpu.get_barrier_semaphore()
    for s in range(1, dp):
        pl.semaphore_signal(barrier, inc=1, device_id={"dp": onward(s)}, device_id_type=MESH)

    def greet(d):
        pl.semaphore_signal(barrier, inc=1, device_id={"expert": lax.rem(me_e + d, experts)}, device_id_type=MESH)

    each_from(1, experts, greet)

    pairs_of = ((ids_hbm, ids), (gates_hbm, gates), (placement_hbm, placement), (tok_hbm, tok),
                (wg_hbm, wg), (wu_hbm, wu), (wd_hbm, wd))
    loads = [pltpu.make_async_copy(a, b, w_sem.at[i]) for i, (a, b) in enumerate(pairs_of)]
    for load in loads:
        load.start()
    for load in loads[:4]:
        load.wait()
    loads = loads[4:]

    lane = lax.broadcasted_iota(jnp.int32, (8, lanes), 1)
    line = lax.broadcasted_iota(jnp.int32, (8, lanes), 0)
    id_f = ids[...].astype(F32)
    gate_f = gates[...].astype(F32)
    info = jnp.zeros((8, lanes), F32)
    for t in range(own):
        for k in range(topk):
            here = lane == (me_j * own + t) * topk + k
            value = jnp.where(line == 0, jnp.broadcast_to(id_f[k:k + 1, t:t + 1], (8, lanes)),
                              jnp.broadcast_to(gate_f[k:k + 1, t:t + 1], (8, lanes)))
            info = jnp.where(here, value, info)
    info_s[...] = info
    for s in range(1, dp):
        tok_s[s] = tok[:, cols(onward(s))]
    tok_r[me_j] = tok[:, cols(me_j)]

    pl.semaphore_wait(barrier, dp - 1 + experts - 1)

    for s in range(1, dp):
        to_dp(info_s, info_r.at[s], si.at[s], ri.at[s], s).start()
    for s in range(1, dp):
        to_dp(tok_s.at[s], tok_r.at[me_j], s1.at[s], r1.at[s], s).start()
    for s in range(1, dp):
        to_dp(info_s, info_r.at[s], si.at[s], ri.at[s], s).wait_recv()
        info = info + info_r[s]

    id_row = info[0:1, :]
    gate_row = info[1:2, :]
    at_row = lax.broadcasted_iota(jnp.int32, (pairs, lanes), 0)
    at_lane = lax.broadcasted_iota(jnp.int32, (pairs, lanes), 1)
    id_col = jnp.sum(jnp.where(at_row == at_lane, jnp.broadcast_to(id_row, (pairs, lanes)), 0.0),
                     axis=1, keepdims=True)
    same = jnp.broadcast_to(id_col, (pairs, lanes)) == jnp.broadcast_to(id_row, (pairs, lanes))
    rank = jnp.sum(jnp.where(same, jnp.where(at_row < at_lane, 1.0, 0.0), 0.0), axis=0, keepdims=True)
    limit = jnp.full((1, lanes), float(first), F32)
    listed = placement[...].astype(F32)
    for h in range(placement.shape[1]):
        limit = jnp.where(id_row == jnp.broadcast_to(listed[0:1, h:h + 1], (1, lanes)), float(slots), limit)
    dest = jnp.where(rank < limit, id_row * float(padded) + rank, -1.0)
    dest = jnp.where(lax.broadcasted_iota(jnp.int32, (1, lanes), 1) < pairs, dest, -1.0)
    pick = lax.broadcasted_iota(jnp.int32, (total, lanes), 0).astype(F32) == jnp.broadcast_to(dest, (total, lanes))
    pair_i = lax.broadcasted_iota(jnp.int32, (lanes, group), 0)
    token_i = lax.broadcasted_iota(jnp.int32, (lanes, group), 1) * topk
    fold = jnp.where(pair_i >= token_i, jnp.where(pair_i < token_i + topk, 1.0, 0.0), 0.0).astype(BF16)
    select = jnp.dot(jnp.where(pick, 1.0, 0.0).astype(BF16), fold, preferred_element_type=F32).astype(BF16)

    for s in range(1, dp):
        to_dp(tok_s.at[s], tok_r.at[backward(s)], s1.at[s], r1.at[s], s).wait_recv()
    for j in range(dp):
        group_x[j * own:(j + 1) * own, :] = tok_r[j].astype(F32)
    rows_f[...] = jnp.dot(select, group_x[...].astype(BF16), preferred_element_type=F32)

    def dispatch(d):
        e = lax.rem(me_e + d, experts)
        start = pl.multiple_of(e * padded, 8)
        disp_s[e] = rows_f[pl.ds(start, slots), :].astype(BF16)
        to_expert(disp_s.at[e], rows_r.at[me_j, me_e], s2.at[d], r2.at[d], d).start()

    each_from(1, experts, dispatch)
    rows_r[me_j, me_e] = rows_f[pl.ds(pl.multiple_of(me_e * padded, 8), slots), :].astype(BF16)

    relayed = dp == 4 and experts <= 8
    direct = (1, 2) if relayed else range(1, dp)

    def forward(d):
        g = lax.rem(me_e + experts - d, experts)
        for s in direct:
            to_dp(rows_r.at[me_j, g], rows_r.at[me_j, g], s3.at[s, d], r3.at[s, d], s).start()

    forward(0)
    wsel[...] = jnp.dot(jnp.where(pick, jnp.broadcast_to(gate_row, (total, lanes)), 0.0).astype(BF16), fold,
                        preferred_element_type=F32)


    def arrive(d):
        g = lax.rem(me_e + experts - d, experts)
        to_expert(disp_s.at[g], rows_r.at[me_j, g], s2.at[d], r2.at[d], d).wait_recv()
        forward(d)

    each_from(1, experts, arrive)

    loads[0].wait()
    loads[1].wait()
    contract = (((1,), (1,)), ((), ()))

    def first_of(d):
        return 1 + d % 2

    def relay(d):
        g = lax.rem(me_e + experts - d, experts)
        side = first_of(d)
        j = onward(side)
        to_dp(rows_r.at[j, g], rows_r.at[j, g], s3.at[side, d], r3.at[side, d], side).wait_recv()
        to_dp(rows_r.at[j, g], rows_r.at[j, g], s3.at[3, d], r3.at[3, d], 3 - side).start()

    gate = up = None
    for s in range(dp):
        j = backward(s)

        def take(d):
            g = lax.rem(me_e + experts - d, experts)
            if s > 0 and not (relayed and s == first_of(d)):
                to_dp(rows_r.at[j, g], rows_r.at[j, g], s3.at[s, d], r3.at[s, d], s).wait_recv()
            rows_f[pl.ds(pl.multiple_of(g * padded, 8), slots), :] = rows_r[j, g].astype(F32)

        each(experts, take)
        x = rows_f[...].astype(BF16)
        gate_part = lax.dot_general(x, wg[:, cols(j)], contract, preferred_element_type=F32)
        up_part = lax.dot_general(x, wu[:, cols(j)], contract, preferred_element_type=F32)
        gate = gate_part if gate is None else gate + gate_part
        up = up_part if up is None else up + up_part
        if relayed and s == 0:
            each(experts, relay)
    hidden = (gate / (1.0 + jnp.exp(-gate)) * up).astype(BF16)

    loads[2].wait()
    for s in reversed(range(dp)):
        j = onward(s)
        part_f[...] = jnp.dot(hidden, wd[:, cols(j)], preferred_element_type=F32)
        target = part_s if s > 0 else part_r

        def split(d):
            g = lax.rem(me_e + d, experts)
            start = pl.multiple_of(g * padded, 8)
            target[s, g] = part_f[pl.ds(start, slots), :].astype(BF16)
            if s > 0:
                to_dp(part_s.at[s, g], part_r.at[s, g], s4.at[s, d], r4.at[s, d], s).start()

        each_from(1, experts, split)
        split(0)

    def summed(d):
        g = lax.rem(me_e + d, experts)
        for s in range(1, dp):
            to_dp(part_s.at[s, g], part_r.at[s, g], s4.at[s, d], r4.at[s, d], s).wait_recv()
        value = part_r[0, g].astype(F32)
        for s in range(1, dp):
            value = value + part_r[s, g].astype(F32)
        return value.astype(BF16)

    def give(d):
        g = lax.rem(me_e + d, experts)
        back_s[g] = summed(d)
        to_expert(back_s.at[g], back_r.at[me_e], s5.at[d], r5.at[d], d).start()

    each_from(1, experts, give)
    back_r[me_e] = summed(0)

    def collect(d):
        e = lax.rem(me_e + experts - d, experts)
        to_expert(back_s.at[e], back_r.at[e], s5.at[d], r5.at[d], d).wait_recv()

    each_from(1, experts, collect)

    def place(e):
        rows_f[pl.ds(e * padded, slots), :] = back_r[e].astype(F32)

    each(experts, place)
    group_x[...] = lax.dot_general(wsel[...].astype(BF16), rows_f[...].astype(BF16), (((0,), (0,)), ((), ())),
                                   preferred_element_type=F32)
    for j in range(dp):
        mix_s[j] = group_x[j * own:(j + 1) * own, :].astype(BF16)
    for s in reversed(range(1, dp)):
        to_dp(mix_s.at[onward(s)], out.at[:, cols(me_j)], s6.at[s], r6.at[s], s).start()
    kept = pltpu.make_async_copy(mix_s.at[me_j], out.at[:, cols(me_j)], s6.at[0])
    kept.start()
    kept.wait()
    for s in range(1, dp):
        j = backward(s)
        to_dp(mix_s.at[j], out.at[:, cols(j)], s6.at[s], r6.at[s], s).wait_recv()

    for s in range(1, dp):
        to_dp(info_s, info_r.at[s], si.at[s], ri.at[s], s).wait_send()
        to_dp(tok_s.at[s], tok_r.at[me_j], s1.at[s], r1.at[s], s).wait_send()
        to_dp(mix_s.at[onward(s)], out.at[:, cols(me_j)], s6.at[s], r6.at[s], s).wait_send()

    def left(d):
        g = lax.rem(me_e + experts - d, experts)
        for s in range(1, dp):
            to_dp(rows_r.at[me_j, g], rows_r.at[me_j, g], s3.at[s, d], r3.at[s, d], s).wait_send()
            to_dp(part_s.at[s, g], part_r.at[s, g], s4.at[s, d], r4.at[s, d], s).wait_send()

    def left_expert(d):
        e = lax.rem(me_e + d, experts)
        to_expert(disp_s.at[e], rows_r.at[me_j, me_e], s2.at[d], r2.at[d], d).wait_send()
        to_expert(back_s.at[e], back_r.at[me_e], s5.at[d], r5.at[d], d).wait_send()

    each(experts, left)
    each_from(1, experts, left_expert)


def relay_kernel(experts, dp, topk, first, slots, pad, bands,
                 tok_hbm, ids_hbm, gates_hbm, placement_hbm, wg_hbm, wu_hbm, wd_hbm, out,
                 ids, gates, placement, rows, flat, wg, wu, wd, hid, part_s, part_r, back_s,
                 l_sem, w_s, w_r, z_s, z_r, d_s, d_r, c_s, c_r, h_s, h_r, p_s, p_r, b_s, b_r):
    me_e = lax.axis_index("expert")
    me_j = lax.axis_index("dp")
    core = lax.rem(me_e, 2)
    z = lax.div(me_e, 2)
    chips = experts // 2
    far = chips - 1
    own = rows.shape[3]
    width = tok_hbm.shape[1]
    half = width // 2
    both = 2 * own
    span = dp * both
    band = width // bands

    def turn(at, q):
        return q + lax.div(at, chips // 2) * (far - 2 * q)

    def chip_at(k):
        q = k - 1 + lax.div(k - 1 + chips - turn(z, z), chips)
        return turn(z, q)

    def seen_from(other):
        q = turn(other, z)
        return q + 1 - lax.div(q + chips - turn(other, other), chips)

    low, high = lax.rem(me_j, 2), lax.div(me_j, 2)
    across = (me_j, high * 2 + (1 - low), (1 - high) * 2 + low, (1 - high) * 2 + (1 - low))
    sibling = z * 2 + (1 - core)

    def to_dp(src, dst, send, recv, s):
        return pltpu.make_async_remote_copy(src_ref=src, dst_ref=dst, send_sem=send, recv_sem=recv,
                                            device_id={"dp": across[s]}, device_id_type=MESH)

    def to_expert(src, dst, send, recv, e):
        return pltpu.make_async_remote_copy(src_ref=src, dst_ref=dst, send_sem=send, recv_sem=recv,
                                            device_id={"expert": e}, device_id_type=MESH)

    def edge(b):
        return 0 if b == 0 else pad + b * band

    def cols(b0, b1):
        return pl.ds(edge(b0), edge(b1) - edge(b0))

    whole = ((0, bands),)
    halves = ((0, bands // 2), (bands // 2, bands))
    single = tuple((b, b + 1) for b in range(bands))
    z_cuts = halves
    cuts = tuple(single if k == far else halves if k == far - 1 else whole for k in range(chips))

    barrier = pltpu.get_barrier_semaphore()
    for s in range(1, dp):
        pl.semaphore_signal(barrier, inc=1, device_id={"dp": across[s]}, device_id_type=MESH)
    for d in range(1, experts):
        pl.semaphore_signal(barrier, inc=1, device_id={"expert": lax.rem(me_e + d, experts)}, device_id_type=MESH)

    mine = rows.at[core, 0, me_j]
    kept = pl.ds(pl.multiple_of(core * half, 128), half)
    given = pl.ds(pl.multiple_of((1 - core) * half, 128), half)
    loads = [pltpu.make_async_copy(a, b, l_sem.at[i]) for i, (a, b) in enumerate((
        (ids_hbm, ids), (gates_hbm, gates), (placement_hbm, placement),
        (tok_hbm, mine.at[:, pl.ds(pad, width)]),
        (wg_hbm, wg), (wu_hbm, wu), (wd_hbm.at[:, kept], wd.at[core])))]
    for load in loads:
        load.start()
    for load in loads[:3]:
        load.wait()

    lane = lax.broadcasted_iota(jnp.int32, (own, pad), 1)
    line = lax.broadcasted_iota(jnp.int32, (own, pad), 0)
    id_f = ids[...].astype(F32)
    gate_f = gates[...].astype(F32)
    info = jnp.zeros((own, pad), F32)
    for t in range(own):
        for k in range(topk):
            for at, table in ((k, id_f), (topk + k, gate_f)):
                here = jnp.where(line == t, lane, -1) == at
                info = jnp.where(here, jnp.broadcast_to(table[k:k + 1, t:t + 1], (own, pad)), info)
    rows[core, 0, me_j, :, 0:pad] = info.astype(BF16)
    loads[3].wait()
    pl.semaphore_wait(barrier, dp - 1 + experts - 1)

    def over_z(k, i):
        other = chip_at(k)
        c = cols(*z_cuts[i])
        return to_expert(mine.at[:, c], rows.at[core, seen_from(other), me_j, :, c], z_s.at[k, i],
                         z_r.at[seen_from(other), i], other * 2 + core)

    def from_z(k, i):
        c = cols(*z_cuts[i])
        here = rows.at[core, k, me_j, :, c]
        return to_expert(here, here, z_s.at[k, i], z_r.at[k, i], sibling)

    def over_dp(k, i, s, at):
        here = rows.at[core, k, at, :, cols(*cuts[k][i])]
        return to_dp(here, here, d_s.at[k, s, i], d_r.at[k, s, i], s)

    def across_core(k, i, c):
        here = rows.at[c, k, :, :, cols(*cuts[k][i])]
        return to_expert(here, here, c_s.at[k, i], c_r.at[k, i], sibling)

    for k in range(1, chips):
        for i in range(len(z_cuts)):
            over_z(k, i).start()
    for s in range(1, dp):
        over_dp(0, 0, s, me_j).start()
    lend = to_expert(wd_hbm.at[:, given], wd.at[core], w_s, w_r, sibling)
    lend.start()

    def pass_on(k):
        for i, (b0, b1) in enumerate(cuts[k]):
            for n, (a0, a1) in enumerate(z_cuts):
                if a0 < b1 and a1 > b0 and a0 >= b0:
                    from_z(k, n).wait_recv()
            for s in range(1, dp):
                over_dp(k, i, s, me_j).start()

    def share(k, i):
        for s in range(1, dp):
            over_dp(k, i, s, across[s]).wait_recv()
        across_core(k, i, core).start()

    def spread(k, i):
        across_core(k, i, 1 - core).wait_recv()
        c = cols(*cuts[k][i])
        at = (k % 2) * span
        for o in range(2):
            for j in range(dp):
                start = at + j * both + o * own
                flat[k // 2, start:start + own, c] = rows[o, k, j, :, c].astype(F32)

    for k in range(1, chips):
        pass_on(k)
    share(0, 0)
    share(1, 0)
    spread(0, 0)
    spread(1, 0)

    contract = (((1,), (1,)), ((), ()))
    loads[4].wait()
    loads[5].wait()

    def gate_up(p, b, gate, up):
        c = pl.ds(b * band, band)
        x = flat[p, :, pl.ds(pad + b * band, band)].astype(BF16)
        gate_part = lax.dot_general(x, wg[:, c], contract, preferred_element_type=F32)
        up_part = lax.dot_general(x, wu[:, c], contract, preferred_element_type=F32)
        return (gate_part, up_part) if gate is None else (gate + gate_part, up + up_part)

    me_f = me_e.astype(F32)
    many = 2 * span
    r = lax.broadcasted_iota(jnp.int32, (many, many), 0)
    q = lax.broadcasted_iota(jnp.int32, (many, many), 1)
    same = jnp.where(lax.div(r, span) == lax.div(q, span), lax.rem(lax.div(r, own), 2), 2) == lax.rem(lax.div(q, own), 2)
    below = jnp.where(same, jnp.where(q < r, 1.0, 0.0), 0.0).astype(BF16)
    listed = placement[0:1, :].astype(F32)
    extra = jnp.sum(jnp.where(listed == me_f, float(slots - first), 0.0), axis=1, keepdims=True)
    limit = float(first) + extra

    def weigh(p):
        told = flat[p, :, 0:pad]
        named = jnp.zeros((many, 1), F32)
        value = jnp.zeros((many, 1), F32)
        for k in range(topk):
            hit = told[:, k:k + 1] == me_f
            named = named + jnp.where(hit, 1.0, 0.0)
            value = value + jnp.where(hit, told[:, topk + k:topk + k + 1], 0.0)
        rank = jnp.dot(below, jnp.broadcast_to(named, (many, 128)).astype(BF16), preferred_element_type=F32)[:, 0:1]
        return jnp.where(rank < limit, value, 0.0)

    def finish(p, gate, up, weight):
        hid[core, p * many:(p + 1) * many, :] = (gate / (1.0 + jnp.exp(-gate)) * up * weight).astype(BF16)

    gate = up = None
    todo = [(k, i) for k in range(2, chips) for i in range(len(cuts[k]))]
    for b in range(bands):
        gate, up = gate_up(0, b, gate, up)
        for k, i in todo[b * len(todo) // bands:(b + 1) * len(todo) // bands]:
            share(k, i)
    finish(0, gate, up, weigh(0))

    gate = up = None
    for b in range(bands):
        for k in range(2, chips):
            for i, (b0, b1) in enumerate(cuts[k]):
                if b0 == b:
                    spread(k, i)
        gate, up = gate_up(1, b, gate, up)
    finish(1, gate, up, weigh(1))

    swap = to_expert(hid.at[core], hid.at[core], h_s, h_r, sibling)
    swap.start()
    loads[6].wait()
    to_expert(wd.at[1 - core], wd.at[1 - core], w_s, w_r, sibling).wait_recv()
    to_expert(hid.at[1 - core], hid.at[1 - core], h_s, h_r, sibling).wait_recv()
    piece = half // bands
    for b in range(bands):
        c = pl.ds(b * piece, piece)
        total = jnp.dot(hid[0], wd[0, :, c], preferred_element_type=F32)
        total = total + jnp.dot(hid[1], wd[1, :, c], preferred_element_type=F32)
        part_s[:, :, c] = total.reshape(chips * dp, both, piece).astype(BF16)

    def over_part(k, s):
        return to_dp(part_s.at[k * dp + across[s]], part_r.at[k, s], p_s.at[k, s], p_r.at[k, s], s)

    for k in reversed(range(chips)):
        for s in reversed(range(1, dp)):
            over_part(k, s).start()

    def over_back(k, o):
        e = sibling if k == 0 else chip_at(k) * 2 + o
        return to_expert(back_s.at[k, o], out.at[z, :, kept], b_s.at[k, o], b_r.at[z, core], e)

    for k in reversed(range(chips)):
        value = part_s[k * dp + me_j].astype(F32)
        for s in range(1, dp):
            over_part(k, s).wait_recv()
            value = value + part_r[k, s].astype(F32)
        for o in range(2):
            back_s[k, o] = value[o * own:(o + 1) * own, :].astype(BF16)
        if k > 0:
            for o in range(2):
                over_back(k, o).start()
    give = to_expert(back_s.at[0, 1 - core], out.at[z, :, kept], b_s.at[0, 0], b_r.at[z, core], sibling)
    give.start()
    keep = pltpu.make_async_copy(back_s.at[0, core], out.at[z, :, kept], b_s.at[0, 1])
    keep.start()

    keep.wait()
    to_expert(back_s.at[0, core], out.at[z, :, given], b_s.at[0, 0], b_r.at[z, 1 - core], sibling).wait_recv()
    for k in range(1, chips):
        other = chip_at(k)
        for o in range(2):
            to_expert(back_s.at[k, o], out.at[other, :, pl.ds(o * half, half)], b_s.at[k, o], b_r.at[other, o],
                      sibling).wait_recv()

    lend.wait_send()
    swap.wait_send()
    give.wait_send()
    for k in range(chips):
        for i in range(len(z_cuts)):
            if k > 0:
                over_z(k, i).wait_send()
        for i in range(len(cuts[k])):
            for s in range(1, dp):
                over_dp(k, i, s, me_j).wait_send()
            across_core(k, i, core).wait_send()
        for s in range(1, dp):
            over_part(k, s).wait_send()
        if k > 0:
            for o in range(2):
                over_back(k, o).wait_send()


def relayed(tokens, expert_ids, gate_weights, placement, w_gate, w_up, w_down, experts, dp, first, slots):
    own, width = tokens.shape
    topk = expert_ids.shape[1]
    units = w_gate.shape[1]
    chips = experts // 2
    bands = 4
    pad = 128
    half = width // 2
    hbm = pl.BlockSpec(memory_space=pl.ANY)
    dma = pltpu.SemaphoreType.DMA
    parts = pl.pallas_call(
        functools.partial(relay_kernel, experts, dp, topk, first, slots, pad, bands),
        out_shape=jax.ShapeDtypeStruct((chips, own, width), BF16),
        in_specs=[hbm] * 7,
        out_specs=hbm,
        scratch_shapes=[
            pltpu.VMEM((topk, own), jnp.int32),
            pltpu.VMEM((topk, own), BF16),
            pltpu.VMEM(placement.shape, jnp.int32),
            pltpu.VMEM((2, chips, dp, own, pad + width), BF16),
            pltpu.VMEM((chips // 2, 4 * dp * own, pad + width), F32),
            pltpu.VMEM((units, width), BF16),
            pltpu.VMEM((units, width), BF16),
            pltpu.VMEM((2, units, half), BF16),
            pltpu.VMEM((2, experts * dp * own, units), BF16),
            pltpu.VMEM((chips * dp, 2 * own, half), BF16),
            pltpu.VMEM((chips, dp, 2 * own, half), BF16),
            pltpu.VMEM((chips, 2, own, half), BF16),
            dma((7,)),
            dma, dma,
            dma((chips, 2)), dma((chips, 2)),
            dma((chips, dp, bands)), dma((chips, dp, bands)),
            dma((chips, bands)), dma((chips, bands)),
            dma, dma,
            dma((chips, dp)), dma((chips, dp)),
            dma((chips, 2)), dma((chips, 2)),
        ],
        compiler_params=pltpu.CompilerParams(
            collective_id=1, has_side_effects=True, vmem_limit_bytes=56 << 20
        ),
    )(tokens, expert_ids.T, gate_weights.T, placement, w_gate[0], w_up[0], w_down[0])
    return jnp.sum(parts.astype(F32), axis=0).astype(BF16)


def body(tokens, expert_ids, gate_weights, placement, w_gate, w_up, w_down):
    experts = lax.axis_size("expert")
    dp = lax.axis_size("dp")
    own, width = tokens.shape
    topk = expert_ids.shape[1]
    group = own * dp
    first = max(2, group * topk // experts)
    slots = first + max(1, first // 2)
    if dp == 4 and experts == 8 and own == 4 and width % 1024 == 0:
        return relayed(tokens, expert_ids, gate_weights, placement, w_gate, w_up, w_down, experts, dp, first, slots)
    padded = -(-slots // 8) * 8
    lanes = -(-group * topk // 128) * 128
    block = width // dp
    units = w_gate.shape[1]
    total = experts * padded
    hbm = pl.BlockSpec(memory_space=pl.ANY)
    dma = pltpu.SemaphoreType.DMA
    return pl.pallas_call(
        functools.partial(kernel, experts, dp, topk, first, slots, padded),
        out_shape=jax.ShapeDtypeStruct((own, width), BF16),
        in_specs=[hbm] * 7,
        out_specs=hbm,
        scratch_shapes=[
            pltpu.VMEM((own, width), BF16),
            pltpu.VMEM((topk, own), jnp.int32),
            pltpu.VMEM((topk, own), BF16),
            pltpu.VMEM(placement.shape, jnp.int32),
            pltpu.VMEM((units, width), BF16),
            pltpu.VMEM((units, width), BF16),
            pltpu.VMEM((units, width), BF16),
            pltpu.VMEM((dp, own, block), BF16),
            pltpu.VMEM((dp, own, block), BF16),
            pltpu.VMEM((8, lanes), F32),
            pltpu.VMEM((dp, 8, lanes), F32),
            pltpu.VMEM((group, block), F32),
            pltpu.VMEM((experts, slots, block), BF16),
            pltpu.VMEM((dp, experts, slots, block), BF16),
            pltpu.VMEM((total, block), F32),
            pltpu.VMEM((total, block), F32),
            pltpu.VMEM((dp, experts, slots, block), BF16),
            pltpu.VMEM((dp, experts, slots, block), BF16),
            pltpu.VMEM((experts, slots, block), BF16),
            pltpu.VMEM((experts, slots, block), BF16),
            pltpu.VMEM((total, group), F32),
            pltpu.VMEM((dp, own, block), BF16),
            dma((7,)),
            dma((dp,)), dma((dp,)), dma((dp,)), dma((dp,)),
            dma((experts,)), dma((experts,)),
            dma((dp, experts)), dma((dp, experts)),
            dma((dp, experts)), dma((dp, experts)),
            dma((experts,)), dma((experts,)),
            dma((dp,)), dma((dp,)),
        ],
        compiler_params=pltpu.CompilerParams(
            collective_id=0, has_side_effects=True, vmem_limit_bytes=56 << 20
        ),
    )(tokens, expert_ids.T, gate_weights.T, placement, w_gate[0], w_up[0], w_down[0])


def solution(mesh):
    placed = (
        P(("groups", "expert", "dp"), None),
        P(("groups", "expert", "dp"), None),
        P(("groups", "expert", "dp"), None),
        P("groups", None),
        P("expert", "dp", None),
        P("expert", "dp", None),
        P("expert", "dp", None),
    )
    return jax.shard_map(
        body,
        mesh=mesh,
        in_specs=placed,
        out_specs=P(("groups", "expert", "dp"), None),
        check_vma=False,
    )
```

```python
import functools

import jax
import jax.numpy as jnp
from jax import lax
from jax.experimental import pallas as pl
from jax.experimental.pallas import tpu as pltpu
from jax.sharding import PartitionSpec as P

MESH = pl.DeviceIdType.MESH
F32 = jnp.float32
BF16 = jnp.bfloat16


def each(count, step):
    if count <= 8:
        for i in range(count):
            step(i)
    else:
        def turn(i, carry):
            step(i)
            return carry

        lax.fori_loop(0, count, turn, 0)


def each_from(first, count, step):
    each(count - first, lambda i: step(i + first))


def kernel(experts, dp, topk, first, slots, padded,
           tok_hbm, ids_hbm, gates_hbm, placement_hbm, wg_hbm, wu_hbm, wd_hbm, out,
           tok, ids, gates, placement,
           wg, wu, wd, tok_s, tok_r, info_s, info_r, group_x, disp_s, rows_r, rows_f, part_f,
           part_s, part_r, back_s, back_r, wsel, mix_s,
           w_sem, s1, r1, si, ri, s2, r2, s3, r3, s4, r4, s5, r5, s6, r6):
    me_e = lax.axis_index("expert")
    me_j = lax.axis_index("dp")
    own, width = tok.shape
    block = width // dp
    group = own * dp
    pairs = group * topk
    lanes = info_s.shape[1]
    total = experts * padded

    if dp == 4:
        low, high = lax.rem(me_j, 2), me_j // 2
        across = (me_j, high * 2 + (1 - low), (1 - high) * 2 + low, (1 - high) * 2 + (1 - low))
        onward = backward = lambda s: across[s]
    else:
        onward = lambda s: lax.rem(me_j + s, dp)
        backward = lambda s: lax.rem(me_j + dp - s, dp)

    def to_dp(src, dst, send, recv, s):
        return pltpu.make_async_remote_copy(
            src_ref=src, dst_ref=dst, send_sem=send, recv_sem=recv,
            device_id={"dp": onward(s)}, device_id_type=MESH)

    def to_expert(src, dst, send, recv, shift):
        return pltpu.make_async_remote_copy(
            src_ref=src, dst_ref=dst, send_sem=send, recv_sem=recv,
            device_id={"expert": lax.rem(me_e + shift, experts)}, device_id_type=MESH)

    def cols(j):
        return pl.ds(pl.multiple_of(j * block, 128), block)

    barrier = pltpu.get_barrier_semaphore()
    for s in range(1, dp):
        pl.semaphore_signal(barrier, inc=1, device_id={"dp": onward(s)}, device_id_type=MESH)

    def greet(d):
        pl.semaphore_signal(barrier, inc=1, device_id={"expert": lax.rem(me_e + d, experts)}, device_id_type=MESH)

    each_from(1, experts, greet)

    pairs_of = ((ids_hbm, ids), (gates_hbm, gates), (placement_hbm, placement), (tok_hbm, tok),
                (wg_hbm, wg), (wu_hbm, wu), (wd_hbm, wd))
    loads = [pltpu.make_async_copy(a, b, w_sem.at[i]) for i, (a, b) in enumerate(pairs_of)]
    for load in loads:
        load.start()
    for load in loads[:4]:
        load.wait()
    loads = loads[4:]

    lane = lax.broadcasted_iota(jnp.int32, (8, lanes), 1)
    line = lax.broadcasted_iota(jnp.int32, (8, lanes), 0)
    id_f = ids[...].astype(F32)
    gate_f = gates[...].astype(F32)
    info = jnp.zeros((8, lanes), F32)
    for t in range(own):
        for k in range(topk):
            here = lane == (me_j * own + t) * topk + k
            value = jnp.where(line == 0, jnp.broadcast_to(id_f[k:k + 1, t:t + 1], (8, lanes)),
                              jnp.broadcast_to(gate_f[k:k + 1, t:t + 1], (8, lanes)))
            info = jnp.where(here, value, info)
    info_s[...] = info
    for s in range(1, dp):
        tok_s[s] = tok[:, cols(onward(s))]
    tok_r[me_j] = tok[:, cols(me_j)]

    pl.semaphore_wait(barrier, dp - 1 + experts - 1)

    for s in range(1, dp):
        to_dp(info_s, info_r.at[s], si.at[s], ri.at[s], s).start()
    for s in range(1, dp):
        to_dp(tok_s.at[s], tok_r.at[me_j], s1.at[s], r1.at[s], s).start()
    for s in range(1, dp):
        to_dp(info_s, info_r.at[s], si.at[s], ri.at[s], s).wait_recv()
        info = info + info_r[s]

    id_row = info[0:1, :]
    gate_row = info[1:2, :]
    at_row = lax.broadcasted_iota(jnp.int32, (pairs, lanes), 0)
    at_lane = lax.broadcasted_iota(jnp.int32, (pairs, lanes), 1)
    id_col = jnp.sum(jnp.where(at_row == at_lane, jnp.broadcast_to(id_row, (pairs, lanes)), 0.0),
                     axis=1, keepdims=True)
    same = jnp.broadcast_to(id_col, (pairs, lanes)) == jnp.broadcast_to(id_row, (pairs, lanes))
    rank = jnp.sum(jnp.where(same, jnp.where(at_row < at_lane, 1.0, 0.0), 0.0), axis=0, keepdims=True)
    limit = jnp.full((1, lanes), float(first), F32)
    listed = placement[...].astype(F32)
    for h in range(placement.shape[1]):
        limit = jnp.where(id_row == jnp.broadcast_to(listed[0:1, h:h + 1], (1, lanes)), float(slots), limit)
    dest = jnp.where(rank < limit, id_row * float(padded) + rank, -1.0)
    dest = jnp.where(lax.broadcasted_iota(jnp.int32, (1, lanes), 1) < pairs, dest, -1.0)
    pick = lax.broadcasted_iota(jnp.int32, (total, lanes), 0).astype(F32) == jnp.broadcast_to(dest, (total, lanes))
    pair_i = lax.broadcasted_iota(jnp.int32, (lanes, group), 0)
    token_i = lax.broadcasted_iota(jnp.int32, (lanes, group), 1) * topk
    fold = jnp.where(pair_i >= token_i, jnp.where(pair_i < token_i + topk, 1.0, 0.0), 0.0).astype(BF16)
    select = jnp.dot(jnp.where(pick, 1.0, 0.0).astype(BF16), fold, preferred_element_type=F32).astype(BF16)

    for s in range(1, dp):
        to_dp(tok_s.at[s], tok_r.at[backward(s)], s1.at[s], r1.at[s], s).wait_recv()
    for j in range(dp):
        group_x[j * own:(j + 1) * own, :] = tok_r[j].astype(F32)
    rows_f[...] = jnp.dot(select, group_x[...].astype(BF16), preferred_element_type=F32)

    def dispatch(d):
        e = lax.rem(me_e + d, experts)
        start = pl.multiple_of(e * padded, 8)
        disp_s[e] = rows_f[pl.ds(start, slots), :].astype(BF16)
        to_expert(disp_s.at[e], rows_r.at[me_j, me_e], s2.at[d], r2.at[d], d).start()

    each_from(1, experts, dispatch)
    rows_r[me_j, me_e] = rows_f[pl.ds(pl.multiple_of(me_e * padded, 8), slots), :].astype(BF16)

    relayed = dp == 4 and experts <= 8
    direct = (1, 2) if relayed else range(1, dp)

    def forward(d):
        g = lax.rem(me_e + experts - d, experts)
        for s in direct:
            to_dp(rows_r.at[me_j, g], rows_r.at[me_j, g], s3.at[s, d], r3.at[s, d], s).start()

    forward(0)
    wsel[...] = jnp.dot(jnp.where(pick, jnp.broadcast_to(gate_row, (total, lanes)), 0.0).astype(BF16), fold,
                        preferred_element_type=F32)


    def arrive(d):
        g = lax.rem(me_e + experts - d, experts)
        to_expert(disp_s.at[g], rows_r.at[me_j, g], s2.at[d], r2.at[d], d).wait_recv()
        forward(d)

    each_from(1, experts, arrive)

    loads[0].wait()
    loads[1].wait()
    contract = (((1,), (1,)), ((), ()))

    def first_of(d):
        return 1 + d % 2

    def relay(d):
        g = lax.rem(me_e + experts - d, experts)
        side = first_of(d)
        j = onward(side)
        to_dp(rows_r.at[j, g], rows_r.at[j, g], s3.at[side, d], r3.at[side, d], side).wait_recv()
        to_dp(rows_r.at[j, g], rows_r.at[j, g], s3.at[3, d], r3.at[3, d], 3 - side).start()

    gate = up = None
    for s in range(dp):
        j = backward(s)

        def take(d):
            g = lax.rem(me_e + experts - d, experts)
            if s > 0 and not (relayed and s == first_of(d)):
                to_dp(rows_r.at[j, g], rows_r.at[j, g], s3.at[s, d], r3.at[s, d], s).wait_recv()
            rows_f[pl.ds(pl.multiple_of(g * padded, 8), slots), :] = rows_r[j, g].astype(F32)

        each(experts, take)
        x = rows_f[...].astype(BF16)
        gate_part = lax.dot_general(x, wg[:, cols(j)], contract, preferred_element_type=F32)
        up_part = lax.dot_general(x, wu[:, cols(j)], contract, preferred_element_type=F32)
        gate = gate_part if gate is None else gate + gate_part
        up = up_part if up is None else up + up_part
        if relayed and s == 0:
            each(experts, relay)
    hidden = (gate / (1.0 + jnp.exp(-gate)) * up).astype(BF16)

    loads[2].wait()
    for s in reversed(range(dp)):
        j = onward(s)
        part_f[...] = jnp.dot(hidden, wd[:, cols(j)], preferred_element_type=F32)
        target = part_s if s > 0 else part_r

        def split(d):
            g = lax.rem(me_e + d, experts)
            start = pl.multiple_of(g * padded, 8)
            target[s, g] = part_f[pl.ds(start, slots), :].astype(BF16)
            if s > 0:
                to_dp(part_s.at[s, g], part_r.at[s, g], s4.at[s, d], r4.at[s, d], s).start()

        each_from(1, experts, split)
        split(0)

    def summed(d):
        g = lax.rem(me_e + d, experts)
        for s in range(1, dp):
            to_dp(part_s.at[s, g], part_r.at[s, g], s4.at[s, d], r4.at[s, d], s).wait_recv()
        value = part_r[0, g].astype(F32)
        for s in range(1, dp):
            value = value + part_r[s, g].astype(F32)
        return value.astype(BF16)

    def give(d):
        g = lax.rem(me_e + d, experts)
        back_s[g] = summed(d)
        to_expert(back_s.at[g], back_r.at[me_e], s5.at[d], r5.at[d], d).start()

    each_from(1, experts, give)
    back_r[me_e] = summed(0)

    def collect(d):
        e = lax.rem(me_e + experts - d, experts)
        to_expert(back_s.at[e], back_r.at[e], s5.at[d], r5.at[d], d).wait_recv()

    each_from(1, experts, collect)

    def place(e):
        rows_f[pl.ds(e * padded, slots), :] = back_r[e].astype(F32)

    each(experts, place)
    group_x[...] = lax.dot_general(wsel[...].astype(BF16), rows_f[...].astype(BF16), (((0,), (0,)), ((), ())),
                                   preferred_element_type=F32)
    for j in range(dp):
        mix_s[j] = group_x[j * own:(j + 1) * own, :].astype(BF16)
    for s in reversed(range(1, dp)):
        to_dp(mix_s.at[onward(s)], out.at[:, cols(me_j)], s6.at[s], r6.at[s], s).start()
    kept = pltpu.make_async_copy(mix_s.at[me_j], out.at[:, cols(me_j)], s6.at[0])
    kept.start()
    kept.wait()
    for s in range(1, dp):
        j = backward(s)
        to_dp(mix_s.at[j], out.at[:, cols(j)], s6.at[s], r6.at[s], s).wait_recv()

    for s in range(1, dp):
        to_dp(info_s, info_r.at[s], si.at[s], ri.at[s], s).wait_send()
        to_dp(tok_s.at[s], tok_r.at[me_j], s1.at[s], r1.at[s], s).wait_send()
        to_dp(mix_s.at[onward(s)], out.at[:, cols(me_j)], s6.at[s], r6.at[s], s).wait_send()

    def left(d):
        g = lax.rem(me_e + experts - d, experts)
        for s in range(1, dp):
            to_dp(rows_r.at[me_j, g], rows_r.at[me_j, g], s3.at[s, d], r3.at[s, d], s).wait_send()
            to_dp(part_s.at[s, g], part_r.at[s, g], s4.at[s, d], r4.at[s, d], s).wait_send()

    def left_expert(d):
        e = lax.rem(me_e + d, experts)
        to_expert(disp_s.at[e], rows_r.at[me_j, me_e], s2.at[d], r2.at[d], d).wait_send()
        to_expert(back_s.at[e], back_r.at[me_e], s5.at[d], r5.at[d], d).wait_send()

    each(experts, left)
    each_from(1, experts, left_expert)


def relay_kernel(experts, dp, topk, first, slots, pad, bands,
                 tok_hbm, ids_hbm, gates_hbm, placement_hbm, wg_hbm, wu_hbm, wd_hbm, out,
                 ids, gates, placement, rows, flat, wg, wu, wd, hid, part_s, part_r, back_s,
                 ready_e, ready_d, l_sem, w_s, w_r, z_s, z_r, d_s, d_r, c_s, c_r, h_s, h_r, p_s, p_r, b_s, b_r):
    me_e = lax.axis_index("expert")
    me_j = lax.axis_index("dp")
    core = lax.rem(me_e, 2)
    z = lax.div(me_e, 2)
    chips = experts // 2
    far = chips - 1
    own = rows.shape[3]
    width = tok_hbm.shape[1]
    half = width // 2
    both = 2 * own
    span = dp * both
    band = width // bands

    def turn(at, q):
        return q + lax.div(at, chips // 2) * (far - 2 * q)

    def chip_at(k):
        q = k - 1 + lax.div(k - 1 + chips - turn(z, z), chips)
        return turn(z, q)

    def seen_from(other):
        q = turn(other, z)
        return q + 1 - lax.div(q + chips - turn(other, other), chips)

    low, high = lax.rem(me_j, 2), lax.div(me_j, 2)
    across = (me_j, high * 2 + (1 - low), (1 - high) * 2 + low, (1 - high) * 2 + (1 - low))
    sibling = z * 2 + (1 - core)

    def to_dp(src, dst, send, recv, s):
        return pltpu.make_async_remote_copy(src_ref=src, dst_ref=dst, send_sem=send, recv_sem=recv,
                                            device_id={"dp": across[s]}, device_id_type=MESH)

    def to_expert(src, dst, send, recv, e):
        return pltpu.make_async_remote_copy(src_ref=src, dst_ref=dst, send_sem=send, recv_sem=recv,
                                            device_id={"expert": e}, device_id_type=MESH)

    def edge(b):
        return 0 if b == 0 else pad + b * band

    def cols(b0, b1):
        return pl.ds(edge(b0), edge(b1) - edge(b0))

    whole = ((0, bands),)
    halves = ((0, bands // 2), (bands // 2, bands))
    single = tuple((b, b + 1) for b in range(bands))
    z_cuts = halves
    cuts = tuple(single if k == far else halves if k == far - 1 else whole for k in range(chips))

    barrier = pltpu.get_barrier_semaphore()

    def tell(sem, axis, to):
        pl.semaphore_signal(sem, inc=1, device_id={axis: to}, device_id_type=MESH)

    tell(barrier, "expert", sibling)
    for s in range(1, dp):
        pl.when(across[s] > me_j)(functools.partial(tell, barrier, "dp", across[s]))
    for q in range(1, chips):
        for o in range(2):
            pl.when(q > z)(functools.partial(tell, barrier, "expert", q * 2 + o))

    def meet_dp(s):
        @pl.when(across[s] > me_j)
        def _():
            pl.semaphore_wait(ready_d.at[s], 1)

    def meet_chip(q, o):
        @pl.when(q > z)
        def _():
            pl.semaphore_wait(ready_e.at[q, o], 1)

    mine = rows.at[core, 0, me_j]
    kept = pl.ds(pl.multiple_of(core * half, 128), half)
    given = pl.ds(pl.multiple_of((1 - core) * half, 128), half)
    loads = [pltpu.make_async_copy(a, b, l_sem.at[i]) for i, (a, b) in enumerate((
        (ids_hbm, ids), (gates_hbm, gates), (placement_hbm, placement),
        (tok_hbm, mine.at[:, pl.ds(pad, width)]),
        (wg_hbm, wg), (wu_hbm, wu), (wd_hbm.at[:, kept], wd.at[core])))]
    for load in loads:
        load.start()
    for load in loads[:3]:
        load.wait()

    lane = lax.broadcasted_iota(jnp.int32, (own, pad), 1)
    line = lax.broadcasted_iota(jnp.int32, (own, pad), 0)
    id_f = ids[...].astype(F32)
    gate_f = gates[...].astype(F32)
    info = jnp.zeros((own, pad), F32)
    for t in range(own):
        for k in range(topk):
            for at, table in ((k, id_f), (topk + k, gate_f)):
                here = jnp.where(line == t, lane, -1) == at
                info = jnp.where(here, jnp.broadcast_to(table[k:k + 1, t:t + 1], (own, pad)), info)
    rows[core, 0, me_j, :, 0:pad] = info.astype(BF16)
    loads[3].wait()
    pl.semaphore_wait(barrier, 1 + 2 * z + me_j)
    for s in range(1, dp):
        pl.when(across[s] < me_j)(functools.partial(tell, ready_d.at[s], "dp", across[s]))
    for q in range(chips - 1):
        for o in range(2):
            pl.when(q < z)(functools.partial(tell, ready_e.at[z, core], "expert", q * 2 + o))

    def sent_to(n):
        before = lax.div(z - n - 1 + chips, chips)
        return before * (z - 1 - n) + (1 - before) * (n + 1)

    def over_z(n, i):
        other = sent_to(n)
        c = cols(*z_cuts[i])
        return to_expert(mine.at[:, c], rows.at[core, seen_from(other), me_j, :, c], z_s.at[n, i],
                         z_r.at[seen_from(other), i], other * 2 + core)

    def from_z(k, i):
        c = cols(*z_cuts[i])
        here = rows.at[core, k, me_j, :, c]
        return to_expert(here, here, z_s.at[k, i], z_r.at[k, i], sibling)

    def over_dp(k, i, s, at):
        here = rows.at[core, k, at, :, cols(*cuts[k][i])]
        return to_dp(here, here, d_s.at[k, s, i], d_r.at[k, s, i], s)

    def across_core(k, i, c):
        here = rows.at[c, k, :, :, cols(*cuts[k][i])]
        return to_expert(here, here, c_s.at[k, i], c_r.at[k, i], sibling)

    for s in range(1, dp):
        meet_dp(s)
        over_dp(0, 0, s, me_j).start()
    for n in range(chips - 1):
        meet_chip(sent_to(n), core)
        for i in range(len(z_cuts)):
            over_z(n, i).start()
    lend = to_expert(wd_hbm.at[:, given], wd.at[core], w_s, w_r, sibling)
    lend.start()

    def pass_on(k):
        for i, (b0, b1) in enumerate(cuts[k]):
            for n, (a0, a1) in enumerate(z_cuts):
                if a0 < b1 and a1 > b0 and a0 >= b0:
                    from_z(k, n).wait_recv()
            for s in range(1, dp):
                over_dp(k, i, s, me_j).start()

    def share(k, i):
        for s in range(1, dp):
            over_dp(k, i, s, across[s]).wait_recv()
        across_core(k, i, core).start()

    def spread(k, i):
        across_core(k, i, 1 - core).wait_recv()
        c = cols(*cuts[k][i])
        at = (k % 2) * span
        for o in range(2):
            for j in range(dp):
                start = at + j * both + o * own
                flat[k // 2, start:start + own, c] = rows[o, k, j, :, c].astype(F32)

    pass_on(1)
    share(0, 0)
    for k in range(2, chips):
        pass_on(k)
    spread(0, 0)
    share(1, 0)
    spread(1, 0)

    contract = (((1,), (1,)), ((), ()))
    loads[4].wait()
    loads[5].wait()

    def gate_up(p, b, gate, up):
        c = pl.ds(b * band, band)
        x = flat[p, :, pl.ds(pad + b * band, band)].astype(BF16)
        gate_part = lax.dot_general(x, wg[:, c], contract, preferred_element_type=F32)
        up_part = lax.dot_general(x, wu[:, c], contract, preferred_element_type=F32)
        return (gate_part, up_part) if gate is None else (gate + gate_part, up + up_part)

    me_f = me_e.astype(F32)
    many = 2 * span
    r = lax.broadcasted_iota(jnp.int32, (many, many), 0)
    q = lax.broadcasted_iota(jnp.int32, (many, many), 1)
    same = jnp.where(lax.div(r, span) == lax.div(q, span), lax.rem(lax.div(r, own), 2), 2) == lax.rem(lax.div(q, own), 2)
    below = jnp.where(same, jnp.where(q < r, 1.0, 0.0), 0.0).astype(BF16)
    listed = placement[0:1, :].astype(F32)
    extra = jnp.sum(jnp.where(listed == me_f, float(slots - first), 0.0), axis=1, keepdims=True)
    limit = float(first) + extra

    def weigh(p):
        told = flat[p, :, 0:pad]
        named = jnp.zeros((many, 1), F32)
        value = jnp.zeros((many, 1), F32)
        for k in range(topk):
            hit = told[:, k:k + 1] == me_f
            named = named + jnp.where(hit, 1.0, 0.0)
            value = value + jnp.where(hit, told[:, topk + k:topk + k + 1], 0.0)
        rank = jnp.dot(below, jnp.broadcast_to(named, (many, 128)).astype(BF16), preferred_element_type=F32)[:, 0:1]
        return jnp.where(rank < limit, value, 0.0)

    def swap(p, at):
        here = hid.at[at, p]
        return to_expert(here, here, h_s.at[p], h_r.at[p], sibling)

    def finish(p, gate, up, weight):
        hid[core, p] = (gate / (1.0 + jnp.exp(-gate)) * up * weight).astype(BF16)
        swap(p, core).start()

    def over_part(k, s):
        return to_dp(part_s.at[k * dp + across[s]], part_r.at[k, s], p_s.at[k, s], p_r.at[k, s], s)

    piece = half // bands

    def down(p):
        swap(p, 1 - core).wait_recv()
        for b in range(bands):
            c = pl.ds(b * piece, piece)
            total = jnp.dot(hid[0, p], wd[0, :, c], preferred_element_type=F32)
            total = total + jnp.dot(hid[1, p], wd[1, :, c], preferred_element_type=F32)
            part_s[2 * p * dp:2 * (p + 1) * dp, :, c] = total.reshape(2 * dp, both, piece).astype(BF16)

    def send_part(k):
        for s in reversed(range(1, dp)):
            over_part(k, s).start()

    gate = up = None
    todo = [(k, i) for k in range(2, chips) for i in range(len(cuts[k]))]
    for b in range(bands):
        gate, up = gate_up(0, b, gate, up)
        for k, i in todo[b * len(todo) // bands:(b + 1) * len(todo) // bands]:
            share(k, i)
    finish(0, gate, up, weigh(0))

    gate = up = None
    for b in range(bands):
        for k in range(2, chips):
            for i, (b0, b1) in enumerate(cuts[k]):
                if b0 == b:
                    spread(k, i)
        gate, up = gate_up(1, b, gate, up)
    finish(1, gate, up, weigh(1))

    loads[6].wait()
    to_expert(wd.at[1 - core], wd.at[1 - core], w_s, w_r, sibling).wait_recv()
    down(0)
    send_part(1)
    down(1)
    for k in (3, 2, 0):
        send_part(k)
    for k in range(1, chips):
        meet_chip(chip_at(k), 1 - core)

    def over_back(k, o):
        e = sibling if k == 0 else chip_at(k) * 2 + o
        return to_expert(back_s.at[k, o], out.at[z, :, kept], b_s.at[k, o], b_r.at[z, core], e)

    for k in (1, 3, 2, 0):
        value = part_s[k * dp + me_j].astype(F32)
        for s in range(1, dp):
            over_part(k, s).wait_recv()
            value = value + part_r[k, s].astype(F32)
        for o in range(2):
            back_s[k, o] = value[o * own:(o + 1) * own, :].astype(BF16)
        if k > 0:
            for o in range(2):
                over_back(k, o).start()
    give = to_expert(back_s.at[0, 1 - core], out.at[z, :, kept], b_s.at[0, 0], b_r.at[z, core], sibling)
    give.start()
    keep = pltpu.make_async_copy(back_s.at[0, core], out.at[z, :, kept], b_s.at[0, 1])
    keep.start()

    keep.wait()
    to_expert(back_s.at[0, core], out.at[z, :, given], b_s.at[0, 0], b_r.at[z, 1 - core], sibling).wait_recv()
    for k in range(1, chips):
        other = chip_at(k)
        for o in range(2):
            to_expert(back_s.at[k, o], out.at[other, :, pl.ds(o * half, half)], b_s.at[k, o], b_r.at[other, o],
                      sibling).wait_recv()

    lend.wait_send()
    for p in range(2):
        swap(p, core).wait_send()
    give.wait_send()
    for k in range(chips):
        for i in range(len(z_cuts)):
            if k > 0:
                over_z(k - 1, i).wait_send()
        for i in range(len(cuts[k])):
            for s in range(1, dp):
                over_dp(k, i, s, me_j).wait_send()
            across_core(k, i, core).wait_send()
        for s in range(1, dp):
            over_part(k, s).wait_send()
        if k > 0:
            for o in range(2):
                over_back(k, o).wait_send()


def relayed(tokens, expert_ids, gate_weights, placement, w_gate, w_up, w_down, experts, dp, first, slots):
    own, width = tokens.shape
    topk = expert_ids.shape[1]
    units = w_gate.shape[1]
    chips = experts // 2
    bands = 4
    pad = 128
    half = width // 2
    hbm = pl.BlockSpec(memory_space=pl.ANY)
    dma = pltpu.SemaphoreType.DMA
    parts = pl.pallas_call(
        functools.partial(relay_kernel, experts, dp, topk, first, slots, pad, bands),
        out_shape=jax.ShapeDtypeStruct((chips, own, width), BF16),
        in_specs=[hbm] * 7,
        out_specs=hbm,
        scratch_shapes=[
            pltpu.VMEM((topk, own), jnp.int32),
            pltpu.VMEM((topk, own), BF16),
            pltpu.VMEM(placement.shape, jnp.int32),
            pltpu.VMEM((2, chips, dp, own, pad + width), BF16),
            pltpu.VMEM((chips // 2, 4 * dp * own, pad + width), F32),
            pltpu.VMEM((units, width), BF16),
            pltpu.VMEM((units, width), BF16),
            pltpu.VMEM((2, units, half), BF16),
            pltpu.VMEM((2, 2, 4 * dp * own, units), BF16),
            pltpu.VMEM((chips * dp, 2 * own, half), BF16),
            pltpu.VMEM((chips, dp, 2 * own, half), BF16),
            pltpu.VMEM((chips, 2, own, half), BF16),
            pltpu.SemaphoreType.REGULAR((chips, 2)), pltpu.SemaphoreType.REGULAR((dp,)),
            dma((7,)),
            dma, dma,
            dma((chips, 2)), dma((chips, 2)),
            dma((chips, dp, bands)), dma((chips, dp, bands)),
            dma((chips, bands)), dma((chips, bands)),
            dma((2,)), dma((2,)),
            dma((chips, dp)), dma((chips, dp)),
            dma((chips, 2)), dma((chips, 2)),
        ],
        compiler_params=pltpu.CompilerParams(
            collective_id=1, has_side_effects=True, vmem_limit_bytes=56 << 20
        ),
    )(tokens, expert_ids.T, gate_weights.T, placement, w_gate[0], w_up[0], w_down[0])
    return jnp.sum(parts.astype(F32), axis=0).astype(BF16)


def body(tokens, expert_ids, gate_weights, placement, w_gate, w_up, w_down):
    experts = lax.axis_size("expert")
    dp = lax.axis_size("dp")
    own, width = tokens.shape
    topk = expert_ids.shape[1]
    group = own * dp
    first = max(2, group * topk // experts)
    slots = first + max(1, first // 2)
    if dp == 4 and experts == 8 and own == 4 and width % 1024 == 0:
        return relayed(tokens, expert_ids, gate_weights, placement, w_gate, w_up, w_down, experts, dp, first, slots)
    padded = -(-slots // 8) * 8
    lanes = -(-group * topk // 128) * 128
    block = width // dp
    units = w_gate.shape[1]
    total = experts * padded
    hbm = pl.BlockSpec(memory_space=pl.ANY)
    dma = pltpu.SemaphoreType.DMA
    return pl.pallas_call(
        functools.partial(kernel, experts, dp, topk, first, slots, padded),
        out_shape=jax.ShapeDtypeStruct((own, width), BF16),
        in_specs=[hbm] * 7,
        out_specs=hbm,
        scratch_shapes=[
            pltpu.VMEM((own, width), BF16),
            pltpu.VMEM((topk, own), jnp.int32),
            pltpu.VMEM((topk, own), BF16),
            pltpu.VMEM(placement.shape, jnp.int32),
            pltpu.VMEM((units, width), BF16),
            pltpu.VMEM((units, width), BF16),
            pltpu.VMEM((units, width), BF16),
            pltpu.VMEM((dp, own, block), BF16),
            pltpu.VMEM((dp, own, block), BF16),
            pltpu.VMEM((8, lanes), F32),
            pltpu.VMEM((dp, 8, lanes), F32),
            pltpu.VMEM((group, block), F32),
            pltpu.VMEM((experts, slots, block), BF16),
            pltpu.VMEM((dp, experts, slots, block), BF16),
            pltpu.VMEM((total, block), F32),
            pltpu.VMEM((total, block), F32),
            pltpu.VMEM((dp, experts, slots, block), BF16),
            pltpu.VMEM((dp, experts, slots, block), BF16),
            pltpu.VMEM((experts, slots, block), BF16),
            pltpu.VMEM((experts, slots, block), BF16),
            pltpu.VMEM((total, group), F32),
            pltpu.VMEM((dp, own, block), BF16),
            dma((7,)),
            dma((dp,)), dma((dp,)), dma((dp,)), dma((dp,)),
            dma((experts,)), dma((experts,)),
            dma((dp, experts)), dma((dp, experts)),
            dma((dp, experts)), dma((dp, experts)),
            dma((experts,)), dma((experts,)),
            dma((dp,)), dma((dp,)),
        ],
        compiler_params=pltpu.CompilerParams(
            collective_id=0, has_side_effects=True, vmem_limit_bytes=56 << 20
        ),
    )(tokens, expert_ids.T, gate_weights.T, placement, w_gate[0], w_up[0], w_down[0])


def solution(mesh):
    placed = (
        P(("groups", "expert", "dp"), None),
        P(("groups", "expert", "dp"), None),
        P(("groups", "expert", "dp"), None),
        P("groups", None),
        P("expert", "dp", None),
        P("expert", "dp", None),
        P("expert", "dp", None),
    )
    return jax.shard_map(
        body,
        mesh=mesh,
        in_specs=placed,
        out_specs=P(("groups", "expert", "dp"), None),
        check_vma=False,
    )
```

```python
import functools

import jax
import jax.numpy as jnp
from jax import lax
from jax.experimental import pallas as pl
from jax.experimental.pallas import tpu as pltpu
from jax.sharding import PartitionSpec as P

MESH = pl.DeviceIdType.MESH
F32 = jnp.float32
BF16 = jnp.bfloat16


def each(count, step):
    if count <= 8:
        for i in range(count):
            step(i)
    else:
        def turn(i, carry):
            step(i)
            return carry

        lax.fori_loop(0, count, turn, 0)


def each_from(first, count, step):
    each(count - first, lambda i: step(i + first))


def kernel(experts, dp, topk, first, slots, padded,
           tok_hbm, ids_hbm, gates_hbm, placement_hbm, wg_hbm, wu_hbm, wd_hbm, out,
           tok, ids, gates, placement,
           wg, wu, wd, tok_s, tok_r, info_s, info_r, group_x, disp_s, rows_r, rows_f, part_f,
           part_s, part_r, back_s, back_r, wsel, mix_s,
           w_sem, s1, r1, si, ri, s2, r2, s3, r3, s4, r4, s5, r5, s6, r6):
    me_e = lax.axis_index("expert")
    me_j = lax.axis_index("dp")
    own, width = tok.shape
    block = width // dp
    group = own * dp
    pairs = group * topk
    lanes = info_s.shape[1]
    total = experts * padded

    if dp == 4:
        low, high = lax.rem(me_j, 2), me_j // 2
        across = (me_j, high * 2 + (1 - low), (1 - high) * 2 + low, (1 - high) * 2 + (1 - low))
        onward = backward = lambda s: across[s]
    else:
        onward = lambda s: lax.rem(me_j + s, dp)
        backward = lambda s: lax.rem(me_j + dp - s, dp)

    def to_dp(src, dst, send, recv, s):
        return pltpu.make_async_remote_copy(
            src_ref=src, dst_ref=dst, send_sem=send, recv_sem=recv,
            device_id={"dp": onward(s)}, device_id_type=MESH)

    def to_expert(src, dst, send, recv, shift):
        return pltpu.make_async_remote_copy(
            src_ref=src, dst_ref=dst, send_sem=send, recv_sem=recv,
            device_id={"expert": lax.rem(me_e + shift, experts)}, device_id_type=MESH)

    def cols(j):
        return pl.ds(pl.multiple_of(j * block, 128), block)

    barrier = pltpu.get_barrier_semaphore()
    for s in range(1, dp):
        pl.semaphore_signal(barrier, inc=1, device_id={"dp": onward(s)}, device_id_type=MESH)

    def greet(d):
        pl.semaphore_signal(barrier, inc=1, device_id={"expert": lax.rem(me_e + d, experts)}, device_id_type=MESH)

    each_from(1, experts, greet)

    pairs_of = ((ids_hbm, ids), (gates_hbm, gates), (placement_hbm, placement), (tok_hbm, tok),
                (wg_hbm, wg), (wu_hbm, wu), (wd_hbm, wd))
    loads = [pltpu.make_async_copy(a, b, w_sem.at[i]) for i, (a, b) in enumerate(pairs_of)]
    for load in loads:
        load.start()
    for load in loads[:4]:
        load.wait()
    loads = loads[4:]

    lane = lax.broadcasted_iota(jnp.int32, (8, lanes), 1)
    line = lax.broadcasted_iota(jnp.int32, (8, lanes), 0)
    id_f = ids[...].astype(F32)
    gate_f = gates[...].astype(F32)
    info = jnp.zeros((8, lanes), F32)
    for t in range(own):
        for k in range(topk):
            here = lane == (me_j * own + t) * topk + k
            value = jnp.where(line == 0, jnp.broadcast_to(id_f[k:k + 1, t:t + 1], (8, lanes)),
                              jnp.broadcast_to(gate_f[k:k + 1, t:t + 1], (8, lanes)))
            info = jnp.where(here, value, info)
    info_s[...] = info
    for s in range(1, dp):
        tok_s[s] = tok[:, cols(onward(s))]
    tok_r[me_j] = tok[:, cols(me_j)]

    pl.semaphore_wait(barrier, dp - 1 + experts - 1)

    for s in range(1, dp):
        to_dp(info_s, info_r.at[s], si.at[s], ri.at[s], s).start()
    for s in range(1, dp):
        to_dp(tok_s.at[s], tok_r.at[me_j], s1.at[s], r1.at[s], s).start()
    for s in range(1, dp):
        to_dp(info_s, info_r.at[s], si.at[s], ri.at[s], s).wait_recv()
        info = info + info_r[s]

    id_row = info[0:1, :]
    gate_row = info[1:2, :]
    at_row = lax.broadcasted_iota(jnp.int32, (pairs, lanes), 0)
    at_lane = lax.broadcasted_iota(jnp.int32, (pairs, lanes), 1)
    id_col = jnp.sum(jnp.where(at_row == at_lane, jnp.broadcast_to(id_row, (pairs, lanes)), 0.0),
                     axis=1, keepdims=True)
    same = jnp.broadcast_to(id_col, (pairs, lanes)) == jnp.broadcast_to(id_row, (pairs, lanes))
    rank = jnp.sum(jnp.where(same, jnp.where(at_row < at_lane, 1.0, 0.0), 0.0), axis=0, keepdims=True)
    limit = jnp.full((1, lanes), float(first), F32)
    listed = placement[...].astype(F32)
    for h in range(placement.shape[1]):
        limit = jnp.where(id_row == jnp.broadcast_to(listed[0:1, h:h + 1], (1, lanes)), float(slots), limit)
    dest = jnp.where(rank < limit, id_row * float(padded) + rank, -1.0)
    dest = jnp.where(lax.broadcasted_iota(jnp.int32, (1, lanes), 1) < pairs, dest, -1.0)
    pick = lax.broadcasted_iota(jnp.int32, (total, lanes), 0).astype(F32) == jnp.broadcast_to(dest, (total, lanes))
    pair_i = lax.broadcasted_iota(jnp.int32, (lanes, group), 0)
    token_i = lax.broadcasted_iota(jnp.int32, (lanes, group), 1) * topk
    fold = jnp.where(pair_i >= token_i, jnp.where(pair_i < token_i + topk, 1.0, 0.0), 0.0).astype(BF16)
    select = jnp.dot(jnp.where(pick, 1.0, 0.0).astype(BF16), fold, preferred_element_type=F32).astype(BF16)

    for s in range(1, dp):
        to_dp(tok_s.at[s], tok_r.at[backward(s)], s1.at[s], r1.at[s], s).wait_recv()
    for j in range(dp):
        group_x[j * own:(j + 1) * own, :] = tok_r[j].astype(F32)
    rows_f[...] = jnp.dot(select, group_x[...].astype(BF16), preferred_element_type=F32)

    def dispatch(d):
        e = lax.rem(me_e + d, experts)
        start = pl.multiple_of(e * padded, 8)
        disp_s[e] = rows_f[pl.ds(start, slots), :].astype(BF16)
        to_expert(disp_s.at[e], rows_r.at[me_j, me_e], s2.at[d], r2.at[d], d).start()

    each_from(1, experts, dispatch)
    rows_r[me_j, me_e] = rows_f[pl.ds(pl.multiple_of(me_e * padded, 8), slots), :].astype(BF16)

    relayed = dp == 4 and experts <= 8
    direct = (1, 2) if relayed else range(1, dp)

    def forward(d):
        g = lax.rem(me_e + experts - d, experts)
        for s in direct:
            to_dp(rows_r.at[me_j, g], rows_r.at[me_j, g], s3.at[s, d], r3.at[s, d], s).start()

    forward(0)
    wsel[...] = jnp.dot(jnp.where(pick, jnp.broadcast_to(gate_row, (total, lanes)), 0.0).astype(BF16), fold,
                        preferred_element_type=F32)


    def arrive(d):
        g = lax.rem(me_e + experts - d, experts)
        to_expert(disp_s.at[g], rows_r.at[me_j, g], s2.at[d], r2.at[d], d).wait_recv()
        forward(d)

    each_from(1, experts, arrive)

    loads[0].wait()
    loads[1].wait()
    contract = (((1,), (1,)), ((), ()))

    def first_of(d):
        return 1 + d % 2

    def relay(d):
        g = lax.rem(me_e + experts - d, experts)
        side = first_of(d)
        j = onward(side)
        to_dp(rows_r.at[j, g], rows_r.at[j, g], s3.at[side, d], r3.at[side, d], side).wait_recv()
        to_dp(rows_r.at[j, g], rows_r.at[j, g], s3.at[3, d], r3.at[3, d], 3 - side).start()

    gate = up = None
    for s in range(dp):
        j = backward(s)

        def take(d):
            g = lax.rem(me_e + experts - d, experts)
            if s > 0 and not (relayed and s == first_of(d)):
                to_dp(rows_r.at[j, g], rows_r.at[j, g], s3.at[s, d], r3.at[s, d], s).wait_recv()
            rows_f[pl.ds(pl.multiple_of(g * padded, 8), slots), :] = rows_r[j, g].astype(F32)

        each(experts, take)
        x = rows_f[...].astype(BF16)
        gate_part = lax.dot_general(x, wg[:, cols(j)], contract, preferred_element_type=F32)
        up_part = lax.dot_general(x, wu[:, cols(j)], contract, preferred_element_type=F32)
        gate = gate_part if gate is None else gate + gate_part
        up = up_part if up is None else up + up_part
        if relayed and s == 0:
            each(experts, relay)
    hidden = (gate / (1.0 + jnp.exp(-gate)) * up).astype(BF16)

    loads[2].wait()
    for s in reversed(range(dp)):
        j = onward(s)
        part_f[...] = jnp.dot(hidden, wd[:, cols(j)], preferred_element_type=F32)
        target = part_s if s > 0 else part_r

        def split(d):
            g = lax.rem(me_e + d, experts)
            start = pl.multiple_of(g * padded, 8)
            target[s, g] = part_f[pl.ds(start, slots), :].astype(BF16)
            if s > 0:
                to_dp(part_s.at[s, g], part_r.at[s, g], s4.at[s, d], r4.at[s, d], s).start()

        each_from(1, experts, split)
        split(0)

    def summed(d):
        g = lax.rem(me_e + d, experts)
        for s in range(1, dp):
            to_dp(part_s.at[s, g], part_r.at[s, g], s4.at[s, d], r4.at[s, d], s).wait_recv()
        value = part_r[0, g].astype(F32)
        for s in range(1, dp):
            value = value + part_r[s, g].astype(F32)
        return value.astype(BF16)

    def give(d):
        g = lax.rem(me_e + d, experts)
        back_s[g] = summed(d)
        to_expert(back_s.at[g], back_r.at[me_e], s5.at[d], r5.at[d], d).start()

    each_from(1, experts, give)
    back_r[me_e] = summed(0)

    def collect(d):
        e = lax.rem(me_e + experts - d, experts)
        to_expert(back_s.at[e], back_r.at[e], s5.at[d], r5.at[d], d).wait_recv()

    each_from(1, experts, collect)

    def place(e):
        rows_f[pl.ds(e * padded, slots), :] = back_r[e].astype(F32)

    each(experts, place)
    group_x[...] = lax.dot_general(wsel[...].astype(BF16), rows_f[...].astype(BF16), (((0,), (0,)), ((), ())),
                                   preferred_element_type=F32)
    for j in range(dp):
        mix_s[j] = group_x[j * own:(j + 1) * own, :].astype(BF16)
    for s in reversed(range(1, dp)):
        to_dp(mix_s.at[onward(s)], out.at[:, cols(me_j)], s6.at[s], r6.at[s], s).start()
    kept = pltpu.make_async_copy(mix_s.at[me_j], out.at[:, cols(me_j)], s6.at[0])
    kept.start()
    kept.wait()
    for s in range(1, dp):
        j = backward(s)
        to_dp(mix_s.at[j], out.at[:, cols(j)], s6.at[s], r6.at[s], s).wait_recv()

    for s in range(1, dp):
        to_dp(info_s, info_r.at[s], si.at[s], ri.at[s], s).wait_send()
        to_dp(tok_s.at[s], tok_r.at[me_j], s1.at[s], r1.at[s], s).wait_send()
        to_dp(mix_s.at[onward(s)], out.at[:, cols(me_j)], s6.at[s], r6.at[s], s).wait_send()

    def left(d):
        g = lax.rem(me_e + experts - d, experts)
        for s in range(1, dp):
            to_dp(rows_r.at[me_j, g], rows_r.at[me_j, g], s3.at[s, d], r3.at[s, d], s).wait_send()
            to_dp(part_s.at[s, g], part_r.at[s, g], s4.at[s, d], r4.at[s, d], s).wait_send()

    def left_expert(d):
        e = lax.rem(me_e + d, experts)
        to_expert(disp_s.at[e], rows_r.at[me_j, me_e], s2.at[d], r2.at[d], d).wait_send()
        to_expert(back_s.at[e], back_r.at[me_e], s5.at[d], r5.at[d], d).wait_send()

    each(experts, left)
    each_from(1, experts, left_expert)


def relay_kernel(experts, dp, topk, first, slots, pad, bands, cuts,
                 tok_hbm, ids_hbm, gates_hbm, placement_hbm, wg_hbm, wu_hbm, wd_hbm, out,
                 ids, gates, placement, rows, flat, wgu, wd, acc, hid, part_s, part_r, back_s,
                 ready_e, ready_d, l_sem, w_sem, z_s, z_r, d_s, d_r, f_s, c_s, c_r, h_sem, p_s, p_r, b_s, b_r):
    me_e = lax.axis_index("expert")
    me_j = lax.axis_index("dp")
    core = lax.rem(me_e, 2)
    z = lax.div(me_e, 2)
    chips = experts // 2
    far = chips - 1
    own = rows.shape[3]
    width = tok_hbm.shape[1]
    units = wg_hbm.shape[0]
    half = width // 2
    both = 2 * own
    span = dp * both
    many = chips * span
    band = width // bands

    def turn(at, q):
        return q + lax.div(at, chips // 2) * (far - 2 * q)

    def chip_at(k):
        q = k - 1 + lax.div(k - 1 + chips - turn(z, z), chips)
        return turn(z, q)

    def seen_from(other):
        q = turn(other, z)
        return q + 1 - lax.div(q + chips - turn(other, other), chips)

    def sent_to(n):
        before = lax.div(z - n - 1 + chips, chips)
        return before * (z - 1 - n) + (1 - before) * (n + 1)

    low, high = lax.rem(me_j, 2), lax.div(me_j, 2)
    across = (me_j, high * 2 + (1 - low), (1 - high) * 2 + low, (1 - high) * 2 + (1 - low))
    sibling = z * 2 + (1 - core)

    def to_dp(src, dst, send, recv, s):
        return pltpu.make_async_remote_copy(src_ref=src, dst_ref=dst, send_sem=send, recv_sem=recv,
                                            device_id={"dp": across[s]}, device_id_type=MESH)

    def to_expert(src, dst, send, recv, e):
        return pltpu.make_async_remote_copy(src_ref=src, dst_ref=dst, send_sem=send, recv_sem=recv,
                                            device_id={"expert": e}, device_id_type=MESH)

    def landed(ref, sem):
        to_expert(ref, ref, sem, sem, sibling).wait_recv()

    def left(ref, sem):
        to_expert(ref, ref, sem, sem, sibling).wait_send()

    def edge(b):
        return 0 if b == 0 else pad + b * band

    def cols(b0, b1):
        return pl.ds(edge(b0), edge(b1) - edge(b0))

    z_cuts = ((0, bands // 2), (bands // 2, bands))
    at_cut = {}
    for k in range(chips):
        for i in range(len(cuts[k])):
            at_cut[k, i] = len(at_cut)

    barrier = pltpu.get_barrier_semaphore()

    def tell(sem, axis, to):
        pl.semaphore_signal(sem, inc=1, device_id={axis: to}, device_id_type=MESH)

    tell(barrier, "expert", sibling)
    for s in range(1, dp):
        pl.when(across[s] > me_j)(functools.partial(tell, barrier, "dp", across[s]))
    for q in range(1, chips):
        for o in range(2):
            pl.when(q > z)(functools.partial(tell, barrier, "expert", q * 2 + o))

    def meet_dp(s):
        @pl.when(across[s] > me_j)
        def _():
            pl.semaphore_wait(ready_d.at[s - 1], 1)

    def meet_chip(q, o):
        @pl.when(q > z)
        def _():
            pl.semaphore_wait(ready_e.at[q - 1, o], 1)

    mine = rows.at[core, 0, me_j]
    kept = pl.ds(pl.multiple_of(core * half, 128), half)
    given = pl.ds(pl.multiple_of((1 - core) * half, 128), half)
    loads = [pltpu.make_async_copy(a, b, l_sem.at[i]) for i, (a, b) in enumerate((
        (ids_hbm, ids), (gates_hbm, gates), (placement_hbm, placement),
        (tok_hbm, mine.at[:, pl.ds(pad, width)]),
        (wg_hbm, wgu.at[pl.ds(0, units)]), (wu_hbm, wgu.at[pl.ds(units, units)]),
        (wd_hbm.at[:, kept], wd.at[core])))]
    for load in loads:
        load.start()
    pl.semaphore_wait(barrier, 1 + 2 * z + me_j)
    for q in range(chips - 1):
        for o in range(2):
            pl.when(q < z)(functools.partial(tell, ready_e.at[z - 1, core], "expert", q * 2 + o))
    for s in range(1, dp):
        pl.when(across[s] < me_j)(functools.partial(tell, ready_d.at[s - 1], "dp", across[s]))

    for load in loads[:3]:
        load.wait()
    lane = lax.broadcasted_iota(jnp.int32, (own, pad), 1)
    line = lax.broadcasted_iota(jnp.int32, (own, pad), 0)
    id_f = ids[...].astype(F32)
    gate_f = gates[...].astype(F32)
    info = jnp.zeros((own, pad), F32)
    for t in range(own):
        for k in range(topk):
            for at, table in ((k, id_f), (topk + k, gate_f)):
                here = jnp.where(line == t, lane, -1) == at
                info = jnp.where(here, jnp.broadcast_to(table[k:k + 1, t:t + 1], (own, pad)), info)
    rows[core, 0, me_j, :, 0:pad] = info.astype(BF16)
    loads[3].wait()

    def over_dp(k, i, s, at):
        here = rows.at[core, k, at, :, cols(*cuts[k][i])]
        return to_dp(here, here, d_s.at[k], d_r.at[at_cut[k, i]], s)

    for s in range(1, dp):
        meet_dp(s)
        over_dp(0, 0, s, me_j).start()
    for n in range(chips - 1):
        other = sent_to(n)
        k = seen_from(other)
        meet_chip(other, core)
        for i in range(len(z_cuts)):
            c = cols(*z_cuts[i])
            to_expert(mine.at[:, c], rows.at[core, k, me_j, :, c], z_s, z_r.at[k - 1, i], other * 2 + core).start()
    lend = to_expert(wd_hbm.at[:, given], wd.at[core], w_sem.at[0], w_sem.at[1], sibling)
    lend.start()

    def pass_on(k):
        for i, (b0, b1) in enumerate(cuts[k]):
            for n, (a0, a1) in enumerate(z_cuts):
                if b0 <= a0 < b1:
                    landed(rows.at[core, k, me_j, :, cols(a0, a1)], z_r.at[k - 1, n])

            def onward():
                for s in range(1, dp):
                    over_dp(k, i, s, me_j).start()

            if k == far:
                pl.when(z != far)(onward)
            else:
                onward()

    def share(k, i):
        c = cols(*cuts[k][i])
        landed(rows.at[core, k, pl.ds(0, dp - 1), :, c], d_r.at[at_cut[k, i]])
        here = rows.at[core, k, :, :, c]
        to_expert(here, here, c_s.at[k], c_r.at[at_cut[k, i]], sibling).start()

    def spread(k, i):
        c = cols(*cuts[k][i])
        landed(rows.at[1 - core, k, :, :, c], c_r.at[at_cut[k, i]])
        for o in range(2):
            for j in range(dp):
                start = k * span + j * both + o * own
                flat[start:start + own, c] = rows[o, k, j, :, c].astype(F32)

    pass_on(1)
    share(0, 0)

    @pl.when(z == 0)
    def _():
        for i in range(len(cuts[far])):
            c = cols(*cuts[far][i])
            for s in range(1, dp):
                to_expert(rows.at[core, 0, across[s], :, c], rows.at[core, far, across[s], :, c], f_s,
                          d_r.at[at_cut[far, i]], far * 2 + core).start()

    for k in range(2, chips):
        pass_on(k)
    spread(0, 0)
    for k in range(1, chips):
        for i in range(len(cuts[k])):
            share(k, i)
        if k > 1:
            for i in range(len(cuts[k - 1])):
                spread(k - 1, i)

    contract = (((1,), (1,)), ((), ()))
    loads[4].wait()
    loads[5].wait()
    me_f = me_e.astype(F32)
    weight = None
    for b in range(bands):
        for i, (b0, b1) in enumerate(cuts[far]):
            if b0 == b:
                spread(far, i)
        x = flat[:, pl.ds(pad + b * band, band)].astype(BF16)
        total = lax.dot_general(x, wgu[:, pl.ds(b * band, band)], contract, preferred_element_type=F32)
        if b == 0:
            r = lax.broadcasted_iota(jnp.int32, (many, many), 0)
            q = lax.broadcasted_iota(jnp.int32, (many, many), 1)
            of_r = jnp.where(lax.div(r, span) == lax.div(q, span), lax.rem(lax.div(r, own), 2), 2)
            same = of_r == lax.rem(lax.div(q, own), 2)
            below = jnp.where(same, jnp.where(q < r, 1.0, 0.0), 0.0).astype(BF16)
            listed = placement[0:1, :].astype(F32)
            extra = jnp.sum(jnp.where(listed == me_f, float(slots - first), 0.0), axis=1, keepdims=True)
            told = flat[:, 0:pad]
            named = jnp.zeros((many, 1), F32)
            value = jnp.zeros((many, 1), F32)
            for k in range(topk):
                hit = told[:, k:k + 1] == me_f
                named = named + jnp.where(hit, 1.0, 0.0)
                value = value + jnp.where(hit, told[:, topk + k:topk + k + 1], 0.0)
            rank = jnp.dot(below, jnp.broadcast_to(named, (many, 128)).astype(BF16), preferred_element_type=F32)[:, 0:1]
            weight = jnp.where(rank < float(first) + extra, value, 0.0)
            acc[...] = total
        elif b < bands - 1:
            acc[...] += total
        else:
            total = acc[...] + total
            gate, up = total[:, :units], total[:, units:]
            hid[core] = (gate / (1.0 + jnp.exp(-gate)) * up * weight).astype(BF16)

    swap = to_expert(hid.at[core], hid.at[core], h_sem.at[0], h_sem.at[1], sibling)
    swap.start()
    loads[6].wait()
    landed(wd.at[1 - core], w_sem.at[1])
    landed(hid.at[1 - core], h_sem.at[1])

    def send_part(k, c):
        for s in reversed(range(1, dp)):
            to_dp(part_s.at[k * dp + across[s], :, c], part_r.at[k, s - 1, :, c], p_s.at[k], p_r.at[k], s).start()

    piece = half // bands
    for b in range(bands):
        c = pl.ds(b * piece, piece)
        total = jnp.dot(hid[0], wd[0, :, c], preferred_element_type=F32)
        total = total + jnp.dot(hid[1], wd[1, :, c], preferred_element_type=F32)
        part_s[:, :, c] = total.reshape(chips * dp, both, piece).astype(BF16)
        send_part(far, c)
    for k in reversed(range(far)):
        send_part(k, pl.ds(0, half))
    for k in range(1, chips):
        meet_chip(chip_at(k), 1 - core)

    for k in reversed(range(chips)):
        value = part_s[k * dp + me_j].astype(F32)
        landed(part_r.at[k], p_r.at[k])
        for s in range(dp - 1):
            value = value + part_r[k, s].astype(F32)
        for o in range(2):
            back_s[k, o] = value[o * own:(o + 1) * own, :].astype(BF16)
        if k > 0:
            for o in range(2):
                to_expert(back_s.at[k, o], out.at[z, :, kept], b_s.at[0], b_r.at[0], chip_at(k) * 2 + o).start()
    give = to_expert(back_s.at[0, 1 - core], out.at[z, :, kept], b_s.at[1], b_r.at[1], sibling)
    give.start()
    keep = pltpu.make_async_copy(back_s.at[0, core], out.at[z, :, kept], b_s.at[2])
    keep.start()

    lend.wait_send()
    swap.wait_send()
    left(rows.at[core, 0, pl.ds(0, chips - 1)], z_s)
    for k in range(chips):
        here = rows.at[core, k, pl.ds(0, dp - 1)]
        if k == far:
            pl.when(z != far)(functools.partial(left, here, d_s.at[k]))
            pl.when(z == 0)(functools.partial(left, here, f_s))
        else:
            left(here, d_s.at[k])
        left(rows.at[core, k], c_s.at[k])
        left(part_r.at[k], p_s.at[k])
    keep.wait()
    give.wait_send()
    left(out.at[pl.ds(0, chips - 1)], b_s.at[0])
    landed(out.at[z, :, given], b_r.at[1])
    landed(out.at[pl.ds(0, chips - 1)], b_r.at[0])


def relayed(tokens, expert_ids, gate_weights, placement, w_gate, w_up, w_down, experts, dp, first, slots):
    own, width = tokens.shape
    topk = expert_ids.shape[1]
    units = w_gate.shape[1]
    chips = experts // 2
    bands = 4
    pad = 128
    half = width // 2
    many = experts * dp * own
    whole = ((0, bands),)
    halves = ((0, bands // 2), (bands // 2, bands))
    single = tuple((b, b + 1) for b in range(bands))
    cuts = tuple(single if k == chips - 1 else halves if k == chips - 2 else whole for k in range(chips))
    parts_of = sum(len(c) for c in cuts)
    hbm = pl.BlockSpec(memory_space=pl.ANY)
    dma = pltpu.SemaphoreType.DMA
    parts = pl.pallas_call(
        functools.partial(relay_kernel, experts, dp, topk, first, slots, pad, bands, cuts),
        out_shape=pltpu.VMEM((chips, own, width), BF16),
        in_specs=[hbm] * 7,
        out_specs=pl.BlockSpec(memory_space=pltpu.VMEM),
        scratch_shapes=[
            pltpu.VMEM((topk, own), jnp.int32),
            pltpu.VMEM((topk, own), BF16),
            pltpu.VMEM(placement.shape, jnp.int32),
            pltpu.VMEM((2, chips, dp, own, pad + width), BF16),
            pltpu.VMEM((many, pad + width), F32),
            pltpu.VMEM((2 * units, width), BF16),
            pltpu.VMEM((2, units, half), BF16),
            pltpu.VMEM((many, 2 * units), F32),
            pltpu.VMEM((2, many, units), BF16),
            pltpu.VMEM((chips * dp, 2 * own, half), BF16),
            pltpu.VMEM((chips, dp - 1, 2 * own, half), BF16),
            pltpu.VMEM((chips, 2, own, half), BF16),
            pltpu.SemaphoreType.REGULAR((chips - 1, 2)), pltpu.SemaphoreType.REGULAR((dp - 1,)),
            dma((7,)),
            dma((2,)),
            dma, dma((chips - 1, 2)),
            dma((chips,)), dma((parts_of,)),
            dma,
            dma((chips,)), dma((parts_of,)),
            dma((2,)),
            dma((chips,)), dma((chips,)),
            dma((3,)), dma((2,)),
        ],
        compiler_params=pltpu.CompilerParams(
            collective_id=1, has_side_effects=True, vmem_limit_bytes=56 << 20
        ),
    )(tokens, expert_ids.T, gate_weights.T, placement, w_gate[0], w_up[0], w_down[0])
    return jnp.sum(parts.astype(F32), axis=0).astype(BF16)


def body(tokens, expert_ids, gate_weights, placement, w_gate, w_up, w_down):
    experts = lax.axis_size("expert")
    dp = lax.axis_size("dp")
    own, width = tokens.shape
    topk = expert_ids.shape[1]
    group = own * dp
    first = max(2, group * topk // experts)
    slots = first + max(1, first // 2)
    if dp == 4 and experts == 8 and own == 4 and width % 1024 == 0:
        return relayed(tokens, expert_ids, gate_weights, placement, w_gate, w_up, w_down, experts, dp, first, slots)
    padded = -(-slots // 8) * 8
    lanes = -(-group * topk // 128) * 128
    block = width // dp
    units = w_gate.shape[1]
    total = experts * padded
    hbm = pl.BlockSpec(memory_space=pl.ANY)
    dma = pltpu.SemaphoreType.DMA
    return pl.pallas_call(
        functools.partial(kernel, experts, dp, topk, first, slots, padded),
        out_shape=jax.ShapeDtypeStruct((own, width), BF16),
        in_specs=[hbm] * 7,
        out_specs=hbm,
        scratch_shapes=[
            pltpu.VMEM((own, width), BF16),
            pltpu.VMEM((topk, own), jnp.int32),
            pltpu.VMEM((topk, own), BF16),
            pltpu.VMEM(placement.shape, jnp.int32),
            pltpu.VMEM((units, width), BF16),
            pltpu.VMEM((units, width), BF16),
            pltpu.VMEM((units, width), BF16),
            pltpu.VMEM((dp, own, block), BF16),
            pltpu.VMEM((dp, own, block), BF16),
            pltpu.VMEM((8, lanes), F32),
            pltpu.VMEM((dp, 8, lanes), F32),
            pltpu.VMEM((group, block), F32),
            pltpu.VMEM((experts, slots, block), BF16),
            pltpu.VMEM((dp, experts, slots, block), BF16),
            pltpu.VMEM((total, block), F32),
            pltpu.VMEM((total, block), F32),
            pltpu.VMEM((dp, experts, slots, block), BF16),
            pltpu.VMEM((dp, experts, slots, block), BF16),
            pltpu.VMEM((experts, slots, block), BF16),
            pltpu.VMEM((experts, slots, block), BF16),
            pltpu.VMEM((total, group), F32),
            pltpu.VMEM((dp, own, block), BF16),
            dma((7,)),
            dma((dp,)), dma((dp,)), dma((dp,)), dma((dp,)),
            dma((experts,)), dma((experts,)),
            dma((dp, experts)), dma((dp, experts)),
            dma((dp, experts)), dma((dp, experts)),
            dma((experts,)), dma((experts,)),
            dma((dp,)), dma((dp,)),
        ],
        compiler_params=pltpu.CompilerParams(
            collective_id=0, has_side_effects=True, vmem_limit_bytes=56 << 20
        ),
    )(tokens, expert_ids.T, gate_weights.T, placement, w_gate[0], w_up[0], w_down[0])


def solution(mesh):
    placed = (
        P(("groups", "expert", "dp"), None),
        P(("groups", "expert", "dp"), None),
        P(("groups", "expert", "dp"), None),
        P("groups", None),
        P("expert", "dp", None),
        P("expert", "dp", None),
        P("expert", "dp", None),
    )
    return jax.shard_map(
        body,
        mesh=mesh,
        in_specs=placed,
        out_specs=P(("groups", "expert", "dp"), None),
        check_vma=False,
    )
```

```python
import functools

import jax
import jax.numpy as jnp
from jax import lax
from jax.experimental import pallas as pl
from jax.experimental.pallas import tpu as pltpu
from jax.sharding import PartitionSpec as P

MESH = pl.DeviceIdType.MESH
F32 = jnp.float32
BF16 = jnp.bfloat16


def each(count, step):
    if count <= 8:
        for i in range(count):
            step(i)
    else:
        def turn(i, carry):
            step(i)
            return carry

        lax.fori_loop(0, count, turn, 0)


def each_from(first, count, step):
    each(count - first, lambda i: step(i + first))


def kernel(experts, dp, topk, first, slots, padded,
           tok_hbm, ids_hbm, gates_hbm, placement_hbm, wg_hbm, wu_hbm, wd_hbm, out,
           tok, ids, gates, placement,
           wg, wu, wd, tok_s, tok_r, info_s, info_r, group_x, disp_s, rows_r, rows_f, part_f,
           part_s, part_r, back_s, back_r, wsel, mix_s,
           w_sem, s1, r1, si, ri, s2, r2, s3, r3, s4, r4, s5, r5, s6, r6):
    me_e = lax.axis_index("expert")
    me_j = lax.axis_index("dp")
    own, width = tok.shape
    block = width // dp
    group = own * dp
    pairs = group * topk
    lanes = info_s.shape[1]
    total = experts * padded

    if dp == 4:
        low, high = lax.rem(me_j, 2), me_j // 2
        across = (me_j, high * 2 + (1 - low), (1 - high) * 2 + low, (1 - high) * 2 + (1 - low))
        onward = backward = lambda s: across[s]
    else:
        onward = lambda s: lax.rem(me_j + s, dp)
        backward = lambda s: lax.rem(me_j + dp - s, dp)

    def to_dp(src, dst, send, recv, s):
        return pltpu.make_async_remote_copy(
            src_ref=src, dst_ref=dst, send_sem=send, recv_sem=recv,
            device_id={"dp": onward(s)}, device_id_type=MESH)

    def to_expert(src, dst, send, recv, shift):
        return pltpu.make_async_remote_copy(
            src_ref=src, dst_ref=dst, send_sem=send, recv_sem=recv,
            device_id={"expert": lax.rem(me_e + shift, experts)}, device_id_type=MESH)

    def cols(j):
        return pl.ds(pl.multiple_of(j * block, 128), block)

    barrier = pltpu.get_barrier_semaphore()
    for s in range(1, dp):
        pl.semaphore_signal(barrier, inc=1, device_id={"dp": onward(s)}, device_id_type=MESH)

    def greet(d):
        pl.semaphore_signal(barrier, inc=1, device_id={"expert": lax.rem(me_e + d, experts)}, device_id_type=MESH)

    each_from(1, experts, greet)

    pairs_of = ((ids_hbm, ids), (gates_hbm, gates), (placement_hbm, placement), (tok_hbm, tok),
                (wg_hbm, wg), (wu_hbm, wu), (wd_hbm, wd))
    loads = [pltpu.make_async_copy(a, b, w_sem.at[i]) for i, (a, b) in enumerate(pairs_of)]
    for load in loads:
        load.start()
    for load in loads[:4]:
        load.wait()
    loads = loads[4:]

    lane = lax.broadcasted_iota(jnp.int32, (8, lanes), 1)
    line = lax.broadcasted_iota(jnp.int32, (8, lanes), 0)
    id_f = ids[...].astype(F32)
    gate_f = gates[...].astype(F32)
    info = jnp.zeros((8, lanes), F32)
    for t in range(own):
        for k in range(topk):
            here = lane == (me_j * own + t) * topk + k
            value = jnp.where(line == 0, jnp.broadcast_to(id_f[k:k + 1, t:t + 1], (8, lanes)),
                              jnp.broadcast_to(gate_f[k:k + 1, t:t + 1], (8, lanes)))
            info = jnp.where(here, value, info)
    info_s[...] = info
    for s in range(1, dp):
        tok_s[s] = tok[:, cols(onward(s))]
    tok_r[me_j] = tok[:, cols(me_j)]

    pl.semaphore_wait(barrier, dp - 1 + experts - 1)

    for s in range(1, dp):
        to_dp(info_s, info_r.at[s], si.at[s], ri.at[s], s).start()
    for s in range(1, dp):
        to_dp(tok_s.at[s], tok_r.at[me_j], s1.at[s], r1.at[s], s).start()
    for s in range(1, dp):
        to_dp(info_s, info_r.at[s], si.at[s], ri.at[s], s).wait_recv()
        info = info + info_r[s]

    id_row = info[0:1, :]
    gate_row = info[1:2, :]
    at_row = lax.broadcasted_iota(jnp.int32, (pairs, lanes), 0)
    at_lane = lax.broadcasted_iota(jnp.int32, (pairs, lanes), 1)
    id_col = jnp.sum(jnp.where(at_row == at_lane, jnp.broadcast_to(id_row, (pairs, lanes)), 0.0),
                     axis=1, keepdims=True)
    same = jnp.broadcast_to(id_col, (pairs, lanes)) == jnp.broadcast_to(id_row, (pairs, lanes))
    rank = jnp.sum(jnp.where(same, jnp.where(at_row < at_lane, 1.0, 0.0), 0.0), axis=0, keepdims=True)
    limit = jnp.full((1, lanes), float(first), F32)
    listed = placement[...].astype(F32)
    for h in range(placement.shape[1]):
        limit = jnp.where(id_row == jnp.broadcast_to(listed[0:1, h:h + 1], (1, lanes)), float(slots), limit)
    dest = jnp.where(rank < limit, id_row * float(padded) + rank, -1.0)
    dest = jnp.where(lax.broadcasted_iota(jnp.int32, (1, lanes), 1) < pairs, dest, -1.0)
    pick = lax.broadcasted_iota(jnp.int32, (total, lanes), 0).astype(F32) == jnp.broadcast_to(dest, (total, lanes))
    pair_i = lax.broadcasted_iota(jnp.int32, (lanes, group), 0)
    token_i = lax.broadcasted_iota(jnp.int32, (lanes, group), 1) * topk
    fold = jnp.where(pair_i >= token_i, jnp.where(pair_i < token_i + topk, 1.0, 0.0), 0.0).astype(BF16)
    select = jnp.dot(jnp.where(pick, 1.0, 0.0).astype(BF16), fold, preferred_element_type=F32).astype(BF16)

    for s in range(1, dp):
        to_dp(tok_s.at[s], tok_r.at[backward(s)], s1.at[s], r1.at[s], s).wait_recv()
    for j in range(dp):
        group_x[j * own:(j + 1) * own, :] = tok_r[j].astype(F32)
    rows_f[...] = jnp.dot(select, group_x[...].astype(BF16), preferred_element_type=F32)

    def dispatch(d):
        e = lax.rem(me_e + d, experts)
        start = pl.multiple_of(e * padded, 8)
        disp_s[e] = rows_f[pl.ds(start, slots), :].astype(BF16)
        to_expert(disp_s.at[e], rows_r.at[me_j, me_e], s2.at[d], r2.at[d], d).start()

    each_from(1, experts, dispatch)
    rows_r[me_j, me_e] = rows_f[pl.ds(pl.multiple_of(me_e * padded, 8), slots), :].astype(BF16)

    relayed = dp == 4 and experts <= 8
    direct = (1, 2) if relayed else range(1, dp)

    def forward(d):
        g = lax.rem(me_e + experts - d, experts)
        for s in direct:
            to_dp(rows_r.at[me_j, g], rows_r.at[me_j, g], s3.at[s, d], r3.at[s, d], s).start()

    forward(0)
    wsel[...] = jnp.dot(jnp.where(pick, jnp.broadcast_to(gate_row, (total, lanes)), 0.0).astype(BF16), fold,
                        preferred_element_type=F32)


    def arrive(d):
        g = lax.rem(me_e + experts - d, experts)
        to_expert(disp_s.at[g], rows_r.at[me_j, g], s2.at[d], r2.at[d], d).wait_recv()
        forward(d)

    each_from(1, experts, arrive)

    loads[0].wait()
    loads[1].wait()
    contract = (((1,), (1,)), ((), ()))

    def first_of(d):
        return 1 + d % 2

    def relay(d):
        g = lax.rem(me_e + experts - d, experts)
        side = first_of(d)
        j = onward(side)
        to_dp(rows_r.at[j, g], rows_r.at[j, g], s3.at[side, d], r3.at[side, d], side).wait_recv()
        to_dp(rows_r.at[j, g], rows_r.at[j, g], s3.at[3, d], r3.at[3, d], 3 - side).start()

    gate = up = None
    for s in range(dp):
        j = backward(s)

        def take(d):
            g = lax.rem(me_e + experts - d, experts)
            if s > 0 and not (relayed and s == first_of(d)):
                to_dp(rows_r.at[j, g], rows_r.at[j, g], s3.at[s, d], r3.at[s, d], s).wait_recv()
            rows_f[pl.ds(pl.multiple_of(g * padded, 8), slots), :] = rows_r[j, g].astype(F32)

        each(experts, take)
        x = rows_f[...].astype(BF16)
        gate_part = lax.dot_general(x, wg[:, cols(j)], contract, preferred_element_type=F32)
        up_part = lax.dot_general(x, wu[:, cols(j)], contract, preferred_element_type=F32)
        gate = gate_part if gate is None else gate + gate_part
        up = up_part if up is None else up + up_part
        if relayed and s == 0:
            each(experts, relay)
    hidden = (gate / (1.0 + jnp.exp(-gate)) * up).astype(BF16)

    loads[2].wait()
    for s in reversed(range(dp)):
        j = onward(s)
        part_f[...] = jnp.dot(hidden, wd[:, cols(j)], preferred_element_type=F32)
        target = part_s if s > 0 else part_r

        def split(d):
            g = lax.rem(me_e + d, experts)
            start = pl.multiple_of(g * padded, 8)
            target[s, g] = part_f[pl.ds(start, slots), :].astype(BF16)
            if s > 0:
                to_dp(part_s.at[s, g], part_r.at[s, g], s4.at[s, d], r4.at[s, d], s).start()

        each_from(1, experts, split)
        split(0)

    def summed(d):
        g = lax.rem(me_e + d, experts)
        for s in range(1, dp):
            to_dp(part_s.at[s, g], part_r.at[s, g], s4.at[s, d], r4.at[s, d], s).wait_recv()
        value = part_r[0, g].astype(F32)
        for s in range(1, dp):
            value = value + part_r[s, g].astype(F32)
        return value.astype(BF16)

    def give(d):
        g = lax.rem(me_e + d, experts)
        back_s[g] = summed(d)
        to_expert(back_s.at[g], back_r.at[me_e], s5.at[d], r5.at[d], d).start()

    each_from(1, experts, give)
    back_r[me_e] = summed(0)

    def collect(d):
        e = lax.rem(me_e + experts - d, experts)
        to_expert(back_s.at[e], back_r.at[e], s5.at[d], r5.at[d], d).wait_recv()

    each_from(1, experts, collect)

    def place(e):
        rows_f[pl.ds(e * padded, slots), :] = back_r[e].astype(F32)

    each(experts, place)
    group_x[...] = lax.dot_general(wsel[...].astype(BF16), rows_f[...].astype(BF16), (((0,), (0,)), ((), ())),
                                   preferred_element_type=F32)
    for j in range(dp):
        mix_s[j] = group_x[j * own:(j + 1) * own, :].astype(BF16)
    for s in reversed(range(1, dp)):
        to_dp(mix_s.at[onward(s)], out.at[:, cols(me_j)], s6.at[s], r6.at[s], s).start()
    kept = pltpu.make_async_copy(mix_s.at[me_j], out.at[:, cols(me_j)], s6.at[0])
    kept.start()
    kept.wait()
    for s in range(1, dp):
        j = backward(s)
        to_dp(mix_s.at[j], out.at[:, cols(j)], s6.at[s], r6.at[s], s).wait_recv()

    for s in range(1, dp):
        to_dp(info_s, info_r.at[s], si.at[s], ri.at[s], s).wait_send()
        to_dp(tok_s.at[s], tok_r.at[me_j], s1.at[s], r1.at[s], s).wait_send()
        to_dp(mix_s.at[onward(s)], out.at[:, cols(me_j)], s6.at[s], r6.at[s], s).wait_send()

    def left(d):
        g = lax.rem(me_e + experts - d, experts)
        for s in range(1, dp):
            to_dp(rows_r.at[me_j, g], rows_r.at[me_j, g], s3.at[s, d], r3.at[s, d], s).wait_send()
            to_dp(part_s.at[s, g], part_r.at[s, g], s4.at[s, d], r4.at[s, d], s).wait_send()

    def left_expert(d):
        e = lax.rem(me_e + d, experts)
        to_expert(disp_s.at[e], rows_r.at[me_j, me_e], s2.at[d], r2.at[d], d).wait_send()
        to_expert(back_s.at[e], back_r.at[me_e], s5.at[d], r5.at[d], d).wait_send()

    each(experts, left)
    each_from(1, experts, left_expert)


def relay_kernel(experts, dp, topk, first, slots, pad, bands, cuts,
                 tok_hbm, ids_hbm, gates_hbm, placement_hbm, wg_hbm, wu_hbm, wd_hbm, out,
                 ids, gates, placement, rows, flat, wgu, wd, acc, hid, partial, part_s, part_r, back_s,
                 ready_e, ready_d, l_sem, w_sem, z_s, z_r, d_s, d_r, f_s, c_s, c_r, h_sem, p_s, p_r, b_s, b_r):
    me_e = lax.axis_index("expert")
    me_j = lax.axis_index("dp")
    core = lax.rem(me_e, 2)
    z = lax.div(me_e, 2)
    chips = experts // 2
    far = chips - 1
    own = rows.shape[3]
    width = tok_hbm.shape[1]
    units = wg_hbm.shape[0]
    half = width // 2
    both = 2 * own
    span = dp * both
    many = chips * span
    band = width // bands

    def turn(at, q):
        return q + lax.div(at, chips // 2) * (far - 2 * q)

    def chip_at(k):
        q = k - 1 + lax.div(k - 1 + chips - turn(z, z), chips)
        return turn(z, q)

    def seen_from(other):
        q = turn(other, z)
        return q + 1 - lax.div(q + chips - turn(other, other), chips)

    def sent_to(n):
        before = lax.div(z - n - 1 + chips, chips)
        return before * (z - 1 - n) + (1 - before) * (n + 1)

    low, high = lax.rem(me_j, 2), lax.div(me_j, 2)
    across = (me_j, high * 2 + (1 - low), (1 - high) * 2 + low, (1 - high) * 2 + (1 - low))
    sibling = z * 2 + (1 - core)

    def to_dp(src, dst, send, recv, s):
        return pltpu.make_async_remote_copy(src_ref=src, dst_ref=dst, send_sem=send, recv_sem=recv,
                                            device_id={"dp": across[s]}, device_id_type=MESH)

    def to_expert(src, dst, send, recv, e):
        return pltpu.make_async_remote_copy(src_ref=src, dst_ref=dst, send_sem=send, recv_sem=recv,
                                            device_id={"expert": e}, device_id_type=MESH)

    def landed(ref, sem):
        to_expert(ref, ref, sem, sem, sibling).wait_recv()

    def left(ref, sem):
        to_expert(ref, ref, sem, sem, sibling).wait_send()

    mid = bands // 2
    split = mid * band

    def edge(b):
        return b * band + (pad if b > mid else 0)

    def cols(b0, b1):
        return pl.ds(edge(b0), edge(b1) - edge(b0))

    z_cuts = ((0, bands // 2), (bands // 2, bands))
    at_cut = {}
    for k in range(chips):
        for i in range(len(cuts[k])):
            at_cut[k, i] = len(at_cut)

    barrier = pltpu.get_barrier_semaphore()

    def tell(sem, axis, to):
        pl.semaphore_signal(sem, inc=1, device_id={axis: to}, device_id_type=MESH)

    tell(barrier, "expert", sibling)
    for s in range(1, dp):
        pl.when(across[s] > me_j)(functools.partial(tell, barrier, "dp", across[s]))
    for q in range(1, chips):
        for o in range(2):
            pl.when(q > z)(functools.partial(tell, barrier, "expert", q * 2 + o))

    def meet_dp(s):
        @pl.when(across[s] > me_j)
        def _():
            pl.semaphore_wait(ready_d.at[s - 1], 1)

    def meet_chip(q, o):
        @pl.when(q > z)
        def _():
            pl.semaphore_wait(ready_e.at[q - 1, o], 1)

    mine = rows.at[core, 0, me_j]
    kept = pl.ds(pl.multiple_of(core * half, 128), half)
    given = pl.ds(pl.multiple_of((1 - core) * half, 128), half)
    loads = [pltpu.make_async_copy(a, b, l_sem.at[i]) for i, (a, b) in enumerate((
        (ids_hbm, ids), (gates_hbm, gates), (placement_hbm, placement),
        (tok_hbm.at[:, pl.ds(0, split)], mine.at[:, pl.ds(0, split)]),
        (tok_hbm.at[:, pl.ds(split, width - split)], mine.at[:, pl.ds(split + pad, width - split)]),
        (wg_hbm, wgu.at[pl.ds(0, units)]), (wu_hbm, wgu.at[pl.ds(units, units)]),
        (wd_hbm.at[:, kept], wd.at[core])))]
    for load in loads:
        load.start()
    pl.semaphore_wait(barrier, 1 + 2 * z + me_j)
    for q in range(chips - 1):
        for o in range(2):
            pl.when(q < z)(functools.partial(tell, ready_e.at[z - 1, core], "expert", q * 2 + o))
    for s in range(1, dp):
        pl.when(across[s] < me_j)(functools.partial(tell, ready_d.at[s - 1], "dp", across[s]))

    def far_send(n, src, c, part):
        other = sent_to(n)
        k = seen_from(other)
        to_expert(src, rows.at[core, k, me_j, :, c], z_s, z_r.at[k - 1, part], other * 2 + core).start()

    def send_tokens(n):
        far_send(n, tok_hbm.at[:, pl.ds(0, split)], pl.ds(0, split), 0)
        far_send(n, tok_hbm.at[:, pl.ds(split, width - split)], pl.ds(split + pad, width - split), 1)

    told_at = pl.ds(split, pad)

    def send_all(n):
        for part, c in enumerate((pl.ds(0, split), pl.ds(split, width + pad - split))):
            far_send(n, mine.at[:, c], c, part)

    def send_told(n):
        far_send(n, mine.at[:, told_at], told_at, 1)

    for n in range(chips - 1):
        pl.when(n < z)(functools.partial(send_tokens, n))

    for load in loads[:3]:
        load.wait()
    lane = lax.broadcasted_iota(jnp.int32, (own, pad), 1)
    line = lax.broadcasted_iota(jnp.int32, (own, pad), 0)
    id_f = ids[...].astype(F32)
    gate_f = gates[...].astype(F32)
    info = jnp.zeros((own, pad), F32)
    for t in range(own):
        for k in range(topk):
            for at, table in ((k, id_f), (topk + k, gate_f)):
                here = jnp.where(line == t, lane, -1) == at
                info = jnp.where(here, jnp.broadcast_to(table[k:k + 1, t:t + 1], (own, pad)), info)
    rows[core, 0, me_j, :, told_at] = info.astype(BF16)
    for n in range(chips - 1):
        pl.when(n < z)(functools.partial(send_told, n))
    loads[3].wait()
    loads[4].wait()

    def over_dp(k, i, s, at):
        here = rows.at[core, k, at, :, cols(*cuts[k][i])]
        return to_dp(here, here, d_s.at[k], d_r.at[at_cut[k, i]], s)

    for s in range(1, dp):
        meet_dp(s)
        over_dp(0, 0, s, me_j).start()
    for n in range(chips - 1):
        @pl.when(n >= z)
        def _():
            meet_chip(sent_to(n), core)
            send_all(n)
    lend = to_expert(wd_hbm.at[:, given], wd.at[core], w_sem.at[0], w_sem.at[1], sibling)
    lend.start()

    def pass_on(k):
        for i, (b0, b1) in enumerate(cuts[k]):
            for n, (a0, a1) in enumerate(z_cuts):
                if b0 <= a0 < b1:
                    landed(rows.at[core, k, me_j, :, cols(a0, a1)], z_r.at[k - 1, n])

            def onward():
                for s in range(1, dp):
                    over_dp(k, i, s, me_j).start()

            if k == far:
                pl.when(z != far)(onward)
            else:
                onward()

    def share(k, i):
        c = cols(*cuts[k][i])
        landed(rows.at[core, k, pl.ds(0, dp - 1), :, c], d_r.at[at_cut[k, i]])
        here = rows.at[core, k, :, :, c]
        to_expert(here, here, c_s.at[k], c_r.at[at_cut[k, i]], sibling).start()

    def spread(k, i):
        c = cols(*cuts[k][i])
        landed(rows.at[1 - core, k, :, :, c], c_r.at[at_cut[k, i]])
        for o in range(2):
            for j in range(dp):
                start = k * span + j * both + o * own
                flat[start:start + own, c] = rows[o, k, j, :, c].astype(F32)

    pass_on(1)
    share(0, 0)

    @pl.when(z == 0)
    def _():
        for i in range(len(cuts[far])):
            c = cols(*cuts[far][i])
            for s in range(1, dp):
                to_expert(rows.at[core, 0, across[s], :, c], rows.at[core, far, across[s], :, c], f_s,
                          d_r.at[at_cut[far, i]], far * 2 + core).start()

    for k in range(2, chips):
        pass_on(k)
    spread(0, 0)
    for k in range(1, chips):
        for i in range(len(cuts[k])):
            share(k, i)
        if k > 1:
            for i in range(len(cuts[k - 1])):
                spread(k - 1, i)

    contract = (((1,), (1,)), ((), ()))
    loads[5].wait()
    loads[6].wait()
    me_f = me_e.astype(F32)
    weight = None
    for b in range(bands):
        for i, (b0, b1) in enumerate(cuts[far]):
            if b0 == b:
                spread(far, i)
        x = flat[:, pl.ds(b * band + (pad if b >= mid else 0), band)].astype(BF16)
        total = lax.dot_general(x, wgu[:, pl.ds(b * band, band)], contract, preferred_element_type=F32)
        if b == mid:
            r = lax.broadcasted_iota(jnp.int32, (many, many), 0)
            q = lax.broadcasted_iota(jnp.int32, (many, many), 1)
            of_r = jnp.where(lax.div(r, span) == lax.div(q, span), lax.rem(lax.div(r, own), 2), 2)
            same = of_r == lax.rem(lax.div(q, own), 2)
            below = jnp.where(same, jnp.where(q < r, 1.0, 0.0), 0.0).astype(BF16)
            listed = placement[0:1, :].astype(F32)
            extra = jnp.sum(jnp.where(listed == me_f, float(slots - first), 0.0), axis=1, keepdims=True)
            told = flat[:, told_at]
            named = jnp.zeros((many, 1), F32)
            value = jnp.zeros((many, 1), F32)
            for k in range(topk):
                hit = told[:, k:k + 1] == me_f
                named = named + jnp.where(hit, 1.0, 0.0)
                value = value + jnp.where(hit, told[:, topk + k:topk + k + 1], 0.0)
            rank = jnp.dot(below, jnp.broadcast_to(named, (many, 128)).astype(BF16), preferred_element_type=F32)[:, 0:1]
            weight = jnp.where(rank < float(first) + extra, value, 0.0)
        if b == 0:
            acc[...] = total
        elif b < bands - 1:
            acc[...] += total
        else:
            total = acc[...] + total
            gate, up = total[:, :units], total[:, units:]
            hid[core] = (gate / (1.0 + jnp.exp(-gate)) * up * weight).astype(BF16)

    swap = to_expert(hid.at[core], hid.at[core], h_sem.at[0], h_sem.at[1], sibling)
    swap.start()
    loads[7].wait()
    piece = half // bands
    for b in range(bands):
        c = pl.ds(b * piece, piece)
        partial[:, c] = jnp.dot(hid[core], wd[core, :, c], preferred_element_type=F32)
    landed(wd.at[1 - core], w_sem.at[1])
    landed(hid.at[1 - core], h_sem.at[1])

    def send_part(k, c):
        for s in reversed(range(1, dp)):
            to_dp(part_s.at[k * dp + across[s], :, c], part_r.at[k, s - 1, :, c], p_s.at[k], p_r.at[k], s).start()

    for b in range(bands):
        c = pl.ds(b * piece, piece)
        total = partial[:, c] + jnp.dot(hid[1 - core], wd[1 - core, :, c], preferred_element_type=F32)
        part_s[:, :, c] = total.reshape(chips * dp, both, piece).astype(BF16)
        send_part(3, c)
    send_part(2, pl.ds(0, half))
    send_part(1, pl.ds(0, half))
    send_part(0, pl.ds(0, half))
    for k in range(1, chips):
        meet_chip(chip_at(k), 1 - core)

    for k in reversed(range(chips)):
        value = part_s[k * dp + me_j].astype(F32)
        landed(part_r.at[k], p_r.at[k])
        for s in range(dp - 1):
            value = value + part_r[k, s].astype(F32)
        for o in range(2):
            back_s[k, o] = value[o * own:(o + 1) * own, :].astype(BF16)
        if k > 0:
            for o in range(2):
                to_expert(back_s.at[k, o], out.at[z, :, kept], b_s.at[0], b_r.at[0], chip_at(k) * 2 + o).start()
    give = to_expert(back_s.at[0, 1 - core], out.at[z, :, kept], b_s.at[1], b_r.at[1], sibling)
    give.start()
    keep = pltpu.make_async_copy(back_s.at[0, core], out.at[z, :, kept], b_s.at[2])
    keep.start()

    lend.wait_send()
    swap.wait_send()
    left(rows.at[core, 0, pl.ds(0, chips - 1)], z_s)
    for k in range(chips):
        here = rows.at[core, k, pl.ds(0, dp - 1)]
        if k == far:
            pl.when(z != far)(functools.partial(left, here, d_s.at[k]))
            pl.when(z == 0)(functools.partial(left, here, f_s))
        else:
            left(here, d_s.at[k])
        left(rows.at[core, k], c_s.at[k])
        if k not in ():
            left(part_r.at[k], p_s.at[k])
    keep.wait()
    give.wait_send()
    left(out.at[pl.ds(0, chips - 1)], b_s.at[0])
    landed(out.at[z, :, given], b_r.at[1])
    landed(out.at[pl.ds(0, chips - 1)], b_r.at[0])


def relayed(tokens, expert_ids, gate_weights, placement, w_gate, w_up, w_down, experts, dp, first, slots):
    own, width = tokens.shape
    topk = expert_ids.shape[1]
    units = w_gate.shape[1]
    chips = experts // 2
    bands = 4
    pad = 128
    half = width // 2
    many = experts * dp * own
    whole = ((0, bands),)
    halves = ((0, bands // 2), (bands // 2, bands))
    single = tuple((b, b + 1) for b in range(bands))
    cuts = tuple(single if k == chips - 1 else halves if k == chips - 2 else whole for k in range(chips))
    parts_of = sum(len(c) for c in cuts)
    hbm = pl.BlockSpec(memory_space=pl.ANY)
    dma = pltpu.SemaphoreType.DMA
    parts = pl.pallas_call(
        functools.partial(relay_kernel, experts, dp, topk, first, slots, pad, bands, cuts),
        out_shape=pltpu.VMEM((chips, own, width), BF16),
        in_specs=[hbm] * 7,
        out_specs=pl.BlockSpec(memory_space=pltpu.VMEM),
        scratch_shapes=[
            pltpu.VMEM((topk, own), jnp.int32),
            pltpu.VMEM((topk, own), BF16),
            pltpu.VMEM(placement.shape, jnp.int32),
            pltpu.VMEM((2, chips, dp, own, pad + width), BF16),
            pltpu.VMEM((many, pad + width), F32),
            pltpu.VMEM((2 * units, width), BF16),
            pltpu.VMEM((2, units, half), BF16),
            pltpu.VMEM((many, 2 * units), F32),
            pltpu.VMEM((2, many, units), BF16),
            pltpu.VMEM((many, half), F32),
            pltpu.VMEM((chips * dp, 2 * own, half), BF16),
            pltpu.VMEM((chips, dp - 1, 2 * own, half), BF16),
            pltpu.VMEM((chips, 2, own, half), BF16),
            pltpu.SemaphoreType.REGULAR((chips - 1, 2)), pltpu.SemaphoreType.REGULAR((dp - 1,)),
            dma((8,)),
            dma((2,)),
            dma, dma((chips - 1, 2)),
            dma((chips,)), dma((parts_of,)),
            dma,
            dma((chips,)), dma((parts_of,)),
            dma((2,)),
            dma((chips,)), dma((chips,)),
            dma((3,)), dma((2,)),
        ],
        compiler_params=pltpu.CompilerParams(
            collective_id=1, has_side_effects=True, vmem_limit_bytes=56 << 20
        ),
    )(tokens, expert_ids.T, gate_weights.T, placement, w_gate[0], w_up[0], w_down[0])
    return jnp.sum(parts.astype(F32), axis=0).astype(BF16)


def body(tokens, expert_ids, gate_weights, placement, w_gate, w_up, w_down):
    experts = lax.axis_size("expert")
    dp = lax.axis_size("dp")
    own, width = tokens.shape
    topk = expert_ids.shape[1]
    group = own * dp
    first = max(2, group * topk // experts)
    slots = first + max(1, first // 2)
    if dp == 4 and experts == 8 and own == 4 and width % 1024 == 0:
        return relayed(tokens, expert_ids, gate_weights, placement, w_gate, w_up, w_down, experts, dp, first, slots)
    padded = -(-slots // 8) * 8
    lanes = -(-group * topk // 128) * 128
    block = width // dp
    units = w_gate.shape[1]
    total = experts * padded
    hbm = pl.BlockSpec(memory_space=pl.ANY)
    dma = pltpu.SemaphoreType.DMA
    return pl.pallas_call(
        functools.partial(kernel, experts, dp, topk, first, slots, padded),
        out_shape=jax.ShapeDtypeStruct((own, width), BF16),
        in_specs=[hbm] * 7,
        out_specs=hbm,
        scratch_shapes=[
            pltpu.VMEM((own, width), BF16),
            pltpu.VMEM((topk, own), jnp.int32),
            pltpu.VMEM((topk, own), BF16),
            pltpu.VMEM(placement.shape, jnp.int32),
            pltpu.VMEM((units, width), BF16),
            pltpu.VMEM((units, width), BF16),
            pltpu.VMEM((units, width), BF16),
            pltpu.VMEM((dp, own, block), BF16),
            pltpu.VMEM((dp, own, block), BF16),
            pltpu.VMEM((8, lanes), F32),
            pltpu.VMEM((dp, 8, lanes), F32),
            pltpu.VMEM((group, block), F32),
            pltpu.VMEM((experts, slots, block), BF16),
            pltpu.VMEM((dp, experts, slots, block), BF16),
            pltpu.VMEM((total, block), F32),
            pltpu.VMEM((total, block), F32),
            pltpu.VMEM((dp, experts, slots, block), BF16),
            pltpu.VMEM((dp, experts, slots, block), BF16),
            pltpu.VMEM((experts, slots, block), BF16),
            pltpu.VMEM((experts, slots, block), BF16),
            pltpu.VMEM((total, group), F32),
            pltpu.VMEM((dp, own, block), BF16),
            dma((7,)),
            dma((dp,)), dma((dp,)), dma((dp,)), dma((dp,)),
            dma((experts,)), dma((experts,)),
            dma((dp, experts)), dma((dp, experts)),
            dma((dp, experts)), dma((dp, experts)),
            dma((experts,)), dma((experts,)),
            dma((dp,)), dma((dp,)),
        ],
        compiler_params=pltpu.CompilerParams(
            collective_id=0, has_side_effects=True, vmem_limit_bytes=56 << 20
        ),
    )(tokens, expert_ids.T, gate_weights.T, placement, w_gate[0], w_up[0], w_down[0])


def solution(mesh):
    placed = (
        P(("groups", "expert", "dp"), None),
        P(("groups", "expert", "dp"), None),
        P(("groups", "expert", "dp"), None),
        P("groups", None),
        P("expert", "dp", None),
        P("expert", "dp", None),
        P("expert", "dp", None),
    )
    return jax.shard_map(
        body,
        mesh=mesh,
        in_specs=placed,
        out_specs=P(("groups", "expert", "dp"), None),
        check_vma=False,
    )
```

```python
import functools

import jax
import jax.numpy as jnp
from jax import lax
from jax.experimental import pallas as pl
from jax.experimental.pallas import tpu as pltpu
from jax.sharding import PartitionSpec as P

MESH = pl.DeviceIdType.MESH
F32 = jnp.float32
BF16 = jnp.bfloat16


def each(count, step):
    if count <= 8:
        for i in range(count):
            step(i)
    else:
        def turn(i, carry):
            step(i)
            return carry

        lax.fori_loop(0, count, turn, 0)


def each_from(first, count, step):
    each(count - first, lambda i: step(i + first))


def kernel(experts, dp, topk, first, slots, padded,
           tok_hbm, ids_hbm, gates_hbm, placement_hbm, wg_hbm, wu_hbm, wd_hbm, out,
           tok, ids, gates, placement,
           wg, wu, wd, tok_s, tok_r, info_s, info_r, group_x, disp_s, rows_r, rows_f, part_f,
           part_s, part_r, back_s, back_r, wsel, mix_s,
           w_sem, s1, r1, si, ri, s2, r2, s3, r3, s4, r4, s5, r5, s6, r6):
    me_e = lax.axis_index("expert")
    me_j = lax.axis_index("dp")
    own, width = tok.shape
    block = width // dp
    group = own * dp
    pairs = group * topk
    lanes = info_s.shape[1]
    total = experts * padded

    if dp == 4:
        low, high = lax.rem(me_j, 2), me_j // 2
        across = (me_j, high * 2 + (1 - low), (1 - high) * 2 + low, (1 - high) * 2 + (1 - low))
        onward = backward = lambda s: across[s]
    else:
        onward = lambda s: lax.rem(me_j + s, dp)
        backward = lambda s: lax.rem(me_j + dp - s, dp)

    def to_dp(src, dst, send, recv, s):
        return pltpu.make_async_remote_copy(
            src_ref=src, dst_ref=dst, send_sem=send, recv_sem=recv,
            device_id={"dp": onward(s)}, device_id_type=MESH)

    def to_expert(src, dst, send, recv, shift):
        return pltpu.make_async_remote_copy(
            src_ref=src, dst_ref=dst, send_sem=send, recv_sem=recv,
            device_id={"expert": lax.rem(me_e + shift, experts)}, device_id_type=MESH)

    def cols(j):
        return pl.ds(pl.multiple_of(j * block, 128), block)

    barrier = pltpu.get_barrier_semaphore()
    for s in range(1, dp):
        pl.semaphore_signal(barrier, inc=1, device_id={"dp": onward(s)}, device_id_type=MESH)

    def greet(d):
        pl.semaphore_signal(barrier, inc=1, device_id={"expert": lax.rem(me_e + d, experts)}, device_id_type=MESH)

    each_from(1, experts, greet)

    pairs_of = ((ids_hbm, ids), (gates_hbm, gates), (placement_hbm, placement), (tok_hbm, tok),
                (wg_hbm, wg), (wu_hbm, wu), (wd_hbm, wd))
    loads = [pltpu.make_async_copy(a, b, w_sem.at[i]) for i, (a, b) in enumerate(pairs_of)]
    for load in loads:
        load.start()
    for load in loads[:4]:
        load.wait()
    loads = loads[4:]

    lane = lax.broadcasted_iota(jnp.int32, (8, lanes), 1)
    line = lax.broadcasted_iota(jnp.int32, (8, lanes), 0)
    id_f = ids[...].astype(F32)
    gate_f = gates[...].astype(F32)
    info = jnp.zeros((8, lanes), F32)
    for t in range(own):
        for k in range(topk):
            here = lane == (me_j * own + t) * topk + k
            value = jnp.where(line == 0, jnp.broadcast_to(id_f[k:k + 1, t:t + 1], (8, lanes)),
                              jnp.broadcast_to(gate_f[k:k + 1, t:t + 1], (8, lanes)))
            info = jnp.where(here, value, info)
    info_s[...] = info
    for s in range(1, dp):
        tok_s[s] = tok[:, cols(onward(s))]
    tok_r[me_j] = tok[:, cols(me_j)]

    pl.semaphore_wait(barrier, dp - 1 + experts - 1)

    for s in range(1, dp):
        to_dp(info_s, info_r.at[s], si.at[s], ri.at[s], s).start()
    for s in range(1, dp):
        to_dp(tok_s.at[s], tok_r.at[me_j], s1.at[s], r1.at[s], s).start()
    for s in range(1, dp):
        to_dp(info_s, info_r.at[s], si.at[s], ri.at[s], s).wait_recv()
        info = info + info_r[s]

    id_row = info[0:1, :]
    gate_row = info[1:2, :]
    at_row = lax.broadcasted_iota(jnp.int32, (pairs, lanes), 0)
    at_lane = lax.broadcasted_iota(jnp.int32, (pairs, lanes), 1)
    id_col = jnp.sum(jnp.where(at_row == at_lane, jnp.broadcast_to(id_row, (pairs, lanes)), 0.0),
                     axis=1, keepdims=True)
    same = jnp.broadcast_to(id_col, (pairs, lanes)) == jnp.broadcast_to(id_row, (pairs, lanes))
    rank = jnp.sum(jnp.where(same, jnp.where(at_row < at_lane, 1.0, 0.0), 0.0), axis=0, keepdims=True)
    limit = jnp.full((1, lanes), float(first), F32)
    listed = placement[...].astype(F32)
    for h in range(placement.shape[1]):
        limit = jnp.where(id_row == jnp.broadcast_to(listed[0:1, h:h + 1], (1, lanes)), float(slots), limit)
    dest = jnp.where(rank < limit, id_row * float(padded) + rank, -1.0)
    dest = jnp.where(lax.broadcasted_iota(jnp.int32, (1, lanes), 1) < pairs, dest, -1.0)
    pick = lax.broadcasted_iota(jnp.int32, (total, lanes), 0).astype(F32) == jnp.broadcast_to(dest, (total, lanes))
    pair_i = lax.broadcasted_iota(jnp.int32, (lanes, group), 0)
    token_i = lax.broadcasted_iota(jnp.int32, (lanes, group), 1) * topk
    fold = jnp.where(pair_i >= token_i, jnp.where(pair_i < token_i + topk, 1.0, 0.0), 0.0).astype(BF16)
    select = jnp.dot(jnp.where(pick, 1.0, 0.0).astype(BF16), fold, preferred_element_type=F32).astype(BF16)

    for s in range(1, dp):
        to_dp(tok_s.at[s], tok_r.at[backward(s)], s1.at[s], r1.at[s], s).wait_recv()
    for j in range(dp):
        group_x[j * own:(j + 1) * own, :] = tok_r[j].astype(F32)
    rows_f[...] = jnp.dot(select, group_x[...].astype(BF16), preferred_element_type=F32)

    def dispatch(d):
        e = lax.rem(me_e + d, experts)
        start = pl.multiple_of(e * padded, 8)
        disp_s[e] = rows_f[pl.ds(start, slots), :].astype(BF16)
        to_expert(disp_s.at[e], rows_r.at[me_j, me_e], s2.at[d], r2.at[d], d).start()

    each_from(1, experts, dispatch)
    rows_r[me_j, me_e] = rows_f[pl.ds(pl.multiple_of(me_e * padded, 8), slots), :].astype(BF16)

    relayed = dp == 4 and experts <= 8
    direct = (1, 2) if relayed else range(1, dp)

    def forward(d):
        g = lax.rem(me_e + experts - d, experts)
        for s in direct:
            to_dp(rows_r.at[me_j, g], rows_r.at[me_j, g], s3.at[s, d], r3.at[s, d], s).start()

    forward(0)
    wsel[...] = jnp.dot(jnp.where(pick, jnp.broadcast_to(gate_row, (total, lanes)), 0.0).astype(BF16), fold,
                        preferred_element_type=F32)


    def arrive(d):
        g = lax.rem(me_e + experts - d, experts)
        to_expert(disp_s.at[g], rows_r.at[me_j, g], s2.at[d], r2.at[d], d).wait_recv()
        forward(d)

    each_from(1, experts, arrive)

    loads[0].wait()
    loads[1].wait()
    contract = (((1,), (1,)), ((), ()))

    def first_of(d):
        return 1 + d % 2

    def relay(d):
        g = lax.rem(me_e + experts - d, experts)
        side = first_of(d)
        j = onward(side)
        to_dp(rows_r.at[j, g], rows_r.at[j, g], s3.at[side, d], r3.at[side, d], side).wait_recv()
        to_dp(rows_r.at[j, g], rows_r.at[j, g], s3.at[3, d], r3.at[3, d], 3 - side).start()

    gate = up = None
    for s in range(dp):
        j = backward(s)

        def take(d):
            g = lax.rem(me_e + experts - d, experts)
            if s > 0 and not (relayed and s == first_of(d)):
                to_dp(rows_r.at[j, g], rows_r.at[j, g], s3.at[s, d], r3.at[s, d], s).wait_recv()
            rows_f[pl.ds(pl.multiple_of(g * padded, 8), slots), :] = rows_r[j, g].astype(F32)

        each(experts, take)
        x = rows_f[...].astype(BF16)
        gate_part = lax.dot_general(x, wg[:, cols(j)], contract, preferred_element_type=F32)
        up_part = lax.dot_general(x, wu[:, cols(j)], contract, preferred_element_type=F32)
        gate = gate_part if gate is None else gate + gate_part
        up = up_part if up is None else up + up_part
        if relayed and s == 0:
            each(experts, relay)
    hidden = (gate / (1.0 + jnp.exp(-gate)) * up).astype(BF16)

    loads[2].wait()
    for s in reversed(range(dp)):
        j = onward(s)
        part_f[...] = jnp.dot(hidden, wd[:, cols(j)], preferred_element_type=F32)
        target = part_s if s > 0 else part_r

        def split(d):
            g = lax.rem(me_e + d, experts)
            start = pl.multiple_of(g * padded, 8)
            target[s, g] = part_f[pl.ds(start, slots), :].astype(BF16)
            if s > 0:
                to_dp(part_s.at[s, g], part_r.at[s, g], s4.at[s, d], r4.at[s, d], s).start()

        each_from(1, experts, split)
        split(0)

    def summed(d):
        g = lax.rem(me_e + d, experts)
        for s in range(1, dp):
            to_dp(part_s.at[s, g], part_r.at[s, g], s4.at[s, d], r4.at[s, d], s).wait_recv()
        value = part_r[0, g].astype(F32)
        for s in range(1, dp):
            value = value + part_r[s, g].astype(F32)
        return value.astype(BF16)

    def give(d):
        g = lax.rem(me_e + d, experts)
        back_s[g] = summed(d)
        to_expert(back_s.at[g], back_r.at[me_e], s5.at[d], r5.at[d], d).start()

    each_from(1, experts, give)
    back_r[me_e] = summed(0)

    def collect(d):
        e = lax.rem(me_e + experts - d, experts)
        to_expert(back_s.at[e], back_r.at[e], s5.at[d], r5.at[d], d).wait_recv()

    each_from(1, experts, collect)

    def place(e):
        rows_f[pl.ds(e * padded, slots), :] = back_r[e].astype(F32)

    each(experts, place)
    group_x[...] = lax.dot_general(wsel[...].astype(BF16), rows_f[...].astype(BF16), (((0,), (0,)), ((), ())),
                                   preferred_element_type=F32)
    for j in range(dp):
        mix_s[j] = group_x[j * own:(j + 1) * own, :].astype(BF16)
    for s in reversed(range(1, dp)):
        to_dp(mix_s.at[onward(s)], out.at[:, cols(me_j)], s6.at[s], r6.at[s], s).start()
    kept = pltpu.make_async_copy(mix_s.at[me_j], out.at[:, cols(me_j)], s6.at[0])
    kept.start()
    kept.wait()
    for s in range(1, dp):
        j = backward(s)
        to_dp(mix_s.at[j], out.at[:, cols(j)], s6.at[s], r6.at[s], s).wait_recv()

    for s in range(1, dp):
        to_dp(info_s, info_r.at[s], si.at[s], ri.at[s], s).wait_send()
        to_dp(tok_s.at[s], tok_r.at[me_j], s1.at[s], r1.at[s], s).wait_send()
        to_dp(mix_s.at[onward(s)], out.at[:, cols(me_j)], s6.at[s], r6.at[s], s).wait_send()

    def left(d):
        g = lax.rem(me_e + experts - d, experts)
        for s in range(1, dp):
            to_dp(rows_r.at[me_j, g], rows_r.at[me_j, g], s3.at[s, d], r3.at[s, d], s).wait_send()
            to_dp(part_s.at[s, g], part_r.at[s, g], s4.at[s, d], r4.at[s, d], s).wait_send()

    def left_expert(d):
        e = lax.rem(me_e + d, experts)
        to_expert(disp_s.at[e], rows_r.at[me_j, me_e], s2.at[d], r2.at[d], d).wait_send()
        to_expert(back_s.at[e], back_r.at[me_e], s5.at[d], r5.at[d], d).wait_send()

    each(experts, left)
    each_from(1, experts, left_expert)


def relay_kernel(experts, dp, topk, first, slots, pad, bands, cuts,
                 tok_hbm, ids_hbm, gates_hbm, placement_hbm, wg_hbm, wu_hbm, wd_hbm, out,
                 ids, gates, placement, rows, flat, wgu, wd, acc, hid, partial, part_s, part_r, diag_r, back_s,
                 ready_e, ready_d, l_sem, w_sem, z_s, z_r, d_s, d_r, g_s, g_r, c_s, c_r, h_sem, p_s, p_r, q_s, q_r, b_s, b_r):
    me_e = lax.axis_index("expert")
    me_j = lax.axis_index("dp")
    core = lax.rem(me_e, 2)
    z = lax.div(me_e, 2)
    chips = experts // 2
    far = chips - 1
    own = rows.shape[3]
    width = tok_hbm.shape[1]
    units = wg_hbm.shape[0]
    half = width // 2
    both = 2 * own
    span = dp * both
    many = chips * span
    band = width // bands

    def turn(at, q):
        return q + lax.div(at, chips // 2) * (far - 2 * q)

    def chip_at(k):
        q = k - 1 + lax.div(k - 1 + chips - turn(z, z), chips)
        return turn(z, q)

    def seen_from(other):
        q = turn(other, z)
        return q + 1 - lax.div(q + chips - turn(other, other), chips)

    def sent_to(n):
        before = lax.div(z - n - 1 + chips, chips)
        return before * (z - 1 - n) + (1 - before) * (n + 1)

    low, high = lax.rem(me_j, 2), lax.div(me_j, 2)
    across = (me_j, high * 2 + (1 - low), (1 - high) * 2 + low, (1 - high) * 2 + (1 - low))
    sibling = z * 2 + (1 - core)

    def to_dp(src, dst, send, recv, s):
        return pltpu.make_async_remote_copy(src_ref=src, dst_ref=dst, send_sem=send, recv_sem=recv,
                                            device_id={"dp": across[s]}, device_id_type=MESH)

    def to_expert(src, dst, send, recv, e):
        return pltpu.make_async_remote_copy(src_ref=src, dst_ref=dst, send_sem=send, recv_sem=recv,
                                            device_id={"expert": e}, device_id_type=MESH)

    def landed(ref, sem):
        to_expert(ref, ref, sem, sem, sibling).wait_recv()

    def left(ref, sem):
        to_expert(ref, ref, sem, sem, sibling).wait_send()

    mid = bands // 2
    split = mid * band

    def edge(b):
        return b * band + (pad if b > mid else 0)

    def cols(b0, b1):
        return pl.ds(edge(b0), edge(b1) - edge(b0))

    z_cuts = ((0, bands // 2), (bands // 2, bands))
    at_cut = {}
    for k in range(chips):
        for i in range(len(cuts[k])):
            at_cut[k, i] = len(at_cut)

    barrier = pltpu.get_barrier_semaphore()

    def tell(sem, axis, to):
        pl.semaphore_signal(sem, inc=1, device_id={axis: to}, device_id_type=MESH)

    tell(barrier, "expert", sibling)
    for s in range(1, dp):
        pl.when(across[s] > me_j)(functools.partial(tell, barrier, "dp", across[s]))
    for q in range(1, chips):
        for o in range(2):
            pl.when(q > z)(functools.partial(tell, barrier, "expert", q * 2 + o))

    def meet_dp(s):
        @pl.when(across[s] > me_j)
        def _():
            pl.semaphore_wait(ready_d.at[s - 1], 1)

    def meet_chip(q, o):
        @pl.when(q > z)
        def _():
            pl.semaphore_wait(ready_e.at[q - 1, o], 1)

    mine = rows.at[core, 0, me_j]
    kept = pl.ds(pl.multiple_of(core * half, 128), half)
    given = pl.ds(pl.multiple_of((1 - core) * half, 128), half)
    loads = [pltpu.make_async_copy(a, b, l_sem.at[i]) for i, (a, b) in enumerate((
        (ids_hbm, ids), (gates_hbm, gates), (placement_hbm, placement),
        (tok_hbm.at[:, pl.ds(0, split)], mine.at[:, pl.ds(0, split)]),
        (tok_hbm.at[:, pl.ds(split, width - split)], mine.at[:, pl.ds(split + pad, width - split)]),
        (wg_hbm, wgu.at[pl.ds(0, units)]), (wu_hbm, wgu.at[pl.ds(units, units)]),
        (wd_hbm.at[:, kept], wd.at[core])))]
    for load in loads[:5]:
        load.start()
    pl.semaphore_wait(barrier, 1 + 2 * z + me_j)
    for q in range(chips - 1):
        for o in range(2):
            pl.when(q < z)(functools.partial(tell, ready_e.at[z - 1, core], "expert", q * 2 + o))
    for s in range(1, dp):
        pl.when(across[s] < me_j)(functools.partial(tell, ready_d.at[s - 1], "dp", across[s]))

    def far_send(n, src, c, part):
        other = sent_to(n)
        k = seen_from(other)
        to_expert(src, rows.at[core, k, me_j, :, c], z_s, z_r.at[k - 1, part], other * 2 + core).start()

    def send_tokens(n):
        far_send(n, tok_hbm.at[:, pl.ds(0, split)], pl.ds(0, split), 0)
        far_send(n, tok_hbm.at[:, pl.ds(split, width - split)], pl.ds(split + pad, width - split), 1)

    told_at = pl.ds(split, pad)

    def send_all(n):
        for part, c in enumerate((pl.ds(0, split), pl.ds(split, width + pad - split))):
            far_send(n, mine.at[:, c], c, part)

    def send_told(n):
        far_send(n, mine.at[:, told_at], told_at, 1)

    for n in range(chips - 1):
        pl.when(n < z)(functools.partial(send_tokens, n))
    for load in loads[5:]:
        load.start()

    for load in loads[:3]:
        load.wait()
    lane = lax.broadcasted_iota(jnp.int32, (own, pad), 1)
    line = lax.broadcasted_iota(jnp.int32, (own, pad), 0)
    id_f = ids[...].astype(F32)
    gate_f = gates[...].astype(F32)
    info = jnp.zeros((own, pad), F32)
    for t in range(own):
        for k in range(topk):
            for at, table in ((k, id_f), (topk + k, gate_f)):
                here = jnp.where(line == t, lane, -1) == at
                info = jnp.where(here, jnp.broadcast_to(table[k:k + 1, t:t + 1], (own, pad)), info)
    rows[core, 0, me_j, :, told_at] = info.astype(BF16)
    for n in range(chips - 1):
        pl.when(n < z)(functools.partial(send_told, n))
    loads[3].wait()
    loads[4].wait()

    def over_dp(k, i, s, at):
        here = rows.at[core, k, at, :, cols(*cuts[k][i])]
        return to_dp(here, here, d_s.at[k], d_r.at[at_cut[k, i]], s)

    for s in range(1, dp):
        meet_dp(s)
        over_dp(0, 0, s, me_j).start()
    for n in range(chips - 1):
        @pl.when(n >= z)
        def _():
            meet_chip(sent_to(n), core)
            send_all(n)
    lend = to_expert(wd_hbm.at[:, given], wd.at[core], w_sem.at[0], w_sem.at[1], sibling)
    lend.start()

    def pass_on(k):
        for i, (b0, b1) in enumerate(cuts[k]):
            for n, (a0, a1) in enumerate(z_cuts):
                if b0 <= a0 < b1:
                    landed(rows.at[core, k, me_j, :, cols(a0, a1)], z_r.at[k - 1, n])

            for s in range(1, dp - 1):
                over_dp(k, i, s, me_j).start()

            @pl.when(chip_at(k) > z)
            def _():
                over_dp(k, i, dp - 1, me_j).start()

    def share(k, i):
        c = cols(*cuts[k][i])

        def wait_for(count):
            landed(rows.at[core, k, pl.ds(0, count), :, c], d_r.at[at_cut[k, i]])

        if k == 0:
            wait_for(dp - 1)
        else:
            pl.when(chip_at(k) > z)(functools.partial(wait_for, dp - 1))

            @pl.when(chip_at(k) < z)
            def _():
                wait_for(dp - 2)
                if i == 0:
                    landed(rows.at[core, k, 0], g_r.at[k - 1])
        here = rows.at[core, k, :, :, c]
        to_expert(here, here, c_s.at[k], c_r.at[at_cut[k, i]], sibling).start()

    def spread(k, i):
        c = cols(*cuts[k][i])
        landed(rows.at[1 - core, k, :, :, c], c_r.at[at_cut[k, i]])
        for o in range(2):
            for j in range(dp):
                start = k * span + j * both + o * own
                flat[start:start + own, c] = rows[o, k, j, :, c].astype(F32)

    def relay(n):
        k = seen_from(sent_to(n))
        return to_expert(rows.at[core, 0, across[dp - 1]], rows.at[core, k, across[dp - 1]], g_s.at[n], g_r.at[k - 1],
                         sent_to(n) * 2 + core)

    def share_own():
        share(0, 0)
        for n in range(chips - 1):
            @pl.when(n >= z)
            def _():
                relay(n).start()

    pass_on(1)
    pl.when(z == 0)(share_own)
    for k in range(2, chips):
        pass_on(k)
    pl.when(z != 0)(share_own)
    spread(0, 0)
    for k in range(1, chips):
        for i in range(len(cuts[k])):
            share(k, i)
        if k > 1:
            for i in range(len(cuts[k - 1])):
                spread(k - 1, i)

    contract = (((1,), (1,)), ((), ()))
    loads[5].wait()
    loads[6].wait()
    me_f = me_e.astype(F32)
    weight = None
    for b in range(bands):
        for i, (b0, b1) in enumerate(cuts[far]):
            if b0 == b:
                spread(far, i)
        x = flat[:, pl.ds(b * band + (pad if b >= mid else 0), band)].astype(BF16)
        total = lax.dot_general(x, wgu[:, pl.ds(b * band, band)], contract, preferred_element_type=F32)
        if b == mid:
            r = lax.broadcasted_iota(jnp.int32, (many, many), 0)
            q = lax.broadcasted_iota(jnp.int32, (many, many), 1)
            of_r = jnp.where(lax.div(r, span) == lax.div(q, span), lax.rem(lax.div(r, own), 2), 2)
            same = of_r == lax.rem(lax.div(q, own), 2)
            below = jnp.where(same, jnp.where(q < r, 1.0, 0.0), 0.0).astype(BF16)
            listed = placement[0:1, :].astype(F32)
            extra = jnp.sum(jnp.where(listed == me_f, float(slots - first), 0.0), axis=1, keepdims=True)
            told = flat[:, told_at]
            named = jnp.zeros((many, 1), F32)
            value = jnp.zeros((many, 1), F32)
            for k in range(topk):
                hit = told[:, k:k + 1] == me_f
                named = named + jnp.where(hit, 1.0, 0.0)
                value = value + jnp.where(hit, told[:, topk + k:topk + k + 1], 0.0)
            rank = jnp.dot(below, jnp.broadcast_to(named, (many, 128)).astype(BF16), preferred_element_type=F32)[:, 0:1]
            weight = jnp.where(rank < float(first) + extra, value, 0.0)
        if b == 0:
            acc[...] = total
        elif b < bands - 1:
            acc[...] += total
        else:
            total = acc[...] + total
            gate, up = total[:, :units], total[:, units:]
            hid[core] = (gate / (1.0 + jnp.exp(-gate)) * up * weight).astype(BF16)

    swap = to_expert(hid.at[core], hid.at[core], h_sem.at[0], h_sem.at[1], sibling)
    swap.start()
    loads[7].wait()
    piece = half // bands
    for b in range(bands):
        c = pl.ds(b * piece, piece)
        partial[:, c] = jnp.dot(hid[core], wd[core, :, c], preferred_element_type=F32)
    landed(wd.at[1 - core], w_sem.at[1])
    landed(hid.at[1 - core], h_sem.at[1])

    ends = z * (far - z) == 0
    diagonal = dp - 1

    def send_part(k, c):
        for s in range(1, diagonal):
            to_dp(part_s.at[k * dp + across[s], :, c], part_r.at[k, s - 1, :, c], p_s.at[k], p_r.at[k], s).start()

    def send_far_diagonal(c):
        to_dp(part_s.at[far * dp + across[diagonal], :, c], part_r.at[far, diagonal - 1, :, c], p_s.at[chips],
              p_r.at[chips], diagonal).start()

    def send_over_z(k, c):
        other = chip_at(k)
        at = seen_from(other) - 1
        to_expert(part_s.at[k * dp + across[diagonal], :, c], diag_r.at[at, :, c], q_s.at[lax.div(k, far)], q_r.at[at],
                  other * 2 + core).start()

    def rest(b):
        return jnp.dot(hid[1 - core], wd[1 - core, :, b * piece:(b + 1) * piece], preferred_element_type=F32)

    ahead = rest(0)
    for b in range(bands):
        c = pl.ds(b * piece, piece)
        total = partial[:, c] + ahead
        if b < bands - 1:
            ahead = rest(b + 1)
        part_s[:, :, c] = total.reshape(chips * dp, both, piece).astype(BF16)
        send_part(far, c)
        if b % 2 == 1:
            c = pl.ds((b - 1) * piece, 2 * piece)
            pl.when(ends)(functools.partial(send_far_diagonal, c))
            pl.when(jnp.logical_not(ends))(functools.partial(send_over_z, far, c))
            for k in range(1, far):
                send_over_z(k, c)
    for k in reversed(range(far)):
        send_part(k, pl.ds(0, half))
    for k in range(1, chips):
        meet_chip(chip_at(k), 1 - core)

    def pack(to, value):
        for o in range(2):
            to[o] = value[o * own:(o + 1) * own, :].astype(BF16)

    def gather_part(k):
        landed(part_r.at[k, pl.ds(0, diagonal - 1)], p_r.at[k])
        value = part_s[k * dp + me_j].astype(F32)
        for s in range(diagonal - 1):
            value = value + part_r[k, s].astype(F32)
        pack(back_s.at[k], value)
        if k == far:
            @pl.when(ends)
            def _():
                landed(part_r.at[far, diagonal - 1], p_r.at[chips])
                pack(back_s.at[k], value + part_r[far, diagonal - 1].astype(F32))
        if k > 0:
            for o in range(2):
                to_expert(back_s.at[k, o], out.at[z, :, kept], b_s.at[0], b_r.at[0], chip_at(k) * 2 + o).start()

    def gather_diagonal():
        value = part_s[across[diagonal]].astype(F32)
        for k in range(1, far):
            landed(diag_r.at[k - 1], q_r.at[k - 1])
            value = value + diag_r[k - 1].astype(F32)
        pack(back_s.at[chips], value)

        @pl.when(jnp.logical_not(ends))
        def _():
            landed(diag_r.at[far - 1], q_r.at[far - 1])
            pack(back_s.at[chips], value + diag_r[far - 1].astype(F32))

        for o in range(2):
            pltpu.make_async_remote_copy(
                src_ref=back_s.at[chips, o], dst_ref=out.at[chips, :, kept], send_sem=b_s.at[3], recv_sem=b_r.at[2],
                device_id={"expert": z * 2 + o, "dp": across[diagonal]}, device_id_type=MESH).start()

    gather_part(3)
    gather_part(2)
    gather_diagonal()
    gather_part(1)
    gather_part(0)
    give = to_expert(back_s.at[0, 1 - core], out.at[z, :, kept], b_s.at[1], b_r.at[1], sibling)
    give.start()
    keep = pltpu.make_async_copy(back_s.at[0, core], out.at[z, :, kept], b_s.at[2])
    keep.start()

    lend.wait_send()
    swap.wait_send()
    left(rows.at[core, 0, pl.ds(0, chips - 1)], z_s)
    for k in range(chips):
        if k == 0:
            left(rows.at[core, k, pl.ds(0, dp - 1)], d_s.at[k])
        else:
            pl.when(chip_at(k) > z)(functools.partial(left, rows.at[core, k, pl.ds(0, dp - 1)], d_s.at[k]))
            pl.when(chip_at(k) < z)(functools.partial(left, rows.at[core, k, pl.ds(0, dp - 2)], d_s.at[k]))
            pl.when(k > z)(functools.partial(left, rows.at[core, 0, 0], g_s.at[k - 1]))
        left(rows.at[core, k], c_s.at[k])
        if k not in ():
            left(part_r.at[k, pl.ds(0, diagonal - 1)], p_s.at[k])
    keep.wait()
    give.wait_send()
    left(diag_r.at[pl.ds(0, far - 1)], q_s.at[0])
    pl.when(ends)(functools.partial(left, diag_r.at[0], p_s.at[chips]))
    pl.when(jnp.logical_not(ends))(functools.partial(left, diag_r.at[0], q_s.at[1]))
    left(out.at[chips], b_s.at[3])
    landed(out.at[chips], b_r.at[2])
    left(out.at[pl.ds(0, chips - 1)], b_s.at[0])
    landed(out.at[z, :, given], b_r.at[1])
    landed(out.at[pl.ds(0, chips - 1)], b_r.at[0])


def relayed(tokens, expert_ids, gate_weights, placement, w_gate, w_up, w_down, experts, dp, first, slots):
    own, width = tokens.shape
    topk = expert_ids.shape[1]
    units = w_gate.shape[1]
    chips = experts // 2
    bands = 4
    pad = 128
    half = width // 2
    many = experts * dp * own
    whole = ((0, bands),)
    halves = ((0, bands // 2), (bands // 2, bands))
    single = tuple((b, b + 1) for b in range(bands))
    cuts = tuple(single if k == chips - 1 else halves if k == chips - 2 else whole for k in range(chips))
    parts_of = sum(len(c) for c in cuts)
    hbm = pl.BlockSpec(memory_space=pl.ANY)
    dma = pltpu.SemaphoreType.DMA
    parts = pl.pallas_call(
        functools.partial(relay_kernel, experts, dp, topk, first, slots, pad, bands, cuts),
        out_shape=pltpu.VMEM((chips + 1, own, width), BF16),
        in_specs=[hbm] * 7,
        out_specs=pl.BlockSpec(memory_space=pltpu.VMEM),
        scratch_shapes=[
            pltpu.VMEM((topk, own), jnp.int32),
            pltpu.VMEM((topk, own), BF16),
            pltpu.VMEM(placement.shape, jnp.int32),
            pltpu.VMEM((2, chips, dp, own, pad + width), BF16),
            pltpu.VMEM((many, pad + width), F32),
            pltpu.VMEM((2 * units, width), BF16),
            pltpu.VMEM((2, units, half), BF16),
            pltpu.VMEM((many, 2 * units), F32),
            pltpu.VMEM((2, many, units), BF16),
            pltpu.VMEM((many, half), F32),
            pltpu.VMEM((chips * dp, 2 * own, half), BF16),
            pltpu.VMEM((chips, dp - 1, 2 * own, half), BF16),
            pltpu.VMEM((chips - 1, 2 * own, half), BF16),
            pltpu.VMEM((chips + 1, 2, own, half), BF16),
            pltpu.SemaphoreType.REGULAR((chips - 1, 2)), pltpu.SemaphoreType.REGULAR((dp - 1,)),
            dma((8,)),
            dma((2,)),
            dma, dma((chips - 1, 2)),
            dma((chips,)), dma((parts_of,)),
            dma((chips - 1,)), dma((chips - 1,)),
            dma((chips,)), dma((parts_of,)),
            dma((2,)),
            dma((chips + 1,)), dma((chips + 1,)),
            dma((2,)), dma((chips - 1,)),
            dma((4,)), dma((3,)),
        ],
        compiler_params=pltpu.CompilerParams(
            collective_id=1, has_side_effects=True, vmem_limit_bytes=56 << 20
        ),
    )(tokens, expert_ids.T, gate_weights.T, placement, w_gate[0], w_up[0], w_down[0])
    return jnp.sum(parts.astype(F32), axis=0).astype(BF16)


def body(tokens, expert_ids, gate_weights, placement, w_gate, w_up, w_down):
    experts = lax.axis_size("expert")
    dp = lax.axis_size("dp")
    own, width = tokens.shape
    topk = expert_ids.shape[1]
    group = own * dp
    first = max(2, group * topk // experts)
    slots = first + max(1, first // 2)
    if dp == 4 and experts == 8 and own == 4 and width % 1024 == 0:
        return relayed(tokens, expert_ids, gate_weights, placement, w_gate, w_up, w_down, experts, dp, first, slots)
    padded = -(-slots // 8) * 8
    lanes = -(-group * topk // 128) * 128
    block = width // dp
    units = w_gate.shape[1]
    total = experts * padded
    hbm = pl.BlockSpec(memory_space=pl.ANY)
    dma = pltpu.SemaphoreType.DMA
    return pl.pallas_call(
        functools.partial(kernel, experts, dp, topk, first, slots, padded),
        out_shape=jax.ShapeDtypeStruct((own, width), BF16),
        in_specs=[hbm] * 7,
        out_specs=hbm,
        scratch_shapes=[
            pltpu.VMEM((own, width), BF16),
            pltpu.VMEM((topk, own), jnp.int32),
            pltpu.VMEM((topk, own), BF16),
            pltpu.VMEM(placement.shape, jnp.int32),
            pltpu.VMEM((units, width), BF16),
            pltpu.VMEM((units, width), BF16),
            pltpu.VMEM((units, width), BF16),
            pltpu.VMEM((dp, own, block), BF16),
            pltpu.VMEM((dp, own, block), BF16),
            pltpu.VMEM((8, lanes), F32),
            pltpu.VMEM((dp, 8, lanes), F32),
            pltpu.VMEM((group, block), F32),
            pltpu.VMEM((experts, slots, block), BF16),
            pltpu.VMEM((dp, experts, slots, block), BF16),
            pltpu.VMEM((total, block), F32),
            pltpu.VMEM((total, block), F32),
            pltpu.VMEM((dp, experts, slots, block), BF16),
            pltpu.VMEM((dp, experts, slots, block), BF16),
            pltpu.VMEM((experts, slots, block), BF16),
            pltpu.VMEM((experts, slots, block), BF16),
            pltpu.VMEM((total, group), F32),
            pltpu.VMEM((dp, own, block), BF16),
            dma((7,)),
            dma((dp,)), dma((dp,)), dma((dp,)), dma((dp,)),
            dma((experts,)), dma((experts,)),
            dma((dp, experts)), dma((dp, experts)),
            dma((dp, experts)), dma((dp, experts)),
            dma((experts,)), dma((experts,)),
            dma((dp,)), dma((dp,)),
        ],
        compiler_params=pltpu.CompilerParams(
            collective_id=0, has_side_effects=True, vmem_limit_bytes=56 << 20
        ),
    )(tokens, expert_ids.T, gate_weights.T, placement, w_gate[0], w_up[0], w_down[0])


def solution(mesh):
    placed = (
        P(("groups", "expert", "dp"), None),
        P(("groups", "expert", "dp"), None),
        P(("groups", "expert", "dp"), None),
        P("groups", None),
        P("expert", "dp", None),
        P("expert", "dp", None),
        P("expert", "dp", None),
    )
    return jax.shard_map(
        body,
        mesh=mesh,
        in_specs=placed,
        out_specs=P(("groups", "expert", "dp"), None),
        check_vma=False,
    )
```

```python
import functools

import jax
import jax.numpy as jnp
from jax import lax
from jax.experimental import pallas as pl
from jax.experimental.pallas import tpu as pltpu
from jax.sharding import PartitionSpec as P

MESH = pl.DeviceIdType.MESH
F32 = jnp.float32
BF16 = jnp.bfloat16


def each(count, step):
    if count <= 8:
        for i in range(count):
            step(i)
    else:
        def turn(i, carry):
            step(i)
            return carry

        lax.fori_loop(0, count, turn, 0)


def each_from(first, count, step):
    each(count - first, lambda i: step(i + first))


def kernel(experts, dp, topk, first, slots, padded,
           tok_hbm, ids_hbm, gates_hbm, placement_hbm, wg_hbm, wu_hbm, wd_hbm, out,
           tok, ids, gates, placement,
           wg, wu, wd, tok_s, tok_r, info_s, info_r, group_x, disp_s, rows_r, rows_f, part_f,
           part_s, part_r, back_s, back_r, wsel, mix_s,
           w_sem, s1, r1, si, ri, s2, r2, s3, r3, s4, r4, s5, r5, s6, r6):
    me_e = lax.axis_index("expert")
    me_j = lax.axis_index("dp")
    own, width = tok.shape
    block = width // dp
    group = own * dp
    pairs = group * topk
    lanes = info_s.shape[1]
    total = experts * padded

    if dp == 4:
        low, high = lax.rem(me_j, 2), me_j // 2
        across = (me_j, high * 2 + (1 - low), (1 - high) * 2 + low, (1 - high) * 2 + (1 - low))
        onward = backward = lambda s: across[s]
    else:
        onward = lambda s: lax.rem(me_j + s, dp)
        backward = lambda s: lax.rem(me_j + dp - s, dp)

    def to_dp(src, dst, send, recv, s):
        return pltpu.make_async_remote_copy(
            src_ref=src, dst_ref=dst, send_sem=send, recv_sem=recv,
            device_id={"dp": onward(s)}, device_id_type=MESH)

    def to_expert(src, dst, send, recv, shift):
        return pltpu.make_async_remote_copy(
            src_ref=src, dst_ref=dst, send_sem=send, recv_sem=recv,
            device_id={"expert": lax.rem(me_e + shift, experts)}, device_id_type=MESH)

    def cols(j):
        return pl.ds(pl.multiple_of(j * block, 128), block)

    barrier = pltpu.get_barrier_semaphore()
    for s in range(1, dp):
        pl.semaphore_signal(barrier, inc=1, device_id={"dp": onward(s)}, device_id_type=MESH)

    def greet(d):
        pl.semaphore_signal(barrier, inc=1, device_id={"expert": lax.rem(me_e + d, experts)}, device_id_type=MESH)

    each_from(1, experts, greet)

    pairs_of = ((ids_hbm, ids), (gates_hbm, gates), (placement_hbm, placement), (tok_hbm, tok),
                (wg_hbm, wg), (wu_hbm, wu), (wd_hbm, wd))
    loads = [pltpu.make_async_copy(a, b, w_sem.at[i]) for i, (a, b) in enumerate(pairs_of)]
    for load in loads:
        load.start()
    for load in loads[:4]:
        load.wait()
    loads = loads[4:]

    lane = lax.broadcasted_iota(jnp.int32, (8, lanes), 1)
    line = lax.broadcasted_iota(jnp.int32, (8, lanes), 0)
    id_f = ids[...].astype(F32)
    gate_f = gates[...].astype(F32)
    info = jnp.zeros((8, lanes), F32)
    for t in range(own):
        for k in range(topk):
            here = lane == (me_j * own + t) * topk + k
            value = jnp.where(line == 0, jnp.broadcast_to(id_f[k:k + 1, t:t + 1], (8, lanes)),
                              jnp.broadcast_to(gate_f[k:k + 1, t:t + 1], (8, lanes)))
            info = jnp.where(here, value, info)
    info_s[...] = info
    for s in range(1, dp):
        tok_s[s] = tok[:, cols(onward(s))]
    tok_r[me_j] = tok[:, cols(me_j)]

    pl.semaphore_wait(barrier, dp - 1 + experts - 1)

    for s in range(1, dp):
        to_dp(info_s, info_r.at[s], si.at[s], ri.at[s], s).start()
    for s in range(1, dp):
        to_dp(tok_s.at[s], tok_r.at[me_j], s1.at[s], r1.at[s], s).start()
    for s in range(1, dp):
        to_dp(info_s, info_r.at[s], si.at[s], ri.at[s], s).wait_recv()
        info = info + info_r[s]

    id_row = info[0:1, :]
    gate_row = info[1:2, :]
    at_row = lax.broadcasted_iota(jnp.int32, (pairs, lanes), 0)
    at_lane = lax.broadcasted_iota(jnp.int32, (pairs, lanes), 1)
    id_col = jnp.sum(jnp.where(at_row == at_lane, jnp.broadcast_to(id_row, (pairs, lanes)), 0.0),
                     axis=1, keepdims=True)
    same = jnp.broadcast_to(id_col, (pairs, lanes)) == jnp.broadcast_to(id_row, (pairs, lanes))
    rank = jnp.sum(jnp.where(same, jnp.where(at_row < at_lane, 1.0, 0.0), 0.0), axis=0, keepdims=True)
    limit = jnp.full((1, lanes), float(first), F32)
    listed = placement[...].astype(F32)
    for h in range(placement.shape[1]):
        limit = jnp.where(id_row == jnp.broadcast_to(listed[0:1, h:h + 1], (1, lanes)), float(slots), limit)
    dest = jnp.where(rank < limit, id_row * float(padded) + rank, -1.0)
    dest = jnp.where(lax.broadcasted_iota(jnp.int32, (1, lanes), 1) < pairs, dest, -1.0)
    pick = lax.broadcasted_iota(jnp.int32, (total, lanes), 0).astype(F32) == jnp.broadcast_to(dest, (total, lanes))
    pair_i = lax.broadcasted_iota(jnp.int32, (lanes, group), 0)
    token_i = lax.broadcasted_iota(jnp.int32, (lanes, group), 1) * topk
    fold = jnp.where(pair_i >= token_i, jnp.where(pair_i < token_i + topk, 1.0, 0.0), 0.0).astype(BF16)
    select = jnp.dot(jnp.where(pick, 1.0, 0.0).astype(BF16), fold, preferred_element_type=F32).astype(BF16)

    for s in range(1, dp):
        to_dp(tok_s.at[s], tok_r.at[backward(s)], s1.at[s], r1.at[s], s).wait_recv()
    for j in range(dp):
        group_x[j * own:(j + 1) * own, :] = tok_r[j].astype(F32)
    rows_f[...] = jnp.dot(select, group_x[...].astype(BF16), preferred_element_type=F32)

    def dispatch(d):
        e = lax.rem(me_e + d, experts)
        start = pl.multiple_of(e * padded, 8)
        disp_s[e] = rows_f[pl.ds(start, slots), :].astype(BF16)
        to_expert(disp_s.at[e], rows_r.at[me_j, me_e], s2.at[d], r2.at[d], d).start()

    each_from(1, experts, dispatch)
    rows_r[me_j, me_e] = rows_f[pl.ds(pl.multiple_of(me_e * padded, 8), slots), :].astype(BF16)

    relayed = dp == 4 and experts <= 8
    direct = (1, 2) if relayed else range(1, dp)

    def forward(d):
        g = lax.rem(me_e + experts - d, experts)
        for s in direct:
            to_dp(rows_r.at[me_j, g], rows_r.at[me_j, g], s3.at[s, d], r3.at[s, d], s).start()

    forward(0)
    wsel[...] = jnp.dot(jnp.where(pick, jnp.broadcast_to(gate_row, (total, lanes)), 0.0).astype(BF16), fold,
                        preferred_element_type=F32)


    def arrive(d):
        g = lax.rem(me_e + experts - d, experts)
        to_expert(disp_s.at[g], rows_r.at[me_j, g], s2.at[d], r2.at[d], d).wait_recv()
        forward(d)

    each_from(1, experts, arrive)

    loads[0].wait()
    loads[1].wait()
    contract = (((1,), (1,)), ((), ()))

    def first_of(d):
        return 1 + d % 2

    def relay(d):
        g = lax.rem(me_e + experts - d, experts)
        side = first_of(d)
        j = onward(side)
        to_dp(rows_r.at[j, g], rows_r.at[j, g], s3.at[side, d], r3.at[side, d], side).wait_recv()
        to_dp(rows_r.at[j, g], rows_r.at[j, g], s3.at[3, d], r3.at[3, d], 3 - side).start()

    gate = up = None
    for s in range(dp):
        j = backward(s)

        def take(d):
            g = lax.rem(me_e + experts - d, experts)
            if s > 0 and not (relayed and s == first_of(d)):
                to_dp(rows_r.at[j, g], rows_r.at[j, g], s3.at[s, d], r3.at[s, d], s).wait_recv()
            rows_f[pl.ds(pl.multiple_of(g * padded, 8), slots), :] = rows_r[j, g].astype(F32)

        each(experts, take)
        x = rows_f[...].astype(BF16)
        gate_part = lax.dot_general(x, wg[:, cols(j)], contract, preferred_element_type=F32)
        up_part = lax.dot_general(x, wu[:, cols(j)], contract, preferred_element_type=F32)
        gate = gate_part if gate is None else gate + gate_part
        up = up_part if up is None else up + up_part
        if relayed and s == 0:
            each(experts, relay)
    hidden = (gate / (1.0 + jnp.exp(-gate)) * up).astype(BF16)

    loads[2].wait()
    for s in reversed(range(dp)):
        j = onward(s)
        part_f[...] = jnp.dot(hidden, wd[:, cols(j)], preferred_element_type=F32)
        target = part_s if s > 0 else part_r

        def split(d):
            g = lax.rem(me_e + d, experts)
            start = pl.multiple_of(g * padded, 8)
            target[s, g] = part_f[pl.ds(start, slots), :].astype(BF16)
            if s > 0:
                to_dp(part_s.at[s, g], part_r.at[s, g], s4.at[s, d], r4.at[s, d], s).start()

        each_from(1, experts, split)
        split(0)

    def summed(d):
        g = lax.rem(me_e + d, experts)
        for s in range(1, dp):
            to_dp(part_s.at[s, g], part_r.at[s, g], s4.at[s, d], r4.at[s, d], s).wait_recv()
        value = part_r[0, g].astype(F32)
        for s in range(1, dp):
            value = value + part_r[s, g].astype(F32)
        return value.astype(BF16)

    def give(d):
        g = lax.rem(me_e + d, experts)
        back_s[g] = summed(d)
        to_expert(back_s.at[g], back_r.at[me_e], s5.at[d], r5.at[d], d).start()

    each_from(1, experts, give)
    back_r[me_e] = summed(0)

    def collect(d):
        e = lax.rem(me_e + experts - d, experts)
        to_expert(back_s.at[e], back_r.at[e], s5.at[d], r5.at[d], d).wait_recv()

    each_from(1, experts, collect)

    def place(e):
        rows_f[pl.ds(e * padded, slots), :] = back_r[e].astype(F32)

    each(experts, place)
    group_x[...] = lax.dot_general(wsel[...].astype(BF16), rows_f[...].astype(BF16), (((0,), (0,)), ((), ())),
                                   preferred_element_type=F32)
    for j in range(dp):
        mix_s[j] = group_x[j * own:(j + 1) * own, :].astype(BF16)
    for s in reversed(range(1, dp)):
        to_dp(mix_s.at[onward(s)], out.at[:, cols(me_j)], s6.at[s], r6.at[s], s).start()
    kept = pltpu.make_async_copy(mix_s.at[me_j], out.at[:, cols(me_j)], s6.at[0])
    kept.start()
    kept.wait()
    for s in range(1, dp):
        j = backward(s)
        to_dp(mix_s.at[j], out.at[:, cols(j)], s6.at[s], r6.at[s], s).wait_recv()

    for s in range(1, dp):
        to_dp(info_s, info_r.at[s], si.at[s], ri.at[s], s).wait_send()
        to_dp(tok_s.at[s], tok_r.at[me_j], s1.at[s], r1.at[s], s).wait_send()
        to_dp(mix_s.at[onward(s)], out.at[:, cols(me_j)], s6.at[s], r6.at[s], s).wait_send()

    def left(d):
        g = lax.rem(me_e + experts - d, experts)
        for s in range(1, dp):
            to_dp(rows_r.at[me_j, g], rows_r.at[me_j, g], s3.at[s, d], r3.at[s, d], s).wait_send()
            to_dp(part_s.at[s, g], part_r.at[s, g], s4.at[s, d], r4.at[s, d], s).wait_send()

    def left_expert(d):
        e = lax.rem(me_e + d, experts)
        to_expert(disp_s.at[e], rows_r.at[me_j, me_e], s2.at[d], r2.at[d], d).wait_send()
        to_expert(back_s.at[e], back_r.at[me_e], s5.at[d], r5.at[d], d).wait_send()

    each(experts, left)
    each_from(1, experts, left_expert)


def relay_kernel(experts, dp, topk, first, slots, pad, bands, cuts,
                 tok_hbm, ids_hbm, gates_hbm, placement_hbm, wg_hbm, wu_hbm, wd_hbm, out,
                 ids, gates, placement, rows, flat, wgu, wd, acc, hid, partial, part_s, part_r, diag_r, back_s,
                 ready_e, ready_d, l_sem, w_sem, z_s, z_r, d_s, d_r, g_s, g_r, c_s, c_r, h_sem, p_s, p_r, q_s, q_r, b_s, b_r):
    me_e = lax.axis_index("expert")
    me_j = lax.axis_index("dp")
    core = lax.rem(me_e, 2)
    z = lax.div(me_e, 2)
    chips = experts // 2
    far = chips - 1
    own = rows.shape[3]
    width = tok_hbm.shape[1]
    units = wg_hbm.shape[0]
    half = width // 2
    both = 2 * own
    span = dp * both
    many = chips * span
    band = width // bands

    def turn(at, q):
        return q + lax.div(at, chips // 2) * (far - 2 * q)

    def chip_at(k):
        q = k - 1 + lax.div(k - 1 + chips - turn(z, z), chips)
        return turn(z, q)

    def seen_from(other):
        q = turn(other, z)
        return q + 1 - lax.div(q + chips - turn(other, other), chips)

    def sent_to(n):
        before = lax.div(z - n - 1 + chips, chips)
        return before * (z - 1 - n) + (1 - before) * (n + 1)

    low, high = lax.rem(me_j, 2), lax.div(me_j, 2)
    across = (me_j, high * 2 + (1 - low), (1 - high) * 2 + low, (1 - high) * 2 + (1 - low))
    sibling = z * 2 + (1 - core)

    def to_dp(src, dst, send, recv, s):
        return pltpu.make_async_remote_copy(src_ref=src, dst_ref=dst, send_sem=send, recv_sem=recv,
                                            device_id={"dp": across[s]}, device_id_type=MESH)

    def to_expert(src, dst, send, recv, e):
        return pltpu.make_async_remote_copy(src_ref=src, dst_ref=dst, send_sem=send, recv_sem=recv,
                                            device_id={"expert": e}, device_id_type=MESH)

    def landed(ref, sem):
        to_expert(ref, ref, sem, sem, sibling).wait_recv()

    def left(ref, sem):
        to_expert(ref, ref, sem, sem, sibling).wait_send()

    mid = bands // 2
    split = mid * band

    def edge(b):
        return b * band + (pad if b > mid else 0)

    def cols(b0, b1):
        return pl.ds(edge(b0), edge(b1) - edge(b0))

    z_cuts = ((0, bands // 2), (bands // 2, bands))
    at_cut = {}
    for k in range(chips):
        for i in range(len(cuts[k])):
            at_cut[k, i] = len(at_cut)

    barrier = pltpu.get_barrier_semaphore()

    def tell(sem, axis, to):
        pl.semaphore_signal(sem, inc=1, device_id={axis: to}, device_id_type=MESH)

    tell(barrier, "expert", sibling)
    for s in range(1, dp):
        pl.when(across[s] > me_j)(functools.partial(tell, barrier, "dp", across[s]))
    for q in range(1, chips):
        for o in range(2):
            pl.when(q > z)(functools.partial(tell, barrier, "expert", q * 2 + o))

    def meet_dp(s):
        @pl.when(across[s] > me_j)
        def _():
            pl.semaphore_wait(ready_d.at[s - 1], 1)

    def meet_chip(q, o):
        @pl.when(q > z)
        def _():
            pl.semaphore_wait(ready_e.at[q - 1, o], 1)

    mine = rows.at[core, 0, me_j]
    kept = pl.ds(pl.multiple_of(core * half, 128), half)
    given = pl.ds(pl.multiple_of((1 - core) * half, 128), half)
    loads = [pltpu.make_async_copy(a, b, l_sem.at[i]) for i, (a, b) in enumerate((
        (ids_hbm, ids), (gates_hbm, gates), (placement_hbm, placement),
        (tok_hbm.at[:, pl.ds(0, split)], mine.at[:, pl.ds(0, split)]),
        (tok_hbm.at[:, pl.ds(split, width - split)], mine.at[:, pl.ds(split + pad, width - split)]),
        (wg_hbm, wgu.at[pl.ds(0, units)]), (wu_hbm, wgu.at[pl.ds(units, units)]),
        (wd_hbm.at[:, kept], wd.at[core])))]
    for load in loads[:5]:
        load.start()
    pl.semaphore_wait(barrier, 1 + 2 * z + me_j)
    for q in range(chips - 1):
        for o in range(2):
            pl.when(q < z)(functools.partial(tell, ready_e.at[z - 1, core], "expert", q * 2 + o))
    for s in range(1, dp):
        pl.when(across[s] < me_j)(functools.partial(tell, ready_d.at[s - 1], "dp", across[s]))

    def far_send(n, src, c, part):
        other = sent_to(n)
        k = seen_from(other)
        to_expert(src, rows.at[core, k, me_j, :, c], z_s, z_r.at[k - 1, part], other * 2 + core).start()

    def send_tokens(n):
        far_send(n, tok_hbm.at[:, pl.ds(0, split)], pl.ds(0, split), 0)
        far_send(n, tok_hbm.at[:, pl.ds(split, width - split)], pl.ds(split + pad, width - split), 1)

    told_at = pl.ds(split, pad)

    def send_all(n):
        for part, c in enumerate((pl.ds(0, split), pl.ds(split, width + pad - split))):
            far_send(n, mine.at[:, c], c, part)

    def send_told(n):
        far_send(n, mine.at[:, told_at], told_at, 1)

    for n in range(chips - 1):
        pl.when(n < z)(functools.partial(send_tokens, n))
    for load in loads[5:]:
        load.start()

    for load in loads[:3]:
        load.wait()
    lane = lax.broadcasted_iota(jnp.int32, (own, pad), 1)
    line = lax.broadcasted_iota(jnp.int32, (own, pad), 0)
    id_f = ids[...].astype(F32)
    gate_f = gates[...].astype(F32)
    info = jnp.zeros((own, pad), F32)
    for t in range(own):
        for k in range(topk):
            for at, table in ((k, id_f), (topk + k, gate_f)):
                here = jnp.where(line == t, lane, -1) == at
                info = jnp.where(here, jnp.broadcast_to(table[k:k + 1, t:t + 1], (own, pad)), info)
    rows[core, 0, me_j, :, told_at] = info.astype(BF16)
    for n in range(chips - 1):
        pl.when(n < z)(functools.partial(send_told, n))
    loads[3].wait()
    loads[4].wait()

    def over_dp(k, i, s, at):
        here = rows.at[core, k, at, :, cols(*cuts[k][i])]
        return to_dp(here, here, d_s.at[k], d_r.at[at_cut[k, i]], s)

    for s in range(1, dp):
        meet_dp(s)
        over_dp(0, 0, s, me_j).start()
    for n in range(chips - 1):
        @pl.when(n >= z)
        def _():
            meet_chip(sent_to(n), core)
            send_all(n)
    lend = to_expert(wd_hbm.at[:, given], wd.at[core], w_sem.at[0], w_sem.at[1], sibling)
    lend.start()

    def pass_on(k):
        for i, (b0, b1) in enumerate(cuts[k]):
            for n, (a0, a1) in enumerate(z_cuts):
                if b0 <= a0 < b1:
                    landed(rows.at[core, k, me_j, :, cols(a0, a1)], z_r.at[k - 1, n])

            for s in range(1, dp - 1):
                over_dp(k, i, s, me_j).start()

            @pl.when(chip_at(k) > z)
            def _():
                over_dp(k, i, dp - 1, me_j).start()

    def share(k, i):
        c = cols(*cuts[k][i])

        def wait_for(count):
            landed(rows.at[core, k, pl.ds(0, count), :, c], d_r.at[at_cut[k, i]])

        if k == 0:
            wait_for(dp - 1)
        else:
            pl.when(chip_at(k) > z)(functools.partial(wait_for, dp - 1))

            @pl.when(chip_at(k) < z)
            def _():
                wait_for(dp - 2)
                if i == 0:
                    landed(rows.at[core, k, 0], g_r.at[k - 1])
        here = rows.at[core, k, :, :, c]
        to_expert(here, here, c_s.at[k], c_r.at[at_cut[k, i]], sibling).start()

    def spread(k, i):
        c = cols(*cuts[k][i])
        landed(rows.at[1 - core, k, :, :, c], c_r.at[at_cut[k, i]])
        for o in range(2):
            for j in range(dp):
                start = k * span + j * both + o * own
                flat[start:start + own, c] = rows[o, k, j, :, c].astype(F32)

    def relay(n):
        k = seen_from(sent_to(n))
        return to_expert(rows.at[core, 0, across[dp - 1]], rows.at[core, k, across[dp - 1]], g_s.at[n], g_r.at[k - 1],
                         sent_to(n) * 2 + core)

    def share_own():
        share(0, 0)
        for n in range(chips - 1):
            @pl.when(n >= z)
            def _():
                relay(n).start()

    pass_on(1)
    pl.when(z == 0)(share_own)
    for k in range(2, chips):
        pass_on(k)
    pl.when(z != 0)(share_own)
    spread(0, 0)
    for k in range(1, chips):
        for i in range(len(cuts[k])):
            share(k, i)
        if k > 1:
            for i in range(len(cuts[k - 1])):
                spread(k - 1, i)

    contract = (((1,), (1,)), ((), ()))
    loads[5].wait()
    loads[6].wait()
    me_f = me_e.astype(F32)
    weight = None
    for b in range(bands):
        for i, (b0, b1) in enumerate(cuts[far]):
            if b0 == b:
                spread(far, i)
        x = flat[:, pl.ds(b * band + (pad if b >= mid else 0), band)].astype(BF16)
        total = lax.dot_general(x, wgu[:, pl.ds(b * band, band)], contract, preferred_element_type=F32)
        if b == mid:
            r = lax.broadcasted_iota(jnp.int32, (many, many), 0)
            q = lax.broadcasted_iota(jnp.int32, (many, many), 1)
            of_r = jnp.where(lax.div(r, span) == lax.div(q, span), lax.rem(lax.div(r, own), 2), 2)
            same = of_r == lax.rem(lax.div(q, own), 2)
            below = jnp.where(same, jnp.where(q < r, 1.0, 0.0), 0.0).astype(BF16)
            listed = placement[0:1, :].astype(F32)
            extra = jnp.sum(jnp.where(listed == me_f, float(slots - first), 0.0), axis=1, keepdims=True)
            told = flat[:, told_at]
            named = jnp.zeros((many, 1), F32)
            value = jnp.zeros((many, 1), F32)
            for k in range(topk):
                hit = told[:, k:k + 1] == me_f
                named = named + jnp.where(hit, 1.0, 0.0)
                value = value + jnp.where(hit, told[:, topk + k:topk + k + 1], 0.0)
            rank = jnp.dot(below, jnp.broadcast_to(named, (many, 128)).astype(BF16), preferred_element_type=F32)[:, 0:1]
            weight = jnp.where(rank < float(first) + extra, value, 0.0)
        if b == 0:
            acc[...] = total
        elif b < bands - 1:
            acc[...] += total
        else:
            total = acc[...] + total
            gate, up = total[:, :units], total[:, units:]
            hid[core] = (gate / (1.0 + jnp.exp(-gate)) * up * weight).astype(BF16)

    swap = to_expert(hid.at[core], hid.at[core], h_sem.at[0], h_sem.at[1], sibling)
    swap.start()
    loads[7].wait()
    piece = half // bands
    for b in range(bands):
        c = pl.ds(b * piece, piece)
        partial[:, c] = jnp.dot(hid[core], wd[core, :, c], preferred_element_type=F32)
    landed(wd.at[1 - core], w_sem.at[1])
    landed(hid.at[1 - core], h_sem.at[1])

    diagonal = dp - 1

    def send_part(k, c):
        for s in range(1, diagonal):
            to_dp(part_s.at[k * dp + across[s], :, c], part_r.at[k, s - 1, :, c], p_s.at[k], p_r.at[k], s).start()

    def send_over_z(k, c):
        other = chip_at(k)
        at = seen_from(other) - 1
        to_expert(part_s.at[k * dp + across[diagonal], :, c], diag_r.at[at, :, c], q_s, q_r.at[at],
                  other * 2 + core).start()

    def rest(b):
        return jnp.dot(hid[1 - core], wd[1 - core, :, b * piece:(b + 1) * piece], preferred_element_type=F32)

    ahead = rest(0)
    for b in range(bands):
        c = pl.ds(b * piece, piece)
        total = partial[:, c] + ahead
        if b < bands - 1:
            ahead = rest(b + 1)
        part_s[:, :, c] = total.reshape(chips * dp, both, piece).astype(BF16)
        send_part(far, c)
        send_over_z(far, c)
    for k in reversed(range(1, far)):
        send_over_z(k, pl.ds(0, half))
    for k in reversed(range(far)):
        send_part(k, pl.ds(0, half))
    for k in range(1, chips):
        meet_chip(chip_at(k), 1 - core)

    def pack(to, value):
        for o in range(2):
            to[o] = value[o * own:(o + 1) * own, :].astype(BF16)

    def gather_part(k):
        landed(part_r.at[k, pl.ds(0, diagonal - 1)], p_r.at[k])
        value = part_s[k * dp + me_j].astype(F32)
        for s in range(diagonal - 1):
            value = value + part_r[k, s].astype(F32)
        pack(back_s.at[k], value)
        if k > 0:
            for o in range(2):
                to_expert(back_s.at[k, o], out.at[z, :, kept], b_s.at[0], b_r.at[0], chip_at(k) * 2 + o).start()

    def gather_diagonal():
        value = part_s[across[diagonal]].astype(F32)
        for k in range(1, chips):
            landed(diag_r.at[k - 1], q_r.at[k - 1])
            value = value + diag_r[k - 1].astype(F32)
        pack(back_s.at[chips], value)

        for o in range(2):
            pltpu.make_async_remote_copy(
                src_ref=back_s.at[chips, o], dst_ref=out.at[chips, :, kept], send_sem=b_s.at[3], recv_sem=b_r.at[2],
                device_id={"expert": z * 2 + o, "dp": across[diagonal]}, device_id_type=MESH).start()

    gather_part(3)
    gather_part(2)
    gather_part(1)
    gather_diagonal()
    gather_part(0)
    give = to_expert(back_s.at[0, 1 - core], out.at[z, :, kept], b_s.at[1], b_r.at[1], sibling)
    give.start()
    keep = pltpu.make_async_copy(back_s.at[0, core], out.at[z, :, kept], b_s.at[2])
    keep.start()

    lend.wait_send()
    swap.wait_send()
    left(rows.at[core, 0, pl.ds(0, chips - 1)], z_s)
    for k in range(chips):
        if k == 0:
            left(rows.at[core, k, pl.ds(0, dp - 1)], d_s.at[k])
        else:
            pl.when(chip_at(k) > z)(functools.partial(left, rows.at[core, k, pl.ds(0, dp - 1)], d_s.at[k]))
            pl.when(chip_at(k) < z)(functools.partial(left, rows.at[core, k, pl.ds(0, dp - 2)], d_s.at[k]))
            pl.when(k > z)(functools.partial(left, rows.at[core, 0, 0], g_s.at[k - 1]))
        left(rows.at[core, k], c_s.at[k])
        if k not in ():
            left(part_r.at[k, pl.ds(0, diagonal - 1)], p_s.at[k])
    keep.wait()
    give.wait_send()
    left(diag_r, q_s)
    left(out.at[chips], b_s.at[3])
    landed(out.at[chips], b_r.at[2])
    left(out.at[pl.ds(0, chips - 1)], b_s.at[0])
    landed(out.at[z, :, given], b_r.at[1])
    landed(out.at[pl.ds(0, chips - 1)], b_r.at[0])


def relayed(tokens, expert_ids, gate_weights, placement, w_gate, w_up, w_down, experts, dp, first, slots):
    own, width = tokens.shape
    topk = expert_ids.shape[1]
    units = w_gate.shape[1]
    chips = experts // 2
    bands = 4
    pad = 128
    half = width // 2
    many = experts * dp * own
    whole = ((0, bands),)
    halves = ((0, bands // 2), (bands // 2, bands))
    single = tuple((b, b + 1) for b in range(bands))
    cuts = tuple(single if k == chips - 1 else halves if k == chips - 2 else whole for k in range(chips))
    parts_of = sum(len(c) for c in cuts)
    hbm = pl.BlockSpec(memory_space=pl.ANY)
    dma = pltpu.SemaphoreType.DMA
    parts = pl.pallas_call(
        functools.partial(relay_kernel, experts, dp, topk, first, slots, pad, bands, cuts),
        out_shape=pltpu.VMEM((chips + 1, own, width), BF16),
        in_specs=[hbm] * 7,
        out_specs=pl.BlockSpec(memory_space=pltpu.VMEM),
        scratch_shapes=[
            pltpu.VMEM((topk, own), jnp.int32),
            pltpu.VMEM((topk, own), BF16),
            pltpu.VMEM(placement.shape, jnp.int32),
            pltpu.VMEM((2, chips, dp, own, pad + width), BF16),
            pltpu.VMEM((many, pad + width), F32),
            pltpu.VMEM((2 * units, width), BF16),
            pltpu.VMEM((2, units, half), BF16),
            pltpu.VMEM((many, 2 * units), F32),
            pltpu.VMEM((2, many, units), BF16),
            pltpu.VMEM((many, half), F32),
            pltpu.VMEM((chips * dp, 2 * own, half), BF16),
            pltpu.VMEM((chips, dp - 2, 2 * own, half), BF16),
            pltpu.VMEM((chips - 1, 2 * own, half), BF16),
            pltpu.VMEM((chips + 1, 2, own, half), BF16),
            pltpu.SemaphoreType.REGULAR((chips - 1, 2)), pltpu.SemaphoreType.REGULAR((dp - 1,)),
            dma((8,)),
            dma((2,)),
            dma, dma((chips - 1, 2)),
            dma((chips,)), dma((parts_of,)),
            dma((chips - 1,)), dma((chips - 1,)),
            dma((chips,)), dma((parts_of,)),
            dma((2,)),
            dma((chips,)), dma((chips,)),
            dma, dma((chips - 1,)),
            dma((4,)), dma((3,)),
        ],
        compiler_params=pltpu.CompilerParams(
            collective_id=1, has_side_effects=True, vmem_limit_bytes=56 << 20
        ),
    )(tokens, expert_ids.T, gate_weights.T, placement, w_gate[0], w_up[0], w_down[0])
    return jnp.sum(parts.astype(F32), axis=0).astype(BF16)


def body(tokens, expert_ids, gate_weights, placement, w_gate, w_up, w_down):
    experts = lax.axis_size("expert")
    dp = lax.axis_size("dp")
    own, width = tokens.shape
    topk = expert_ids.shape[1]
    group = own * dp
    first = max(2, group * topk // experts)
    slots = first + max(1, first // 2)
    if dp == 4 and experts == 8 and own == 4 and width % 1024 == 0:
        return relayed(tokens, expert_ids, gate_weights, placement, w_gate, w_up, w_down, experts, dp, first, slots)
    padded = -(-slots // 8) * 8
    lanes = -(-group * topk // 128) * 128
    block = width // dp
    units = w_gate.shape[1]
    total = experts * padded
    hbm = pl.BlockSpec(memory_space=pl.ANY)
    dma = pltpu.SemaphoreType.DMA
    return pl.pallas_call(
        functools.partial(kernel, experts, dp, topk, first, slots, padded),
        out_shape=jax.ShapeDtypeStruct((own, width), BF16),
        in_specs=[hbm] * 7,
        out_specs=hbm,
        scratch_shapes=[
            pltpu.VMEM((own, width), BF16),
            pltpu.VMEM((topk, own), jnp.int32),
            pltpu.VMEM((topk, own), BF16),
            pltpu.VMEM(placement.shape, jnp.int32),
            pltpu.VMEM((units, width), BF16),
            pltpu.VMEM((units, width), BF16),
            pltpu.VMEM((units, width), BF16),
            pltpu.VMEM((dp, own, block), BF16),
            pltpu.VMEM((dp, own, block), BF16),
            pltpu.VMEM((8, lanes), F32),
            pltpu.VMEM((dp, 8, lanes), F32),
            pltpu.VMEM((group, block), F32),
            pltpu.VMEM((experts, slots, block), BF16),
            pltpu.VMEM((dp, experts, slots, block), BF16),
            pltpu.VMEM((total, block), F32),
            pltpu.VMEM((total, block), F32),
            pltpu.VMEM((dp, experts, slots, block), BF16),
            pltpu.VMEM((dp, experts, slots, block), BF16),
            pltpu.VMEM((experts, slots, block), BF16),
            pltpu.VMEM((experts, slots, block), BF16),
            pltpu.VMEM((total, group), F32),
            pltpu.VMEM((dp, own, block), BF16),
            dma((7,)),
            dma((dp,)), dma((dp,)), dma((dp,)), dma((dp,)),
            dma((experts,)), dma((experts,)),
            dma((dp, experts)), dma((dp, experts)),
            dma((dp, experts)), dma((dp, experts)),
            dma((experts,)), dma((experts,)),
            dma((dp,)), dma((dp,)),
        ],
        compiler_params=pltpu.CompilerParams(
            collective_id=0, has_side_effects=True, vmem_limit_bytes=56 << 20
        ),
    )(tokens, expert_ids.T, gate_weights.T, placement, w_gate[0], w_up[0], w_down[0])


def solution(mesh):
    placed = (
        P(("groups", "expert", "dp"), None),
        P(("groups", "expert", "dp"), None),
        P(("groups", "expert", "dp"), None),
        P("groups", None),
        P("expert", "dp", None),
        P("expert", "dp", None),
        P("expert", "dp", None),
    )
    return jax.shard_map(
        body,
        mesh=mesh,
        in_specs=placed,
        out_specs=P(("groups", "expert", "dp"), None),
        check_vma=False,
    )
```

```python
import functools

import jax
import jax.numpy as jnp
from jax import lax
from jax.experimental import pallas as pl
from jax.experimental.pallas import tpu as pltpu
from jax.sharding import PartitionSpec as P

MESH = pl.DeviceIdType.MESH
F32 = jnp.float32
BF16 = jnp.bfloat16


def each(count, step):
    if count <= 8:
        for i in range(count):
            step(i)
    else:
        def turn(i, carry):
            step(i)
            return carry

        lax.fori_loop(0, count, turn, 0)


def each_from(first, count, step):
    each(count - first, lambda i: step(i + first))


def kernel(experts, dp, topk, first, slots, padded,
           tok_hbm, ids_hbm, gates_hbm, placement_hbm, wg_hbm, wu_hbm, wd_hbm, out,
           tok, ids, gates, placement,
           wg, wu, wd, tok_s, tok_r, info_s, info_r, group_x, disp_s, rows_r, rows_f, part_f,
           part_s, part_r, back_s, back_r, wsel, mix_s,
           w_sem, s1, r1, si, ri, s2, r2, s3, r3, s4, r4, s5, r5, s6, r6):
    me_e = lax.axis_index("expert")
    me_j = lax.axis_index("dp")
    own, width = tok.shape
    block = width // dp
    group = own * dp
    pairs = group * topk
    lanes = info_s.shape[1]
    total = experts * padded

    if dp == 4:
        low, high = lax.rem(me_j, 2), me_j // 2
        across = (me_j, high * 2 + (1 - low), (1 - high) * 2 + low, (1 - high) * 2 + (1 - low))
        onward = backward = lambda s: across[s]
    else:
        onward = lambda s: lax.rem(me_j + s, dp)
        backward = lambda s: lax.rem(me_j + dp - s, dp)

    def to_dp(src, dst, send, recv, s):
        return pltpu.make_async_remote_copy(
            src_ref=src, dst_ref=dst, send_sem=send, recv_sem=recv,
            device_id={"dp": onward(s)}, device_id_type=MESH)

    def to_expert(src, dst, send, recv, shift):
        return pltpu.make_async_remote_copy(
            src_ref=src, dst_ref=dst, send_sem=send, recv_sem=recv,
            device_id={"expert": lax.rem(me_e + shift, experts)}, device_id_type=MESH)

    def cols(j):
        return pl.ds(pl.multiple_of(j * block, 128), block)

    barrier = pltpu.get_barrier_semaphore()
    for s in range(1, dp):
        pl.semaphore_signal(barrier, inc=1, device_id={"dp": onward(s)}, device_id_type=MESH)

    def greet(d):
        pl.semaphore_signal(barrier, inc=1, device_id={"expert": lax.rem(me_e + d, experts)}, device_id_type=MESH)

    each_from(1, experts, greet)

    pairs_of = ((ids_hbm, ids), (gates_hbm, gates), (placement_hbm, placement), (tok_hbm, tok),
                (wg_hbm, wg), (wu_hbm, wu), (wd_hbm, wd))
    loads = [pltpu.make_async_copy(a, b, w_sem.at[i]) for i, (a, b) in enumerate(pairs_of)]
    for load in loads:
        load.start()
    for load in loads[:4]:
        load.wait()
    loads = loads[4:]

    lane = lax.broadcasted_iota(jnp.int32, (8, lanes), 1)
    line = lax.broadcasted_iota(jnp.int32, (8, lanes), 0)
    id_f = ids[...].astype(F32)
    gate_f = gates[...].astype(F32)
    info = jnp.zeros((8, lanes), F32)
    for t in range(own):
        for k in range(topk):
            here = lane == (me_j * own + t) * topk + k
            value = jnp.where(line == 0, jnp.broadcast_to(id_f[k:k + 1, t:t + 1], (8, lanes)),
                              jnp.broadcast_to(gate_f[k:k + 1, t:t + 1], (8, lanes)))
            info = jnp.where(here, value, info)
    info_s[...] = info
    for s in range(1, dp):
        tok_s[s] = tok[:, cols(onward(s))]
    tok_r[me_j] = tok[:, cols(me_j)]

    pl.semaphore_wait(barrier, dp - 1 + experts - 1)

    for s in range(1, dp):
        to_dp(info_s, info_r.at[s], si.at[s], ri.at[s], s).start()
    for s in range(1, dp):
        to_dp(tok_s.at[s], tok_r.at[me_j], s1.at[s], r1.at[s], s).start()
    for s in range(1, dp):
        to_dp(info_s, info_r.at[s], si.at[s], ri.at[s], s).wait_recv()
        info = info + info_r[s]

    id_row = info[0:1, :]
    gate_row = info[1:2, :]
    at_row = lax.broadcasted_iota(jnp.int32, (pairs, lanes), 0)
    at_lane = lax.broadcasted_iota(jnp.int32, (pairs, lanes), 1)
    id_col = jnp.sum(jnp.where(at_row == at_lane, jnp.broadcast_to(id_row, (pairs, lanes)), 0.0),
                     axis=1, keepdims=True)
    same = jnp.broadcast_to(id_col, (pairs, lanes)) == jnp.broadcast_to(id_row, (pairs, lanes))
    rank = jnp.sum(jnp.where(same, jnp.where(at_row < at_lane, 1.0, 0.0), 0.0), axis=0, keepdims=True)
    limit = jnp.full((1, lanes), float(first), F32)
    listed = placement[...].astype(F32)
    for h in range(placement.shape[1]):
        limit = jnp.where(id_row == jnp.broadcast_to(listed[0:1, h:h + 1], (1, lanes)), float(slots), limit)
    dest = jnp.where(rank < limit, id_row * float(padded) + rank, -1.0)
    dest = jnp.where(lax.broadcasted_iota(jnp.int32, (1, lanes), 1) < pairs, dest, -1.0)
    pick = lax.broadcasted_iota(jnp.int32, (total, lanes), 0).astype(F32) == jnp.broadcast_to(dest, (total, lanes))
    pair_i = lax.broadcasted_iota(jnp.int32, (lanes, group), 0)
    token_i = lax.broadcasted_iota(jnp.int32, (lanes, group), 1) * topk
    fold = jnp.where(pair_i >= token_i, jnp.where(pair_i < token_i + topk, 1.0, 0.0), 0.0).astype(BF16)
    select = jnp.dot(jnp.where(pick, 1.0, 0.0).astype(BF16), fold, preferred_element_type=F32).astype(BF16)

    for s in range(1, dp):
        to_dp(tok_s.at[s], tok_r.at[backward(s)], s1.at[s], r1.at[s], s).wait_recv()
    for j in range(dp):
        group_x[j * own:(j + 1) * own, :] = tok_r[j].astype(F32)
    rows_f[...] = jnp.dot(select, group_x[...].astype(BF16), preferred_element_type=F32)

    def dispatch(d):
        e = lax.rem(me_e + d, experts)
        start = pl.multiple_of(e * padded, 8)
        disp_s[e] = rows_f[pl.ds(start, slots), :].astype(BF16)
        to_expert(disp_s.at[e], rows_r.at[me_j, me_e], s2.at[d], r2.at[d], d).start()

    each_from(1, experts, dispatch)
    rows_r[me_j, me_e] = rows_f[pl.ds(pl.multiple_of(me_e * padded, 8), slots), :].astype(BF16)

    relayed = dp == 4 and experts <= 8
    direct = (1, 2) if relayed else range(1, dp)

    def forward(d):
        g = lax.rem(me_e + experts - d, experts)
        for s in direct:
            to_dp(rows_r.at[me_j, g], rows_r.at[me_j, g], s3.at[s, d], r3.at[s, d], s).start()

    forward(0)
    wsel[...] = jnp.dot(jnp.where(pick, jnp.broadcast_to(gate_row, (total, lanes)), 0.0).astype(BF16), fold,
                        preferred_element_type=F32)


    def arrive(d):
        g = lax.rem(me_e + experts - d, experts)
        to_expert(disp_s.at[g], rows_r.at[me_j, g], s2.at[d], r2.at[d], d).wait_recv()
        forward(d)

    each_from(1, experts, arrive)

    loads[0].wait()
    loads[1].wait()
    contract = (((1,), (1,)), ((), ()))

    def first_of(d):
        return 1 + d % 2

    def relay(d):
        g = lax.rem(me_e + experts - d, experts)
        side = first_of(d)
        j = onward(side)
        to_dp(rows_r.at[j, g], rows_r.at[j, g], s3.at[side, d], r3.at[side, d], side).wait_recv()
        to_dp(rows_r.at[j, g], rows_r.at[j, g], s3.at[3, d], r3.at[3, d], 3 - side).start()

    gate = up = None
    for s in range(dp):
        j = backward(s)

        def take(d):
            g = lax.rem(me_e + experts - d, experts)
            if s > 0 and not (relayed and s == first_of(d)):
                to_dp(rows_r.at[j, g], rows_r.at[j, g], s3.at[s, d], r3.at[s, d], s).wait_recv()
            rows_f[pl.ds(pl.multiple_of(g * padded, 8), slots), :] = rows_r[j, g].astype(F32)

        each(experts, take)
        x = rows_f[...].astype(BF16)
        gate_part = lax.dot_general(x, wg[:, cols(j)], contract, preferred_element_type=F32)
        up_part = lax.dot_general(x, wu[:, cols(j)], contract, preferred_element_type=F32)
        gate = gate_part if gate is None else gate + gate_part
        up = up_part if up is None else up + up_part
        if relayed and s == 0:
            each(experts, relay)
    hidden = (gate / (1.0 + jnp.exp(-gate)) * up).astype(BF16)

    loads[2].wait()
    for s in reversed(range(dp)):
        j = onward(s)
        part_f[...] = jnp.dot(hidden, wd[:, cols(j)], preferred_element_type=F32)
        target = part_s if s > 0 else part_r

        def split(d):
            g = lax.rem(me_e + d, experts)
            start = pl.multiple_of(g * padded, 8)
            target[s, g] = part_f[pl.ds(start, slots), :].astype(BF16)
            if s > 0:
                to_dp(part_s.at[s, g], part_r.at[s, g], s4.at[s, d], r4.at[s, d], s).start()

        each_from(1, experts, split)
        split(0)

    def summed(d):
        g = lax.rem(me_e + d, experts)
        for s in range(1, dp):
            to_dp(part_s.at[s, g], part_r.at[s, g], s4.at[s, d], r4.at[s, d], s).wait_recv()
        value = part_r[0, g].astype(F32)
        for s in range(1, dp):
            value = value + part_r[s, g].astype(F32)
        return value.astype(BF16)

    def give(d):
        g = lax.rem(me_e + d, experts)
        back_s[g] = summed(d)
        to_expert(back_s.at[g], back_r.at[me_e], s5.at[d], r5.at[d], d).start()

    each_from(1, experts, give)
    back_r[me_e] = summed(0)

    def collect(d):
        e = lax.rem(me_e + experts - d, experts)
        to_expert(back_s.at[e], back_r.at[e], s5.at[d], r5.at[d], d).wait_recv()

    each_from(1, experts, collect)

    def place(e):
        rows_f[pl.ds(e * padded, slots), :] = back_r[e].astype(F32)

    each(experts, place)
    group_x[...] = lax.dot_general(wsel[...].astype(BF16), rows_f[...].astype(BF16), (((0,), (0,)), ((), ())),
                                   preferred_element_type=F32)
    for j in range(dp):
        mix_s[j] = group_x[j * own:(j + 1) * own, :].astype(BF16)
    for s in reversed(range(1, dp)):
        to_dp(mix_s.at[onward(s)], out.at[:, cols(me_j)], s6.at[s], r6.at[s], s).start()
    kept = pltpu.make_async_copy(mix_s.at[me_j], out.at[:, cols(me_j)], s6.at[0])
    kept.start()
    kept.wait()
    for s in range(1, dp):
        j = backward(s)
        to_dp(mix_s.at[j], out.at[:, cols(j)], s6.at[s], r6.at[s], s).wait_recv()

    for s in range(1, dp):
        to_dp(info_s, info_r.at[s], si.at[s], ri.at[s], s).wait_send()
        to_dp(tok_s.at[s], tok_r.at[me_j], s1.at[s], r1.at[s], s).wait_send()
        to_dp(mix_s.at[onward(s)], out.at[:, cols(me_j)], s6.at[s], r6.at[s], s).wait_send()

    def left(d):
        g = lax.rem(me_e + experts - d, experts)
        for s in range(1, dp):
            to_dp(rows_r.at[me_j, g], rows_r.at[me_j, g], s3.at[s, d], r3.at[s, d], s).wait_send()
            to_dp(part_s.at[s, g], part_r.at[s, g], s4.at[s, d], r4.at[s, d], s).wait_send()

    def left_expert(d):
        e = lax.rem(me_e + d, experts)
        to_expert(disp_s.at[e], rows_r.at[me_j, me_e], s2.at[d], r2.at[d], d).wait_send()
        to_expert(back_s.at[e], back_r.at[me_e], s5.at[d], r5.at[d], d).wait_send()

    each(experts, left)
    each_from(1, experts, left_expert)


def relay_kernel(experts, dp, topk, first, slots, pad, bands, cuts,
                 tok_hbm, ids_hbm, gates_hbm, placement_hbm, wg_hbm, wu_hbm, wd_hbm, out,
                 ids, gates, placement, rows, flat, wgu, wd, acc, hid, partial, part_s, part_r, diag_r, back_s,
                 ready_e, ready_d, l_sem, w_sem, z_s, z_r, d_s, d_r, g_s, g_r, c_s, c_r, h_sem, p_s, p_r, q_s, q_r, b_s, b_r):
    me_e = lax.axis_index("expert")
    me_j = lax.axis_index("dp")
    core = lax.rem(me_e, 2)
    z = lax.div(me_e, 2)
    chips = experts // 2
    far = chips - 1
    own = rows.shape[3]
    width = tok_hbm.shape[1]
    units = wg_hbm.shape[0]
    half = width // 2
    both = 2 * own
    span = dp * both
    many = chips * span
    band = width // bands

    def turn(at, q):
        return q + lax.div(at, chips // 2) * (far - 2 * q)

    def chip_at(k):
        q = k - 1 + lax.div(k - 1 + chips - turn(z, z), chips)
        return turn(z, q)

    def seen_from(other):
        q = turn(other, z)
        return q + 1 - lax.div(q + chips - turn(other, other), chips)

    def sent_to(n):
        before = lax.div(z - n - 1 + chips, chips)
        return before * (z - 1 - n) + (1 - before) * (n + 1)

    low, high = lax.rem(me_j, 2), lax.div(me_j, 2)
    across = (me_j, high * 2 + (1 - low), (1 - high) * 2 + low, (1 - high) * 2 + (1 - low))
    sibling = z * 2 + (1 - core)

    def to_dp(src, dst, send, recv, s):
        return pltpu.make_async_remote_copy(src_ref=src, dst_ref=dst, send_sem=send, recv_sem=recv,
                                            device_id={"dp": across[s]}, device_id_type=MESH)

    def to_expert(src, dst, send, recv, e):
        return pltpu.make_async_remote_copy(src_ref=src, dst_ref=dst, send_sem=send, recv_sem=recv,
                                            device_id={"expert": e}, device_id_type=MESH)

    def landed(ref, sem):
        to_expert(ref, ref, sem, sem, sibling).wait_recv()

    def left(ref, sem):
        to_expert(ref, ref, sem, sem, sibling).wait_send()

    mid = bands // 2
    split = mid * band

    def edge(b):
        return b * band + (pad if b > mid else 0)

    def cols(b0, b1):
        return pl.ds(edge(b0), edge(b1) - edge(b0))

    z_cuts = ((0, bands // 2), (bands // 2, bands))
    at_cut = {}
    for k in range(chips):
        for i in range(len(cuts[k])):
            at_cut[k, i] = len(at_cut)

    barrier = pltpu.get_barrier_semaphore()

    def tell(sem, axis, to):
        pl.semaphore_signal(sem, inc=1, device_id={axis: to}, device_id_type=MESH)

    tell(barrier, "expert", sibling)
    for s in range(1, dp):
        pl.when(across[s] > me_j)(functools.partial(tell, barrier, "dp", across[s]))
    for q in range(1, chips):
        for o in range(2):
            pl.when(q > z)(functools.partial(tell, barrier, "expert", q * 2 + o))

    def meet_dp(s):
        @pl.when(across[s] > me_j)
        def _():
            pl.semaphore_wait(ready_d.at[s - 1], 1)

    def meet_chip(q, o):
        @pl.when(q > z)
        def _():
            pl.semaphore_wait(ready_e.at[q - 1, o], 1)

    mine = rows.at[core, 0, me_j]
    kept = pl.ds(pl.multiple_of(core * half, 128), half)
    given = pl.ds(pl.multiple_of((1 - core) * half, 128), half)
    loads = [pltpu.make_async_copy(a, b, l_sem.at[i]) for i, (a, b) in enumerate((
        (ids_hbm, ids), (gates_hbm, gates), (placement_hbm, placement),
        (tok_hbm.at[:, pl.ds(0, split)], mine.at[:, pl.ds(0, split)]),
        (tok_hbm.at[:, pl.ds(split, width - split)], mine.at[:, pl.ds(split + pad, width - split)]),
        (wg_hbm, wgu.at[pl.ds(0, units)]), (wu_hbm, wgu.at[pl.ds(units, units)]),
        (wd_hbm.at[:, kept], wd.at[core])))]
    for load in loads[:5]:
        load.start()
    pl.semaphore_wait(barrier, 1 + 2 * z + me_j)
    for q in range(chips - 1):
        for o in range(2):
            pl.when(q < z)(functools.partial(tell, ready_e.at[z - 1, core], "expert", q * 2 + o))
    for s in range(1, dp):
        pl.when(across[s] < me_j)(functools.partial(tell, ready_d.at[s - 1], "dp", across[s]))

    def far_send(n, src, c, part):
        other = sent_to(n)
        k = seen_from(other)
        to_expert(src, rows.at[core, k, me_j, :, c], z_s, z_r.at[k - 1, part], other * 2 + core).start()

    def send_tokens(n):
        far_send(n, tok_hbm.at[:, pl.ds(0, split)], pl.ds(0, split), 0)
        far_send(n, tok_hbm.at[:, pl.ds(split, width - split)], pl.ds(split + pad, width - split), 1)

    told_at = pl.ds(split, pad)

    def send_all(n):
        for part, c in enumerate((pl.ds(0, split), pl.ds(split, width + pad - split))):
            far_send(n, mine.at[:, c], c, part)

    def send_told(n):
        far_send(n, mine.at[:, told_at], told_at, 1)

    for n in range(chips - 1):
        pl.when(n < z)(functools.partial(send_tokens, n))
    for load in loads[5:]:
        load.start()

    for load in loads[:3]:
        load.wait()
    lane = lax.broadcasted_iota(jnp.int32, (own, pad), 1)
    line = lax.broadcasted_iota(jnp.int32, (own, pad), 0)
    id_f = ids[...].astype(F32)
    gate_f = gates[...].astype(F32)
    info = jnp.zeros((own, pad), F32)
    for t in range(own):
        for k in range(topk):
            for at, table in ((k, id_f), (topk + k, gate_f)):
                here = jnp.where(line == t, lane, -1) == at
                info = jnp.where(here, jnp.broadcast_to(table[k:k + 1, t:t + 1], (own, pad)), info)
    rows[core, 0, me_j, :, told_at] = info.astype(BF16)
    for n in range(chips - 1):
        pl.when(n < z)(functools.partial(send_told, n))
    loads[3].wait()
    loads[4].wait()

    def over_dp(k, i, s, at):
        here = rows.at[core, k, at, :, cols(*cuts[k][i])]
        return to_dp(here, here, d_s.at[k], d_r.at[at_cut[k, i]], s)

    for s in range(1, dp):
        meet_dp(s)
        over_dp(0, 0, s, me_j).start()
    for n in range(chips - 1):
        @pl.when(n >= z)
        def _():
            meet_chip(sent_to(n), core)
            send_all(n)
    lend = to_expert(wd_hbm.at[:, given], wd.at[core], w_sem.at[0], w_sem.at[1], sibling)
    lend.start()

    def pass_on(k):
        for i, (b0, b1) in enumerate(cuts[k]):
            for n, (a0, a1) in enumerate(z_cuts):
                if b0 <= a0 < b1:
                    landed(rows.at[core, k, me_j, :, cols(a0, a1)], z_r.at[k - 1, n])

            for s in range(1, dp - 1):
                over_dp(k, i, s, me_j).start()

            @pl.when(chip_at(k) > z)
            def _():
                over_dp(k, i, dp - 1, me_j).start()

    def share(k, i):
        c = cols(*cuts[k][i])

        def wait_for(count):
            landed(rows.at[core, k, pl.ds(0, count), :, c], d_r.at[at_cut[k, i]])

        if k == 0:
            wait_for(dp - 1)
        else:
            pl.when(chip_at(k) > z)(functools.partial(wait_for, dp - 1))

            @pl.when(chip_at(k) < z)
            def _():
                wait_for(dp - 2)
                if i == 0:
                    landed(rows.at[core, k, 0], g_r.at[k - 1])
        here = rows.at[core, k, :, :, c]
        to_expert(here, here, c_s.at[k], c_r.at[at_cut[k, i]], sibling).start()

    def spread(k, i):
        c = cols(*cuts[k][i])
        landed(rows.at[1 - core, k, :, :, c], c_r.at[at_cut[k, i]])
        for o in range(2):
            for j in range(dp):
                start = k * span + j * both + o * own
                flat[start:start + own, c] = rows[o, k, j, :, c].astype(F32)

    def relay(n):
        k = seen_from(sent_to(n))
        return to_expert(rows.at[core, 0, across[dp - 1]], rows.at[core, k, across[dp - 1]], g_s.at[n], g_r.at[k - 1],
                         sent_to(n) * 2 + core)

    def share_own():
        share(0, 0)
        for n in range(chips - 1):
            @pl.when(n >= z)
            def _():
                relay(n).start()

    pass_on(1)
    pl.when(z == 0)(share_own)
    for k in range(2, chips):
        pass_on(k)
    pl.when(z != 0)(share_own)
    spread(0, 0)
    for k in range(1, chips):
        for i in range(len(cuts[k])):
            share(k, i)
        if k > 1:
            for i in range(len(cuts[k - 1])):
                spread(k - 1, i)

    contract = (((1,), (1,)), ((), ()))
    loads[5].wait()
    loads[6].wait()
    me_f = me_e.astype(F32)
    weight = None
    for b in range(bands):
        for i, (b0, b1) in enumerate(cuts[far]):
            if b0 == b:
                spread(far, i)
        x = flat[:, pl.ds(b * band + (pad if b >= mid else 0), band)].astype(BF16)
        total = lax.dot_general(x, wgu[:, pl.ds(b * band, band)], contract, preferred_element_type=F32)
        if b == mid:
            r = lax.broadcasted_iota(jnp.int32, (many, many), 0)
            q = lax.broadcasted_iota(jnp.int32, (many, many), 1)
            of_r = jnp.where(lax.div(r, span) == lax.div(q, span), lax.rem(lax.div(r, own), 2), 2)
            same = of_r == lax.rem(lax.div(q, own), 2)
            below = jnp.where(same, jnp.where(q < r, 1.0, 0.0), 0.0).astype(BF16)
            listed = placement[0:1, :].astype(F32)
            extra = jnp.sum(jnp.where(listed == me_f, float(slots - first), 0.0), axis=1, keepdims=True)
            told = flat[:, told_at]
            named = jnp.zeros((many, 1), F32)
            value = jnp.zeros((many, 1), F32)
            for k in range(topk):
                hit = told[:, k:k + 1] == me_f
                named = named + jnp.where(hit, 1.0, 0.0)
                value = value + jnp.where(hit, told[:, topk + k:topk + k + 1], 0.0)
            rank = jnp.dot(below, jnp.broadcast_to(named, (many, 128)).astype(BF16), preferred_element_type=F32)[:, 0:1]
            weight = jnp.where(rank < float(first) + extra, value, 0.0)
        if b == 0:
            acc[...] = total
        elif b < bands - 1:
            acc[...] += total
        else:
            total = acc[...] + total
            gate, up = total[:, :units], total[:, units:]
            hid[core] = (gate / (1.0 + jnp.exp(-gate)) * up * weight).astype(BF16)

    swap = to_expert(hid.at[core], hid.at[core], h_sem.at[0], h_sem.at[1], sibling)
    swap.start()
    loads[7].wait()
    piece = half // bands
    for b in range(bands):
        c = pl.ds(b * piece, piece)
        partial[:, c] = jnp.dot(hid[core], wd[core, :, c], preferred_element_type=F32)
    landed(wd.at[1 - core], w_sem.at[1])
    landed(hid.at[1 - core], h_sem.at[1])

    diagonal = dp - 1

    def send_part(k, c):
        for s in range(1, diagonal):
            to_dp(part_s.at[k * dp + across[s], :, c], part_r.at[k, s - 1, :, c], p_s.at[k], p_r.at[k], s).start()

    def send_over_z(k, c):
        other = chip_at(k)
        at = seen_from(other) - 1
        to_expert(part_s.at[k * dp + across[diagonal], :, c], diag_r.at[at, :, c], q_s, q_r.at[at],
                  other * 2 + core).start()

    def rest(b):
        return jnp.dot(hid[1 - core], wd[1 - core, :, b * piece:(b + 1) * piece], preferred_element_type=F32)

    ahead = rest(0)
    for b in range(bands):
        c = pl.ds(b * piece, piece)
        total = partial[:, c] + ahead
        if b < bands - 1:
            ahead = rest(b + 1)
        part_s[:, :, c] = total.reshape(chips * dp, both, piece).astype(BF16)
        send_part(far, c)
        send_over_z(far, c)
    for k in reversed(range(1, far)):
        send_over_z(k, pl.ds(0, half))
    for k in reversed(range(far)):
        send_part(k, pl.ds(0, half))
    for k in range(1, chips):
        meet_chip(chip_at(k), 1 - core)

    def pack(to, value):
        for o in range(2):
            to[o] = value[o * own:(o + 1) * own, :].astype(BF16)

    def gather_part(k):
        landed(part_r.at[k, pl.ds(0, diagonal - 1)], p_r.at[k])
        value = part_s[k * dp + me_j].astype(F32)
        for s in range(diagonal - 1):
            value = value + part_r[k, s].astype(F32)
        pack(back_s.at[k], value)
        if k > 0:
            for o in range(2):
                to_expert(back_s.at[k, o], out.at[z, :, kept], b_s.at[0], b_r.at[0], chip_at(k) * 2 + o).start()

    def gather_diagonal():
        value = part_s[across[diagonal]].astype(F32)
        for k in range(1, chips):
            landed(diag_r.at[k - 1], q_r.at[k - 1])
            value = value + diag_r[k - 1].astype(F32)
        pack(back_s.at[chips], value)

        for o in range(2):
            pltpu.make_async_remote_copy(
                src_ref=back_s.at[chips, o], dst_ref=out.at[chips, :, kept], send_sem=b_s.at[3], recv_sem=b_r.at[2],
                device_id={"expert": z * 2 + o, "dp": across[diagonal]}, device_id_type=MESH).start()

    gather_part(3)
    gather_part(2)
    gather_part(1)
    gather_part(0)
    give = to_expert(back_s.at[0, 1 - core], out.at[z, :, kept], b_s.at[1], b_r.at[1], sibling)
    give.start()
    keep = pltpu.make_async_copy(back_s.at[0, core], out.at[z, :, kept], b_s.at[2])
    keep.start()
    gather_diagonal()
    lend.wait_send()
    swap.wait_send()
    left(rows.at[core, 0, pl.ds(0, chips - 1)], z_s)
    for k in range(chips):
        if k == 0:
            left(rows.at[core, k, pl.ds(0, dp - 1)], d_s.at[k])
        else:
            pl.when(chip_at(k) > z)(functools.partial(left, rows.at[core, k, pl.ds(0, dp - 1)], d_s.at[k]))
            pl.when(chip_at(k) < z)(functools.partial(left, rows.at[core, k, pl.ds(0, dp - 2)], d_s.at[k]))
            pl.when(k > z)(functools.partial(left, rows.at[core, 0, 0], g_s.at[k - 1]))
        left(rows.at[core, k], c_s.at[k])
        if k not in ():
            left(part_r.at[k, pl.ds(0, diagonal - 1)], p_s.at[k])
    keep.wait()
    give.wait_send()
    left(diag_r, q_s)
    left(out.at[chips], b_s.at[3])
    landed(out.at[chips], b_r.at[2])
    left(out.at[pl.ds(0, chips - 1)], b_s.at[0])
    landed(out.at[z, :, given], b_r.at[1])
    landed(out.at[pl.ds(0, chips - 1)], b_r.at[0])


def relayed(tokens, expert_ids, gate_weights, placement, w_gate, w_up, w_down, experts, dp, first, slots):
    own, width = tokens.shape
    topk = expert_ids.shape[1]
    units = w_gate.shape[1]
    chips = experts // 2
    bands = 4
    pad = 128
    half = width // 2
    many = experts * dp * own
    whole = ((0, bands),)
    halves = ((0, bands // 2), (bands // 2, bands))
    single = tuple((b, b + 1) for b in range(bands))
    cuts = tuple(single if k >= chips - 2 else whole for k in range(chips))
    parts_of = sum(len(c) for c in cuts)
    hbm = pl.BlockSpec(memory_space=pl.ANY)
    dma = pltpu.SemaphoreType.DMA
    parts = pl.pallas_call(
        functools.partial(relay_kernel, experts, dp, topk, first, slots, pad, bands, cuts),
        out_shape=pltpu.VMEM((chips + 1, own, width), BF16),
        in_specs=[hbm] * 7,
        out_specs=pl.BlockSpec(memory_space=pltpu.VMEM),
        scratch_shapes=[
            pltpu.VMEM((topk, own), jnp.int32),
            pltpu.VMEM((topk, own), BF16),
            pltpu.VMEM(placement.shape, jnp.int32),
            pltpu.VMEM((2, chips, dp, own, pad + width), BF16),
            pltpu.VMEM((many, pad + width), F32),
            pltpu.VMEM((2 * units, width), BF16),
            pltpu.VMEM((2, units, half), BF16),
            pltpu.VMEM((many, 2 * units), F32),
            pltpu.VMEM((2, many, units), BF16),
            pltpu.VMEM((many, half), F32),
            pltpu.VMEM((chips * dp, 2 * own, half), BF16),
            pltpu.VMEM((chips, dp - 2, 2 * own, half), BF16),
            pltpu.VMEM((chips - 1, 2 * own, half), BF16),
            pltpu.VMEM((chips + 1, 2, own, half), BF16),
            pltpu.SemaphoreType.REGULAR((chips - 1, 2)), pltpu.SemaphoreType.REGULAR((dp - 1,)),
            dma((8,)),
            dma((2,)),
            dma, dma((chips - 1, 2)),
            dma((chips,)), dma((parts_of,)),
            dma((chips - 1,)), dma((chips - 1,)),
            dma((chips,)), dma((parts_of,)),
            dma((2,)),
            dma((chips,)), dma((chips,)),
            dma, dma((chips - 1,)),
            dma((4,)), dma((3,)),
        ],
        compiler_params=pltpu.CompilerParams(
            collective_id=1, has_side_effects=True, vmem_limit_bytes=56 << 20
        ),
    )(tokens, expert_ids.T, gate_weights.T, placement, w_gate[0], w_up[0], w_down[0])
    return jnp.sum(parts.astype(F32), axis=0).astype(BF16)


def body(tokens, expert_ids, gate_weights, placement, w_gate, w_up, w_down):
    experts = lax.axis_size("expert")
    dp = lax.axis_size("dp")
    own, width = tokens.shape
    topk = expert_ids.shape[1]
    group = own * dp
    first = max(2, group * topk // experts)
    slots = first + max(1, first // 2)
    if dp == 4 and experts == 8 and own == 4 and width % 1024 == 0:
        return relayed(tokens, expert_ids, gate_weights, placement, w_gate, w_up, w_down, experts, dp, first, slots)
    padded = -(-slots // 8) * 8
    lanes = -(-group * topk // 128) * 128
    block = width // dp
    units = w_gate.shape[1]
    total = experts * padded
    hbm = pl.BlockSpec(memory_space=pl.ANY)
    dma = pltpu.SemaphoreType.DMA
    return pl.pallas_call(
        functools.partial(kernel, experts, dp, topk, first, slots, padded),
        out_shape=jax.ShapeDtypeStruct((own, width), BF16),
        in_specs=[hbm] * 7,
        out_specs=hbm,
        scratch_shapes=[
            pltpu.VMEM((own, width), BF16),
            pltpu.VMEM((topk, own), jnp.int32),
            pltpu.VMEM((topk, own), BF16),
            pltpu.VMEM(placement.shape, jnp.int32),
            pltpu.VMEM((units, width), BF16),
            pltpu.VMEM((units, width), BF16),
            pltpu.VMEM((units, width), BF16),
            pltpu.VMEM((dp, own, block), BF16),
            pltpu.VMEM((dp, own, block), BF16),
            pltpu.VMEM((8, lanes), F32),
            pltpu.VMEM((dp, 8, lanes), F32),
            pltpu.VMEM((group, block), F32),
            pltpu.VMEM((experts, slots, block), BF16),
            pltpu.VMEM((dp, experts, slots, block), BF16),
            pltpu.VMEM((total, block), F32),
            pltpu.VMEM((total, block), F32),
            pltpu.VMEM((dp, experts, slots, block), BF16),
            pltpu.VMEM((dp, experts, slots, block), BF16),
            pltpu.VMEM((experts, slots, block), BF16),
            pltpu.VMEM((experts, slots, block), BF16),
            pltpu.VMEM((total, group), F32),
            pltpu.VMEM((dp, own, block), BF16),
            dma((7,)),
            dma((dp,)), dma((dp,)), dma((dp,)), dma((dp,)),
            dma((experts,)), dma((experts,)),
            dma((dp, experts)), dma((dp, experts)),
            dma((dp, experts)), dma((dp, experts)),
            dma((experts,)), dma((experts,)),
            dma((dp,)), dma((dp,)),
        ],
        compiler_params=pltpu.CompilerParams(
            collective_id=0, has_side_effects=True, vmem_limit_bytes=56 << 20
        ),
    )(tokens, expert_ids.T, gate_weights.T, placement, w_gate[0], w_up[0], w_down[0])


def solution(mesh):
    placed = (
        P(("groups", "expert", "dp"), None),
        P(("groups", "expert", "dp"), None),
        P(("groups", "expert", "dp"), None),
        P("groups", None),
        P("expert", "dp", None),
        P("expert", "dp", None),
        P("expert", "dp", None),
    )
    return jax.shard_map(
        body,
        mesh=mesh,
        in_specs=placed,
        out_specs=P(("groups", "expert", "dp"), None),
        check_vma=False,
    )
```
